32 devices in a mesh: groups: 2 (over y), lat: 8 (over z, x), lon: 2 (over core).
Axes of the slice: x: 2, y: 2, z: 4, core: 2. Of those that a mesh axis runs over, the one named last changes fastest.
Arguments:
- tokens: bfloat16 [16, 256, 768], P(('groups', 'lat'), 'lon'), parts along dimension 0, may hold values from -5 to 5
- gain_attn: float32 [768], replicated, may hold values from 0.25 to 1.75
- w_qkv: bfloat16 [768, 2304], P('lat'), may hold values from -0.048353085 to 0.048353085
- key_bias: bfloat16 [8, 12, 256], P('lat', None, 'lon'), may hold values from -3 to 250
- w_out: bfloat16 [768, 768], P('lat'), may hold values from -0.21875 to 0.21875
- gain_conv: float32 [768], replicated, may hold values from 0.25 to 1.75
- w_conv: bfloat16 [2, 768, 64], replicated, may hold values from -0.75 to 0.75
- lat_taps: float32 [16, 2], replicated, may hold values from -2 to 2
- lon_half: int32 [8], P('lat'), may hold values from 1 to 128, as said below
- lat_half: int32 [8], P('lat'), may hold values from 0 to 1, as said below
- quad_off: int32 [8], P('lat'), may hold values from 0 to 13
Outputs:
- updated: bfloat16 [16, 256, 768], P(('groups', 'lat'), 'lon'), parts along dimension 0
The draws below stay inside these ranges and needn't reach their ends.
There are 2 independent parts, one for each index of `groups`. The reference program is written for one: setup_inputs(seed, part) draws one part's arguments, and reference() takes and returns one part's arrays. A program takes and returns all parts, laid end to end along the dimension named above; an argument that names none is the same for every part. Nothing has to cross between parts.
Inputs may be any that keep to these rules, and one draw needn't show every extreme that they name: `lon_half`: the bands at either pole reach 128. `lat_half`: both polar bands have 1.
All inputs are finite; a program needn't handle non-finite values.
Results may differ from the reference program's by a relative error of at most 0.008.
Values may be sent and summed in bfloat16 or wider, within the bound.
A program may use at most 64 MiB of HBM per device.

```python
import math
import jax
import jax.numpy as jnp
from jax import lax

D = 768
H = 12
DH = 64
GW = 64
KB = 2
TAPS = 16
NLON = 256
NLAT = 8


def draw_tokens(key, part):
    col_key, main_key, base_key, wave_key = jax.random.split(key, 4)
    lon_angle = 2.0 * math.pi / NLON * jnp.arange(NLON, dtype=jnp.float32)
    first_cos = jnp.cos(lon_angle)[None, :, None]
    first_sin = jnp.sin(lon_angle)[None, :, None]
    wave_coef = jax.random.normal(wave_key, (4, NLAT, 1, D), jnp.float32)
    col_scale = jnp.exp(jax.random.uniform(col_key, (D,), jnp.float32, math.log(0.2), math.log(2.0)))
    rough_part = jnp.clip(jax.random.normal(main_key, (NLAT, NLON, D), jnp.float32), -3.0, 3.0) * col_scale
    base_part = 0.9 * jax.random.normal(base_key, (NLAT, 1, D), jnp.float32)
    smooth_part = 0.4 * (wave_coef[0] * first_cos + wave_coef[1] * first_sin)
    values = rough_part + base_part + smooth_part
    return jnp.clip(values, -5.0, 5.0).astype(jnp.bfloat16)


def draw_w_qkv(key, part):
    sign_key, size_key = jax.random.split(jax.random.fold_in(key, 23), 2)
    sign_flip = 2.0 * jax.random.randint(sign_key, (D, 3 * D), 0, 2).astype(jnp.float32) - 1.0
    jitter = jax.random.uniform(size_key, (D, 3 * D), jnp.float32, 1.1, 1.3)
    return (sign_flip * jitter * float(D) ** (-0.5)).astype(jnp.bfloat16)


def draw_key_bias(key, part):
    base_key = jax.random.fold_in(key, 0)
    values = jnp.clip(0.6 * jax.random.normal(base_key, (NLAT, H, NLON), jnp.float32), -3.0, 3.0)
    return values.astype(jnp.bfloat16)


def draw_lat_taps(key, part):
    sign_key, size_key = jax.random.split(key)
    sign_flip = 2.0 * jax.random.randint(sign_key, (TAPS, KB), 0, 2).astype(jnp.float32) - 1.0
    magnitude = jax.random.uniform(size_key, (TAPS, KB), jnp.float32, 0.8, 2.0)
    return sign_flip * magnitude


def draw_lon_half(key, part):
    factor = jax.random.randint(key, (NLAT,), 4, 8)
    band_ids = jnp.arange(NLAT, dtype=jnp.int32)
    from_pole = jnp.minimum(band_ids, NLAT - 1 - band_ids)
    widths = factor * NLON * NLAT // (128 * (2 * from_pole + 1))
    widths = jnp.where(from_pole == 0, NLON // 2, widths)
    return jnp.clip(widths, 1, NLON // 2)


def draw_lat_half(key, part):
    pick_key, zero_key = jax.random.split(jax.random.fold_in(key, 11))
    picked = jax.random.randint(pick_key, (NLAT,), 0, 2)
    band_ids = jnp.arange(NLAT, dtype=jnp.int32)
    centre = NLAT // 2
    near_centre = jnp.abs(band_ids - centre) <= 1
    zero_band = jax.random.randint(zero_key, (), 1, NLAT - 4)
    zero_band = jnp.where(zero_band >= centre - 1, zero_band + 3, zero_band)
    picked = jnp.where(near_centre, 1, picked)
    picked = jnp.where(band_ids == zero_band, 0, picked)
    at_pole = (band_ids == 0) | (band_ids == NLAT - 1)
    return jnp.where(at_pole, 1, picked)


def set_ends(values, rng, least, top_value):
    longest = values.shape.index(max(values.shape))
    spots = []
    for shift in (0, 1):
        where = [jax.random.randint(jax.random.fold_in(rng, axis), (), 0, length) for axis, length in enumerate(values.shape)]
        where[longest] = (where[longest] + shift) % values.shape[longest]
        spots.append(tuple(where))
    return values.at[spots[0]].set(least).at[spots[1]].set(top_value)


def level_of(own_key, dims, pieces, least, high):
    def one(dim, blocks):
        draws = jax.random.uniform(jax.random.fold_in(jax.random.fold_in(own_key, 6), dim), (blocks,), jnp.float32, least / len(pieces), high / len(pieces))
        return jnp.repeat(jnp.exp(draws), dims[dim] // blocks).reshape((-1,) + (1,) * (len(dims) - dim - 1))

    loudness = one(*pieces[0])
    for cut in pieces[1:]:
        loudness = loudness * one(*cut)
    return loudness


def normal_values(stream_key, shape, width, most, cuts=(), held_as=jnp.bfloat16):
    level = level_of(stream_key, shape, cuts, -0.22, 0.18) if cuts else 1.0
    drawn = jax.random.normal(stream_key, shape, jnp.float32) * width * level
    return jnp.minimum(jnp.maximum(drawn, -most), most).astype(held_as)


def setup_inputs(seed: int = 0, part: int = 0) -> dict:
    arg_keys = jax.random.split(jax.random.key(seed), 12)
    part_keys = jax.random.split(jax.random.fold_in(arg_keys[11], part), 12)
    tokens = draw_tokens(jax.random.fold_in(jax.random.fold_in(arg_keys[11], part), 71), part)
    gain_attn = jnp.clip(1.0 + 0.15 * jax.random.normal(arg_keys[1], (D,), jnp.float32), 0.25, 1.75)
    w_qkv = draw_w_qkv(jax.random.fold_in(arg_keys[11], 71), part)
    key_bias = draw_key_bias(jax.random.fold_in(arg_keys[11], 71), part)
    w_out = normal_values(arg_keys[4], (D, D), D ** -0.5, 0.21875, ((0, 8),))
    gain_conv = jnp.clip(1.0 + 0.15 * jax.random.normal(arg_keys[5], (D,), jnp.float32), 0.25, 1.75)
    w_conv = normal_values(arg_keys[6], (KB, D, GW), GW ** -0.5, 0.75)
    lat_taps = draw_lat_taps(jax.random.fold_in(arg_keys[11], 71), part)
    lon_half = draw_lon_half(jax.random.fold_in(arg_keys[11], 71), part)
    lat_half = draw_lat_half(jax.random.fold_in(arg_keys[11], 71), part)
    quad_off = set_ends(jax.random.randint(arg_keys[10], (NLAT,), 0, TAPS - 2), jax.random.fold_in(arg_keys[10], 1), 0, (TAPS - 2) - 1).astype(jnp.int32)
    return dict(tokens=tokens, gain_attn=gain_attn, w_qkv=w_qkv, key_bias=key_bias, w_out=w_out, gain_conv=gain_conv, w_conv=w_conv, lat_taps=lat_taps, lon_half=lon_half, lat_half=lat_half, quad_off=quad_off)


def layer_norm(inputs, gain):
    values = inputs.astype(jnp.float32)
    average = lax.optimization_barrier(jnp.mean(values, axis=-1, keepdims=True))
    centered = values - average
    variance = lax.optimization_barrier(jnp.mean(centered * centered, axis=-1, keepdims=True))
    return centered * lax.rsqrt(variance + 1e-05) * gain

def group_mix(inputs, w_conv):
    basis, length, channels = inputs.shape
    group_width = w_conv.shape[2]
    groups = channels // group_width
    mixed_rows = jnp.einsum('kjgc,kgce->kjge', inputs.reshape(basis, length, groups, group_width).astype(jnp.float32), w_conv.reshape(basis, groups, group_width, group_width).astype(jnp.float32))
    return mixed_rows.reshape(basis, length, channels).astype(jnp.bfloat16)

def lon_weights(row_ids, col_ids, half_width, lon_total):
    offset_lon = jnp.mod(col_ids[None, :] - row_ids[:, None] + lon_total // 2, lon_total) - lon_total // 2
    distance = jnp.abs(offset_lon).astype(jnp.float32)
    span_plus = (half_width + 1).astype(jnp.float32)
    tent_weight = jnp.where(distance <= half_width.astype(jnp.float32), (1.0 - distance / span_plus) / span_plus, 0.0)
    odd_weight = tent_weight * offset_lon.astype(jnp.float32) / span_plus
    return jnp.stack([tent_weight, odd_weight]).astype(jnp.bfloat16)

def reference(tokens, gain_attn, w_qkv, key_bias, w_out, gain_conv, w_conv, lat_taps, lon_half, lat_half, quad_off):
    score_scale = DH ** (-0.5)

    def attend_row(inputs):
        band_tokens, band_bias = inputs
        normed = layer_norm(band_tokens, gain_attn).astype(jnp.bfloat16)
        projected = jnp.dot(normed, w_qkv, preferred_element_type=jnp.float32).astype(jnp.bfloat16)
        queries = projected[:, :D].reshape(NLON, H, DH).astype(jnp.float32)
        key_rows = projected[:, D:2 * D].reshape(NLON, H, DH).astype(jnp.float32)
        value_rows = projected[:, 2 * D:].reshape(NLON, H, DH).astype(jnp.float32)
        scores = jnp.einsum('qhd,khd->hqk', queries, key_rows) * score_scale + band_bias.astype(jnp.float32)[:, None, :]
        exp_scores = jnp.exp(scores - lax.optimization_barrier(jnp.max(scores, axis=-1, keepdims=True)))
        totals = lax.optimization_barrier(jnp.sum(exp_scores, axis=-1))
        weighted = jnp.einsum('hqk,khd->qhd', exp_scores.astype(jnp.bfloat16).astype(jnp.float32), value_rows)
        attended = (weighted / totals.T[:, :, None]).reshape(NLON, D).astype(jnp.bfloat16)
        return (band_tokens.astype(jnp.float32) + jnp.dot(attended, w_out, preferred_element_type=jnp.float32)).astype(jnp.bfloat16)
    middle = lax.map(attend_row, (tokens, key_bias))
    conv_in = lax.map(lambda band_rows: layer_norm(band_rows, gain_conv).astype(jnp.bfloat16), middle)
    zero_row = jnp.zeros((1, NLON, D), jnp.bfloat16)
    padded = jnp.concatenate([zero_row, conv_in, zero_row], axis=0)
    offsets = jnp.arange(3, dtype=jnp.int32) - 1
    lon_ids = jnp.arange(NLON, dtype=jnp.int32)

    def conv_row(band_index):
        stacked = lax.dynamic_slice_in_dim(padded, band_index, 3, 0)
        tap_vals = lat_taps[quad_off[band_index] + offsets + 1]
        tap_vals = jnp.where((jnp.abs(offsets) <= lat_half[band_index])[:, None], tap_vals, 0.0)
        summed = jnp.einsum('rk,rjd->kjd', tap_vals, stacked.astype(jnp.float32), precision=lax.Precision.HIGHEST).astype(jnp.bfloat16)
        own_row = lax.dynamic_index_in_dim(conv_in, band_index, 0, keepdims=False)
        pole_gain = jnp.where(band_index == 0, tap_vals[0], 0.0) + jnp.where(band_index == NLAT - 1, tap_vals[2], 0.0)
        pole_rows = (pole_gain[:, None, None] * own_row.astype(jnp.float32)[None]).astype(jnp.bfloat16)
        mixed_rows = group_mix(summed, w_conv)
        pole_mixed = group_mix(pole_rows, w_conv)
        blended = (mixed_rows.astype(jnp.float32) + jnp.roll(pole_mixed, -(NLON // 2), axis=1).astype(jnp.float32)).astype(jnp.bfloat16)
        coeffs = lon_weights(lon_ids, lon_ids, lon_half[band_index], NLON)
        conv_out = jnp.einsum('kjc,kcd->jd', coeffs.astype(jnp.float32), blended.astype(jnp.float32))
        own_mid = lax.dynamic_index_in_dim(middle, band_index, 0, keepdims=False)
        return (own_mid.astype(jnp.float32) + conv_out).astype(jnp.bfloat16)
    return lax.map(conv_row, jnp.arange(NLAT, dtype=jnp.int32))
```

```python
import jax
import jax.numpy as jnp
from jax import lax
from jax.experimental import pallas as pl
from jax.experimental.pallas import tpu as pltpu
from jax.sharding import PartitionSpec as P


def padded(cells, sides, width):
    for axis, dim in sides:
        count = lax.axis_size(axis)
        ends = count - 1
        head = lax.slice_in_dim(cells, 0, width, axis=dim)
        tail = lax.slice_in_dim(cells, cells.shape[dim] - width, cells.shape[dim], axis=dim)
        cells = jnp.concatenate(
            [
                lax.ppermute(tail, axis, [(i, (i + 1) % count) for i in range(ends)]),
                cells,
                lax.ppermute(head, axis, [((i + 1) % count, i) for i in range(ends)]),
            ],
            axis=dim,
        )
    return cells


def layer_norm(inputs, gain):
    values = inputs.astype(jnp.float32)
    average = jnp.mean(values, axis=-1, keepdims=True)
    centered = values - average
    variance = jnp.mean(centered * centered, axis=-1, keepdims=True)
    return centered * lax.rsqrt(variance + 1e-05) * gain


def group_mix(inputs, w_conv):
    basis, length, channels = inputs.shape
    group_width = w_conv.shape[2]
    groups = channels // group_width
    mixed_rows = jnp.einsum(
        "kjgc,kgce->kjge",
        inputs.reshape(basis, length, groups, group_width),
        w_conv.reshape(basis, groups, group_width, group_width),
        preferred_element_type=jnp.float32,
    )
    return mixed_rows.reshape(basis, length, channels).astype(jnp.bfloat16)


def lon_weights(row_ids, col_ids, half_width, lon_total):
    offset_lon = (
        jnp.mod(col_ids[None, :] - row_ids[:, None] + lon_total // 2, lon_total) - lon_total // 2
    )
    distance = jnp.abs(offset_lon).astype(jnp.float32)
    span_plus = (half_width + 1).astype(jnp.float32)
    tent_weight = jnp.where(
        distance <= half_width.astype(jnp.float32), (1.0 - distance / span_plus) / span_plus, 0.0
    )
    odd_weight = tent_weight * offset_lon.astype(jnp.float32) / span_plus
    return jnp.stack([tent_weight, odd_weight]).astype(jnp.bfloat16)


def start_state(query_count, head_count, head_dim):
    running_max = jnp.full((head_count, query_count), -jnp.inf, jnp.float32)
    running_sum = jnp.zeros((head_count, query_count), jnp.float32)
    running_out = jnp.zeros((query_count, head_count, head_dim), jnp.float32)
    return (running_max, running_sum, running_out)


def attend_keys(carry_state, queries, key_rows, value_rows, bias_rows, score_scale):
    key_count = key_rows.shape[0]
    for offset in range(0, key_count, 128):
        running_max, running_sum, running_out = carry_state
        key_block = key_rows[offset : offset + 128]
        value_block = value_rows[offset : offset + 128]
        bias_block = bias_rows[offset : offset + 128]
        scores = (
            jnp.einsum("qhd,khd->hqk", queries, key_block, preferred_element_type=jnp.float32)
            * score_scale
        )
        scores = scores + bias_block.T.astype(jnp.float32)[:, None, :]
        new_max = jnp.maximum(running_max, jnp.max(scores, axis=-1))
        rescale = jnp.exp(running_max - new_max)
        exp_scores = jnp.exp(scores - new_max[:, :, None])
        running_sum = running_sum * rescale + jnp.sum(exp_scores, axis=-1)
        running_out = running_out * rescale.T[:, :, None] + jnp.einsum(
            "hqk,khd->qhd",
            exp_scores.astype(jnp.bfloat16),
            value_block,
            preferred_element_type=jnp.float32,
        )
        carry_state = (new_max, running_sum, running_out)
    return carry_state


def finish_state(carry_state):
    running_max, running_sum, running_out = carry_state
    finished = running_out / running_sum.T[:, :, None]
    return finished.reshape(finished.shape[0], -1).astype(jnp.bfloat16)


def lon_conv(blended, half_width, first_col, out_cols):
    lon_total = blended.shape[1]
    block_cols = min(128, lon_total)
    block_count = lon_total // block_cols
    first_block = jnp.floor_divide(first_col - half_width, block_cols)
    last_block = jnp.floor_divide(first_col + out_cols - 1 + half_width, block_cols)
    turn_count = jnp.minimum(block_count, last_block - first_block + 1)
    row_ids = first_col + jnp.arange(out_cols, dtype=jnp.int32)

    def add_block(turn_index, running_out):
        block_at = jnp.mod(first_block + turn_index, block_count)
        lon_block = lax.dynamic_slice_in_dim(blended, block_at * block_cols, block_cols, 1)
        col_ids = block_at * block_cols + jnp.arange(block_cols, dtype=jnp.int32)
        coeffs = lon_weights(row_ids, col_ids, half_width, lon_total)
        return running_out + jnp.einsum(
            "kjc,kcd->jd", coeffs, lon_block, preferred_element_type=jnp.float32
        )

    initial = jnp.zeros((out_cols, blended.shape[2]), jnp.float32)
    return lax.fori_loop(0, turn_count, add_block, initial)


def per_device(
    tokens,
    gain_attn,
    w_qkv,
    key_bias,
    w_out,
    gain_conv,
    w_conv,
    lat_taps,
    lon_half,
    lat_half,
    quad_off,
):
    own_tokens = tokens[0]
    count_lon, model_width = own_tokens.shape
    head_count = key_bias.shape[1]
    head_dim = model_width // head_count
    score_scale = head_dim ** (-0.5)
    lon_place = lax.axis_index("lon")
    normed = layer_norm(own_tokens, gain_attn).astype(jnp.bfloat16)
    bias_rows = key_bias[0].T
    full_qkv, full_out = (
        lax.all_gather(w_qkv, "lat", axis=0, tiled=True),
        lax.all_gather(w_out, "lat", axis=0, tiled=True),
    )
    projected = jnp.dot(normed, full_qkv, preferred_element_type=jnp.float32).astype(jnp.bfloat16)
    queries = projected[:, :model_width].reshape(count_lon, head_count, head_dim)
    key_here = projected[:, model_width : 2 * model_width]
    value_here = projected[:, 2 * model_width :]
    key_piece = lax.all_gather(key_here, "lon", axis=0, tiled=True)
    value_piece = lax.all_gather(value_here, "lon", axis=0, tiled=True)
    bias_piece = lax.all_gather(bias_rows, "lon", axis=0, tiled=True)
    length = key_piece.shape[0]
    carry_state = attend_keys(
        start_state(count_lon, head_count, head_dim),
        queries,
        key_piece.reshape(length, head_count, head_dim),
        value_piece.reshape(length, head_count, head_dim),
        bias_piece,
        score_scale,
    )
    attended = finish_state(carry_state)
    branch_out = jnp.dot(attended, full_out, preferred_element_type=jnp.float32)
    middle = (own_tokens.astype(jnp.float32) + branch_out).astype(jnp.bfloat16)
    conv_in = layer_norm(middle, gain_conv).astype(jnp.bfloat16)
    stacked = padded(conv_in[None], (("lat", 0),), 1)
    lat_row = lax.axis_index("lat")
    last_band = lax.axis_size("lat") - 1
    offsets = jnp.arange(3, dtype=jnp.int32) - 1
    one_hot = (
        (quad_off[0] + offsets + 1)[:, None]
        == jnp.arange(lat_taps.shape[0], dtype=jnp.int32)[None, :]
    ).astype(jnp.float32)
    tap_vals = jnp.dot(one_hot, lat_taps, precision=lax.Precision.HIGHEST)
    tap_vals = jnp.where((jnp.abs(offsets) <= lat_half[0])[:, None], tap_vals, 0.0)
    summed = jnp.einsum(
        "rk,rjd->kjd", tap_vals, stacked.astype(jnp.float32), precision=lax.Precision.HIGHEST
    ).astype(jnp.bfloat16)
    pole_gain = jnp.where(lat_row == 0, tap_vals[0], 0.0) + jnp.where(
        lat_row == last_band, tap_vals[2], 0.0
    )
    first_col = lon_place * count_lon
    pole_rows = (pole_gain[:, None, None] * conv_in.astype(jnp.float32)[None]).astype(jnp.bfloat16)
    mixed_rows = group_mix(summed, w_conv)
    pole_mixed = group_mix(pole_rows, w_conv)
    circle_rows, pole_all = (
        lax.all_gather(mixed_rows, "lon", axis=1, tiled=True),
        lax.all_gather(pole_mixed, "lon", axis=1, tiled=True),
    )
    lon_total = circle_rows.shape[1]
    blended = (
        circle_rows.astype(jnp.float32)
        + jnp.roll(pole_all, -(lon_total // 2), axis=1).astype(jnp.float32)
    ).astype(jnp.bfloat16)
    conv_out = lon_conv(blended, lon_half[0], first_col, count_lon)
    return (middle.astype(jnp.float32) + conv_out).astype(jnp.bfloat16)[None]


BF = jnp.bfloat16
F32 = jnp.float32
MESH = pl.DeviceIdType.MESH


def norm_rows(values, gain):
    values = values.astype(F32)
    average = jnp.mean(values, axis=-1, keepdims=True)
    centered = values - average
    variance = jnp.mean(centered * centered, axis=-1, keepdims=True)
    return (centered * lax.rsqrt(variance + 1e-05) * gain).astype(BF)


def fused_kernel(
    nx, nz,
    lat_taps_h, lon_half_h, lat_half_h, quad_off_h,
    tokens_h, gain_attn_h, w_qkv_h, key_bias_h, w_out_h, gain_conv_h, w_conv_h,
    out,
    lat_taps, lon_half, lat_half, quad_off, gain_attn, w_qkv, gain_conv, w_conv, load,
    ws, wq, wo, tok, normed, bias, bias_f, att_out, att_in, stage, normed_conv, middle, mid_rows,
    mixer, polar, mixed, coeff, done_out, done_in,
    xq_send, xq_recv, dq_send, zq_send, zq_recv, yq_send, yq_recv,
    xo_send, xo_recv, do_send, zo_send, zo_recv, yo_send, yo_recv, so_send, so_recv,
    t_send, t_recv, b_send, b_recv, a_send, a_recv,
    c_send, c_recv, h_send, h_recv,
):
    y, place, c = lax.axis_index("groups"), lax.axis_index("lat"), lax.axis_index("lon")
    z, x = lax.div(place, nx), lax.rem(place, nx)
    quad = x * 2 + c
    x_place = z * nx + (1 - x)
    x_peer, x_diag = (y, x_place, c), (y, x_place, 1 - c)
    sibling = (y, place, 1 - c)
    y_peer = (1 - y, place, c)
    z_up, z_down = (y, place + nx, c), (y, place - nx, c)
    has_up, has_down = z < nz - 1, z > 0
    last_place = nx * nz - 1
    shard = w_qkv.shape[0]
    hs = shard // 2
    width = tokens_h.shape[1]
    rows = tokens_h.shape[0]
    head = 64
    part = width // 4
    half = width // 2

    barrier = pltpu.get_barrier_semaphore()

    def greet(device):
        pl.semaphore_signal(barrier, inc=1, device_id=device, device_id_type=MESH)

    def when(cond, run):
        if cond is None:
            run()
        else:
            pl.when(cond)(run)

    for device in (x_peer, x_diag, sibling, y_peer):
        greet(device)
    leap = nz - 1
    aims = [(has_up, z + 1), (z >= leap, z - leap), (has_down, z - 1)]
    for cond, zz in ((has_up, z + 1), (has_down, z - 1), (z < nz - leap, z + leap)):
        def both(zz=zz):
            greet((y, zz * nx, c))
            greet((y, zz * nx + 1, c))

        when(cond, both)
    for cond, shift in ((has_up, nx), (has_down, -nx)):
        when(cond, lambda shift=shift: greet((y, place + shift, 1 - c)))

    loads = [
        pltpu.make_async_copy(source, target, load.at[k])
        for k, (source, target) in enumerate(
            (
                (w_qkv_h.at[pl.ds(y * hs, hs), :], w_qkv.at[pl.ds(y * hs, hs), :]),
                (tokens_h, tok.at[x, pl.ds(c * rows, rows), :]),
                (gain_attn_h, gain_attn),
                (w_conv_h.at[:, :, pl.ds(c * half, half)], w_conv),
                (key_bias_h, bias.at[x, c]),
                (w_out_h, wo.at[pl.ds(place * shard, shard), :]),
                (gain_conv_h, gain_conv),
                (lat_taps_h, lat_taps),
                (lon_half_h, lon_half),
                (lat_half_h, lat_half),
                (quad_off_h, quad_off),
                (w_qkv_h.at[pl.ds((1 - y) * hs, hs), :], w_qkv.at[pl.ds((1 - y) * hs, hs), :]),
            )
        )
    ]
    loads[0].start()
    loads[1].start()
    loads[11].start()
    for copy in loads[2:11]:
        copy.start()

    def columns(pick, h):
        return jnp.concatenate(
            [
                w_qkv[pl.ds(h * hs, hs), j * width + pick * part : j * width + (pick + 1) * part]
                for j in range(3)
            ],
            axis=1,
        )

    def spread(h):
        for pick in range(4):
            @pl.when(quad == pick)
            def _(pick=pick):
                ws[pl.ds(h * hs, hs), :] = columns((pick + 2) % 4, h)
                wq[pl.ds(place * shard + h * hs, hs), :] = columns(pick, h)

    loads[0].wait()
    spread(y)
    pl.semaphore_wait(
        barrier,
        4 + 3 * has_up.astype(jnp.int32) + 3 * has_down.astype(jnp.int32) + 2 * (z >= leap).astype(jnp.int32),
    )

    def remote(source, target, send, recv, device):
        return pltpu.make_async_remote_copy(
            src_ref=source, dst_ref=target, send_sem=send, recv_sem=recv,
            device_id=device, device_id_type=MESH,
        )

    start = lambda d: d.start()
    finish = lambda d: d.wait_send()

    def q_at(slot, h):
        return wq.at[pl.ds(slot * shard + h * hs, hs), :]

    def o_at(slot, h, cc):
        return wo.at[pl.ds(slot * shard + h * hs, hs), pl.ds(cc * half, half)]

    def q_cross(k):
        h = y if k == 0 else 1 - y
        return remote(ws.at[pl.ds(h * hs, hs), :], q_at(place, h), xq_send.at[k], xq_recv.at[k], x_peer)

    def q_crossed(k):
        h = y if k == 0 else 1 - y
        return remote(ws.at[pl.ds(h * hs, hs), :], q_at(x_place, h), xq_send.at[k], xq_recv.at[k], x_peer)

    def q_direct(zz, other):
        xx = (1 - x) if other else x
        source = ws.at[pl.ds(y * hs, hs), :] if other else q_at(place, y)
        return remote(
            source, q_at(place, y), dq_send.at[zz * nx + xx], zq_recv.at[place],
            (y, zz * nx + xx, c),
        )

    def q_along(slot, device):
        return remote(q_at(slot, y), q_at(slot, y), zq_send.at[slot], zq_recv.at[slot], device)

    def q_over(slot, h):
        return remote(q_at(slot, h), q_at(slot, h), yq_send.at[slot], yq_recv.at[slot], y_peer)

    def o_cross(slot, k):
        h = y if k == 0 else 1 - y
        return remote(o_at(slot, h, c), o_at(slot, h, c), xo_send.at[k], xo_recv.at[k], x_peer)

    def o_direct(zz, other):
        xx = (1 - x) if other else x
        return remote(
            o_at(place, y, c), o_at(place, y, c), do_send.at[zz * nx + xx], zo_recv.at[place],
            (y, zz * nx + xx, c),
        )

    def o_along(slot, device):
        return remote(o_at(slot, y, c), o_at(slot, y, c), zo_send.at[slot], zo_recv.at[slot], device)

    def o_over(slot, h):
        return remote(o_at(slot, h, c), o_at(slot, h, c), yo_send.at[slot], yo_recv.at[slot], y_peer)

    def o_side(slot, h, cc):
        return remote(
            o_at(slot, h, cc), o_at(slot, h, cc), so_send.at[slot, h], so_recv.at[slot, h], sibling
        )

    def deal(direct, act):
        for cond, zz in aims:
            def both(zz=zz):
                act(direct(zz, True))
                act(direct(zz, False))

            when(cond, both)

    far = []
    for t in range(1, nz):
        for sign, reach, going, device in (
            (-1, z >= t, has_up, z_up),
            (1, z + t <= nz - 1, has_down if 1 <= t < leap - 1 else None, z_down),
        ):
            for xx in (x, 1 - x):
                far.append(
                    (
                        t, reach, (z + sign * t) * nx + xx,
                        None if going is None else jnp.logical_and(reach, going), device,
                    )
                )

    def q_step(t, act):
        for tt, reach, slot, going, device in far:
            if tt == t:
                if act is start:
                    when(reach, lambda slot=slot: q_along(slot, z_up).wait_recv())
                if going is not None:
                    when(going, lambda slot=slot, device=device: act(q_along(slot, device)))
                when(reach, lambda slot=slot: act(q_over(slot, y)))

    def o_step(t, act):
        for tt, reach, slot, going, device in far:
            if tt == t:
                if act is start:
                    when(reach, lambda slot=slot: o_along(slot, z_up).wait_recv())
                if going is not None:
                    when(going, lambda slot=slot, device=device: act(o_along(slot, device)))
                when(reach, lambda slot=slot: act(o_over(slot, y)))
                when(reach, lambda slot=slot: act(o_side(slot, y, c)))

    def o_gather(act):
        for _, reach, slot, _, _ in far:
            if act is start:
                when(reach, lambda slot=slot: o_over(slot, 1 - y).wait_recv())
            when(reach, lambda slot=slot: act(o_side(slot, 1 - y, c)))

    def o_near(act):
        for k, h in ((0, y), (1, 1 - y)):
            if act is start:
                o_cross(x_place, k).wait_recv()
            act(o_side(x_place, h, c))

    def tok_at(b, cc):
        return tok.at[b, pl.ds(cc * rows, rows), :]

    tok_copies = [
        remote(tok_at(x, c), tok_at(x, c), t_send.at[0], t_recv.at[0], x_peer),
        remote(tok_at(x, c), tok_at(x, c), t_send.at[1], t_recv.at[1], sibling),
        remote(tok_at(1 - x, c), tok_at(1 - x, c), t_send.at[2], t_recv.at[2], sibling),
    ]
    bias_copies = [
        remote(bias.at[x, c], bias.at[x, c], b_send.at[k], b_recv.at[k], device)
        for k, device in enumerate((x_peer, sibling, x_diag))
    ]

    deal(q_direct, start)
    loads[1].wait()
    tok_copies[1].start()
    tok_copies[0].start()
    loads[11].wait()
    spread(1 - y)
    q_cross(0).start()
    q_cross(1).start()
    loads[4].wait()
    for copy in bias_copies:
        copy.start()
    loads[2].wait()
    gain_a = gain_attn[...][None]

    def norm_block(b, cc):
        normed[b, pl.ds(cc * rows, rows), :] = norm_rows(tok[b, pl.ds(cc * rows, rows), :], gain_a)

    norm_block(x, c)
    tok_copies[1].wait_recv()
    norm_block(x, 1 - c)
    q_step(1, start)
    tok_copies[0].wait_recv()
    tok_copies[2].start()
    loads[5].wait()
    deal(o_direct, start)
    o_cross(place, 0).start()
    o_cross(place, 1).start()
    norm_block(1 - x, c)
    q_step(2, start)
    tok_copies[2].wait_recv()
    norm_block(1 - x, 1 - c)
    q_step(3, start)
    o_near(start)

    loads[3].wait()
    pair_row = lax.broadcasted_iota(jnp.int32, (2 * head, half), 0)
    pair_col = lax.broadcasted_iota(jnp.int32, (2 * head, half), 1)
    same = lax.rem(lax.div(pair_col, head), 2) == lax.div(pair_row, head)
    for b in range(2):
        wide = jnp.concatenate([w_conv[b], w_conv[b]], axis=0).astype(F32)
        mixer[b] = jnp.where(same, wide, 0.0).astype(BF)
    for copy in bias_copies:
        copy.wait_recv()
    for b in range(2):
        bias_f[b] = jnp.concatenate([bias[b, 0], bias[b, 1]], axis=1).astype(F32)
    for k in range(6, 11):
        loads[k].wait()

    o_step(1, start)
    q_crossed(0).wait_recv()
    q_crossed(1).wait_recv()
    for _, reach, slot, _, _ in far:
        when(reach, lambda slot=slot: q_over(slot, 1 - y).wait_recv())

    def att_copies(b, n):
        return [
            remote(
                att_out.at[b, pl.ds(cc * rows, rows), :], att_in.at[b, quad],
                a_send.at[n, k], a_recv.at[b, quad], device,
            )
            for k, (cc, device) in enumerate(((c, x_peer), (1 - c, x_diag), (1 - c, sibling)))
        ]

    def attend(b, between):
        projected = jnp.dot(normed[b], wq[...], preferred_element_type=F32).astype(BF)
        between()
        pieces = []
        for h in range(3):
            queries = projected[:, h * head : (h + 1) * head] * jnp.asarray(head ** -0.5, BF)
            keys = projected[:, part + h * head : part + (h + 1) * head]
            vals = projected[:, 2 * part + h * head : 2 * part + (h + 1) * head]
            scores = lax.dot_general(
                queries, keys, (((1,), (1,)), ((), ())), preferred_element_type=F32
            ) + bias_f[b, pl.ds(quad * 3 + h, 1), :]
            expd = jnp.exp(scores - jnp.max(scores, axis=-1, keepdims=True))
            totals = jnp.sum(expd, axis=-1, keepdims=True)
            pieces.append(jnp.dot(expd.astype(BF), vals, preferred_element_type=F32) / totals)
        att_out[b] = jnp.concatenate(pieces, axis=1).astype(BF)

    attend(x, lambda: None)
    for copy in att_copies(x, 0):
        copy.start()
    att_in[x, quad] = att_out[x, pl.ds(c * rows, rows), :]
    o_step(2, start)
    attend(1 - x, lambda: None)
    for copy in att_copies(1 - x, 1):
        copy.start()
    att_in[1 - x, quad] = att_out[1 - x, pl.ds(c * rows, rows), :]
    o_step(3, start)
    o_gather(start)

    span = (lon_half[0] + 1).astype(F32)
    limit = lon_half[0].astype(F32)
    lons = 2 * rows
    diff = lax.broadcasted_iota(jnp.int32, (lons, lons), 1) - lax.broadcasted_iota(
        jnp.int32, (lons, lons), 0
    )
    offset = jnp.where(diff >= rows, diff - lons, jnp.where(diff < -rows, diff + lons, diff))
    offset = offset.astype(F32)
    distance = jnp.abs(offset)
    tent = jnp.where(distance <= limit, (1.0 - distance / span) / span, 0.0)
    coeff[:, :lons] = tent.astype(BF)
    coeff[:, lons:] = (tent * offset / span).astype(BF)

    for _, reach, slot, _, _ in far:
        def landed(slot=slot):
            o_side(slot, 0, 1 - c).wait_recv()
            o_side(slot, 1, 1 - c).wait_recv()

        when(reach, landed)
    o_side(x_place, 0, 1 - c).wait_recv()
    o_side(x_place, 1, 1 - c).wait_recv()

    near, away = 2 * (1 - x), 2 * x
    passes = jnp.logical_or(jnp.logical_and(x == 0, has_up), jnp.logical_and(x == 1, has_down))
    gets = jnp.logical_or(jnp.logical_and(x == 0, has_down), jnp.logical_and(x == 1, has_up))
    onward = place + nx * (1 - 2 * x)

    def band(b):
        for source in (x * 2 + 1 - c, (1 - x) * 2 + c, (1 - x) * 2 + 1 - c):
            remote(att_in.at[b, source], att_in.at[b, source], a_send.at[0, 0], a_recv.at[b, source], sibling).wait_recv()
        branch = tok[b, pl.ds(c * rows, rows), :].astype(F32)
        for p in range(4):
            branch = branch + jnp.dot(
                att_in[b, p], wo[p * part : (p + 1) * part, :], preferred_element_type=F32
            )
        return branch.astype(BF)

    gain_c = gain_conv[...][None]
    own_rows = pl.ds(c * rows, rows)
    side_rows = pl.ds((1 - c) * rows, rows)
    own_cols = pl.ds(c * half, half)
    side_cols = pl.ds((1 - c) * half, half)

    def conv_copy(source, which, cc, k, device):
        return remote(
            source, normed_conv.at[which, pl.ds(cc * rows, rows), :],
            c_send.at[k], c_recv.at[which, cc], device,
        )

    stage[0] = norm_rows(band(1 - x), gain_c)
    to_far = [
        conv_copy(stage.at[0, :, own_cols], away, c, 0, (y, onward, c)),
        conv_copy(stage.at[0, :, side_cols], away, c, 1, (y, onward, 1 - c)),
    ]

    @pl.when(passes)
    def _():
        for d in to_far:
            d.start()

    to_side = [conv_copy(stage.at[0, :, side_cols], near, c, 2, sibling)]
    to_side[0].start()
    normed_conv[near, own_rows, :] = stage[0, :, own_cols]

    mid = band(x)
    middle[...] = mid
    stage[1] = norm_rows(mid, gain_c)
    to_side.append(conv_copy(stage.at[1, :, side_cols], 1, c, 3, sibling))
    to_side[1].start()
    to_mid = remote(middle.at[:, side_cols], mid_rows.at[own_rows, :], h_send.at[0], h_recv.at[0], sibling)
    to_mid.start()
    normed_conv[1, own_rows, :] = stage[1, :, own_cols]
    mid_rows[own_rows, :] = middle[:, own_cols]

    @pl.when(jnp.logical_not(gets))
    def _():
        normed_conv[away] = jnp.zeros((lons, half), BF)

    base = quad_off[0]
    wide_ok = lat_half[0] >= 1
    taps = [
        [
            lat_taps[b, base + r] if r == 1 else jnp.where(wide_ok, lat_taps[b, base + r], 0.0)
            for b in range(2)
        ]
        for r in range(3)
    ]

    def mix(values, b):
        return jnp.concatenate(
            [
                lax.dot_general(
                    values[:, p * 2 * head : (p + 1) * 2 * head],
                    mixer[b, :, p * 2 * head : (p + 1) * 2 * head],
                    (((1,), (1,)), ((), ())),
                    preferred_element_type=F32,
                )
                for p in range(half // (2 * head))
            ],
            axis=1,
        ).astype(BF)

    conv_copy(stage.at[1, :, side_cols], 1, 1 - c, 3, sibling).wait_recv()
    for b in range(2):
        gain = jnp.where(place == 0, taps[0][b], 0.0) + jnp.where(place == last_place, taps[2][b], 0.0)
        pole = mix((gain * normed_conv[1].astype(F32)).astype(BF), b)
        polar[b, :rows] = pole[rows:]
        polar[b, rows:] = pole[:rows]
    conv_copy(stage.at[0, :, side_cols], near, 1 - c, 2, sibling).wait_recv()
    remote(middle.at[:, side_cols], mid_rows.at[side_rows, :], h_send.at[0], h_recv.at[0], sibling).wait_recv()

    @pl.when(gets)
    def _():
        conv_copy(stage.at[0, :, own_cols], away, 0, 0, sibling).wait_recv()
        conv_copy(stage.at[0, :, own_cols], away, 1, 0, sibling).wait_recv()

    for b in range(2):
        summed = (
            taps[0][b] * normed_conv[0].astype(F32)
            + taps[1][b] * normed_conv[1].astype(F32)
            + taps[2][b] * normed_conv[2].astype(F32)
        ).astype(BF)
        mixed[b * lons : (b + 1) * lons, :] = (
            mix(summed, b).astype(F32) + polar[b].astype(F32)
        ).astype(BF)

    def convolve(at):
        return (
            mid_rows[at, :].astype(F32)
            + jnp.dot(coeff[at, :], mixed[...], preferred_element_type=F32)
        ).astype(BF)

    done_out[...] = convolve(side_rows)
    to_done = remote(done_out, done_in, h_send.at[1], h_recv.at[1], sibling)
    to_done.start()
    out[:, own_cols] = convolve(own_rows)

    q_cross(0).wait_send()
    q_cross(1).wait_send()
    o_cross(place, 0).wait_send()
    o_cross(place, 1).wait_send()
    deal(q_direct, finish)
    deal(o_direct, finish)
    o_near(finish)
    for t in range(1, nz):
        q_step(t, finish)
        o_step(t, finish)
    o_gather(finish)
    for d in tok_copies + bias_copies + att_copies(x, 0) + att_copies(1 - x, 1) + to_side + [to_mid]:
        d.wait_send()

    @pl.when(passes)
    def _():
        for d in to_far:
            d.wait_send()

    to_done.wait_recv()
    out[:, side_cols] = done_in[...]
    to_done.wait_send()


def in_hbm(value):
    return pltpu.with_memory_space_constraint(value, pltpu.HBM)


def fused_device(
    tokens, gain_attn, w_qkv, key_bias, w_out, gain_conv, w_conv, lat_taps, lon_half, lat_half, quad_off
):
    rows, width = tokens.shape[1:]
    shard = w_qkv.shape[0]
    heads = key_bias.shape[1]
    lat_count = width // shard
    nx = 2
    nz = lat_count // nx
    part, half, lons = width // 4, width // 2, 2 * rows
    vmem = pl.BlockSpec(memory_space=pltpu.VMEM)
    anywhere = pl.BlockSpec(memory_space=pltpu.HBM)
    dma = pltpu.SemaphoreType.DMA
    out = pl.pallas_call(
        lambda *refs: fused_kernel(nx, nz, *refs),
        out_shape=pltpu.VMEM((rows, width), BF),
        in_specs=[anywhere] * 11,
        out_specs=vmem,
        scratch_shapes=[
            pltpu.SMEM((2, lat_taps.shape[0]), F32),
            pltpu.SMEM((1,), jnp.int32),
            pltpu.SMEM((1,), jnp.int32),
            pltpu.SMEM((1,), jnp.int32),
            pltpu.VMEM((width,), F32),
            pltpu.VMEM(w_qkv.shape, BF),
            pltpu.VMEM((width,), F32),
            pltpu.VMEM((2, 64, half), BF),
            dma((12,)),
            pltpu.VMEM((shard, 3 * part), BF),
            pltpu.VMEM((width, 3 * part), BF),
            pltpu.VMEM((width, width), BF),
            pltpu.VMEM((2, lons, width), BF),
            pltpu.VMEM((2, lons, width), BF),
            pltpu.VMEM((2, 2, heads, rows), BF),
            pltpu.VMEM((2, heads, lons), F32),
            pltpu.VMEM((2, lons, part), BF),
            pltpu.VMEM((2, 4, rows, part), BF),
            pltpu.VMEM((2, rows, width), BF),
            pltpu.VMEM((3, lons, half), BF),
            pltpu.VMEM((rows, width), BF),
            pltpu.VMEM((lons, half), BF),
            pltpu.VMEM((2, 128, half), BF),
            pltpu.VMEM((2, lons, half), BF),
            pltpu.VMEM((2 * lons, half), BF),
            pltpu.VMEM((lons, 2 * lons), BF),
            pltpu.VMEM((rows, half), BF),
            pltpu.VMEM((rows, half), BF),
            dma((2,)), dma((2,)),
            dma((lat_count,)), dma((lat_count,)), dma((lat_count,)),
            dma((lat_count,)), dma((lat_count,)),
            dma((2,)), dma((2,)),
            dma((lat_count,)), dma((lat_count,)), dma((lat_count,)),
            dma((lat_count,)), dma((lat_count,)),
            dma((lat_count, 2)), dma((lat_count, 2)),
            dma((3,)), dma((3,)),
            dma((3,)), dma((3,)),
            dma((2, 3)), dma((2, 4)),
            dma((4,)), dma((3, 2)),
            dma((2,)), dma((2,)),
        ],
        compiler_params=pltpu.CompilerParams(
            collective_id=0, has_side_effects=True, vmem_limit_bytes=40 * 1024 * 1024
        ),
    )(
        in_hbm(lat_taps.T), lon_half, lat_half, quad_off,
        *[
            in_hbm(v)
            for v in (
                tokens[0], gain_attn, w_qkv, key_bias[0], w_out, gain_conv, jnp.swapaxes(w_conv, 1, 2)
            )
        ],
    )
    return out[None]


def solution(mesh):
    sizes = (mesh.shape["groups"], mesh.shape["lat"], mesh.shape["lon"])
    return jax.shard_map(
        fused_device if sizes == (2, 8, 2) else per_device,
        mesh=mesh,
        in_specs=(
            P(("groups", "lat"), "lon", None),
            P(),
            P("lat", None),
            P("lat", None, "lon"),
            P("lat", None),
            P(),
            P(),
            P(),
            P("lat"),
            P("lat"),
            P("lat"),
        ),
        out_specs=P(("groups", "lat"), "lon", None),
        check_vma=False,
    )
```

```python
import jax
import jax.numpy as jnp
from jax import lax
from jax.experimental import pallas as pl
from jax.experimental.pallas import tpu as pltpu
from jax.sharding import PartitionSpec as P


def padded(cells, sides, width):
    for axis, dim in sides:
        count = lax.axis_size(axis)
        ends = count - 1
        head = lax.slice_in_dim(cells, 0, width, axis=dim)
        tail = lax.slice_in_dim(cells, cells.shape[dim] - width, cells.shape[dim], axis=dim)
        cells = jnp.concatenate(
            [
                lax.ppermute(tail, axis, [(i, (i + 1) % count) for i in range(ends)]),
                cells,
                lax.ppermute(head, axis, [((i + 1) % count, i) for i in range(ends)]),
            ],
            axis=dim,
        )
    return cells


def layer_norm(inputs, gain):
    values = inputs.astype(jnp.float32)
    average = jnp.mean(values, axis=-1, keepdims=True)
    centered = values - average
    variance = jnp.mean(centered * centered, axis=-1, keepdims=True)
    return centered * lax.rsqrt(variance + 1e-05) * gain


def group_mix(inputs, w_conv):
    basis, length, channels = inputs.shape
    group_width = w_conv.shape[2]
    groups = channels // group_width
    mixed_rows = jnp.einsum(
        "kjgc,kgce->kjge",
        inputs.reshape(basis, length, groups, group_width),
        w_conv.reshape(basis, groups, group_width, group_width),
        preferred_element_type=jnp.float32,
    )
    return mixed_rows.reshape(basis, length, channels).astype(jnp.bfloat16)


def lon_weights(row_ids, col_ids, half_width, lon_total):
    offset_lon = (
        jnp.mod(col_ids[None, :] - row_ids[:, None] + lon_total // 2, lon_total) - lon_total // 2
    )
    distance = jnp.abs(offset_lon).astype(jnp.float32)
    span_plus = (half_width + 1).astype(jnp.float32)
    tent_weight = jnp.where(
        distance <= half_width.astype(jnp.float32), (1.0 - distance / span_plus) / span_plus, 0.0
    )
    odd_weight = tent_weight * offset_lon.astype(jnp.float32) / span_plus
    return jnp.stack([tent_weight, odd_weight]).astype(jnp.bfloat16)


def start_state(query_count, head_count, head_dim):
    running_max = jnp.full((head_count, query_count), -jnp.inf, jnp.float32)
    running_sum = jnp.zeros((head_count, query_count), jnp.float32)
    running_out = jnp.zeros((query_count, head_count, head_dim), jnp.float32)
    return (running_max, running_sum, running_out)


def attend_keys(carry_state, queries, key_rows, value_rows, bias_rows, score_scale):
    key_count = key_rows.shape[0]
    for offset in range(0, key_count, 128):
        running_max, running_sum, running_out = carry_state
        key_block = key_rows[offset : offset + 128]
        value_block = value_rows[offset : offset + 128]
        bias_block = bias_rows[offset : offset + 128]
        scores = (
            jnp.einsum("qhd,khd->hqk", queries, key_block, preferred_element_type=jnp.float32)
            * score_scale
        )
        scores = scores + bias_block.T.astype(jnp.float32)[:, None, :]
        new_max = jnp.maximum(running_max, jnp.max(scores, axis=-1))
        rescale = jnp.exp(running_max - new_max)
        exp_scores = jnp.exp(scores - new_max[:, :, None])
        running_sum = running_sum * rescale + jnp.sum(exp_scores, axis=-1)
        running_out = running_out * rescale.T[:, :, None] + jnp.einsum(
            "hqk,khd->qhd",
            exp_scores.astype(jnp.bfloat16),
            value_block,
            preferred_element_type=jnp.float32,
        )
        carry_state = (new_max, running_sum, running_out)
    return carry_state


def finish_state(carry_state):
    running_max, running_sum, running_out = carry_state
    finished = running_out / running_sum.T[:, :, None]
    return finished.reshape(finished.shape[0], -1).astype(jnp.bfloat16)


def lon_conv(blended, half_width, first_col, out_cols):
    lon_total = blended.shape[1]
    block_cols = min(128, lon_total)
    block_count = lon_total // block_cols
    first_block = jnp.floor_divide(first_col - half_width, block_cols)
    last_block = jnp.floor_divide(first_col + out_cols - 1 + half_width, block_cols)
    turn_count = jnp.minimum(block_count, last_block - first_block + 1)
    row_ids = first_col + jnp.arange(out_cols, dtype=jnp.int32)

    def add_block(turn_index, running_out):
        block_at = jnp.mod(first_block + turn_index, block_count)
        lon_block = lax.dynamic_slice_in_dim(blended, block_at * block_cols, block_cols, 1)
        col_ids = block_at * block_cols + jnp.arange(block_cols, dtype=jnp.int32)
        coeffs = lon_weights(row_ids, col_ids, half_width, lon_total)
        return running_out + jnp.einsum(
            "kjc,kcd->jd", coeffs, lon_block, preferred_element_type=jnp.float32
        )

    initial = jnp.zeros((out_cols, blended.shape[2]), jnp.float32)
    return lax.fori_loop(0, turn_count, add_block, initial)


def per_device(
    tokens,
    gain_attn,
    w_qkv,
    key_bias,
    w_out,
    gain_conv,
    w_conv,
    lat_taps,
    lon_half,
    lat_half,
    quad_off,
):
    own_tokens = tokens[0]
    count_lon, model_width = own_tokens.shape
    head_count = key_bias.shape[1]
    head_dim = model_width // head_count
    score_scale = head_dim ** (-0.5)
    lon_place = lax.axis_index("lon")
    normed = layer_norm(own_tokens, gain_attn).astype(jnp.bfloat16)
    bias_rows = key_bias[0].T
    full_qkv, full_out = (
        lax.all_gather(w_qkv, "lat", axis=0, tiled=True),
        lax.all_gather(w_out, "lat", axis=0, tiled=True),
    )
    projected = jnp.dot(normed, full_qkv, preferred_element_type=jnp.float32).astype(jnp.bfloat16)
    queries = projected[:, :model_width].reshape(count_lon, head_count, head_dim)
    key_here = projected[:, model_width : 2 * model_width]
    value_here = projected[:, 2 * model_width :]
    key_piece = lax.all_gather(key_here, "lon", axis=0, tiled=True)
    value_piece = lax.all_gather(value_here, "lon", axis=0, tiled=True)
    bias_piece = lax.all_gather(bias_rows, "lon", axis=0, tiled=True)
    length = key_piece.shape[0]
    carry_state = attend_keys(
        start_state(count_lon, head_count, head_dim),
        queries,
        key_piece.reshape(length, head_count, head_dim),
        value_piece.reshape(length, head_count, head_dim),
        bias_piece,
        score_scale,
    )
    attended = finish_state(carry_state)
    branch_out = jnp.dot(attended, full_out, preferred_element_type=jnp.float32)
    middle = (own_tokens.astype(jnp.float32) + branch_out).astype(jnp.bfloat16)
    conv_in = layer_norm(middle, gain_conv).astype(jnp.bfloat16)
    stacked = padded(conv_in[None], (("lat", 0),), 1)
    lat_row = lax.axis_index("lat")
    last_band = lax.axis_size("lat") - 1
    offsets = jnp.arange(3, dtype=jnp.int32) - 1
    one_hot = (
        (quad_off[0] + offsets + 1)[:, None]
        == jnp.arange(lat_taps.shape[0], dtype=jnp.int32)[None, :]
    ).astype(jnp.float32)
    tap_vals = jnp.dot(one_hot, lat_taps, precision=lax.Precision.HIGHEST)
    tap_vals = jnp.where((jnp.abs(offsets) <= lat_half[0])[:, None], tap_vals, 0.0)
    summed = jnp.einsum(
        "rk,rjd->kjd", tap_vals, stacked.astype(jnp.float32), precision=lax.Precision.HIGHEST
    ).astype(jnp.bfloat16)
    pole_gain = jnp.where(lat_row == 0, tap_vals[0], 0.0) + jnp.where(
        lat_row == last_band, tap_vals[2], 0.0
    )
    first_col = lon_place * count_lon
    pole_rows = (pole_gain[:, None, None] * conv_in.astype(jnp.float32)[None]).astype(jnp.bfloat16)
    mixed_rows = group_mix(summed, w_conv)
    pole_mixed = group_mix(pole_rows, w_conv)
    circle_rows, pole_all = (
        lax.all_gather(mixed_rows, "lon", axis=1, tiled=True),
        lax.all_gather(pole_mixed, "lon", axis=1, tiled=True),
    )
    lon_total = circle_rows.shape[1]
    blended = (
        circle_rows.astype(jnp.float32)
        + jnp.roll(pole_all, -(lon_total // 2), axis=1).astype(jnp.float32)
    ).astype(jnp.bfloat16)
    conv_out = lon_conv(blended, lon_half[0], first_col, count_lon)
    return (middle.astype(jnp.float32) + conv_out).astype(jnp.bfloat16)[None]


BF = jnp.bfloat16
F32 = jnp.float32
MESH = pl.DeviceIdType.MESH


def norm_rows(values, gain):
    values = values.astype(F32)
    average = jnp.mean(values, axis=-1, keepdims=True)
    centered = values - average
    variance = jnp.mean(centered * centered, axis=-1, keepdims=True)
    return (centered * lax.rsqrt(variance + 1e-05) * gain).astype(BF)


def fused_kernel(
    nx, nz,
    lat_taps_h, lon_half_h, lat_half_h, quad_off_h,
    tokens_h, gain_attn_h, w_qkv_h, key_bias_h, w_out_h, gain_conv_h, w_conv_h,
    out,
    lat_taps, lon_half, lat_half, quad_off, gain_attn, w_qkv, gain_conv, w_conv, load,
    ws, wq, wo, tok, normed, bias, bias_f, att_out, att_in, stage, normed_conv, middle, mid_rows,
    mixer, polar, mixed, coeff, done_out, done_in,
    xq_send, xq_recv, dq_send, zq_send, zq_recv, yq_send, yq_recv,
    xo_send, xo_recv, do_send, zo_send, zo_recv, yo_send, yo_recv, so_send, so_recv,
    t_send, t_recv, b_send, b_recv, a_send, a_recv,
    c_send, c_recv, h_send, h_recv,
):
    y, place, c = lax.axis_index("groups"), lax.axis_index("lat"), lax.axis_index("lon")
    z, x = lax.div(place, nx), lax.rem(place, nx)
    quad = x * 2 + c
    x_place = z * nx + (1 - x)
    x_peer, x_diag = (y, x_place, c), (y, x_place, 1 - c)
    sibling = (y, place, 1 - c)
    y_peer = (1 - y, place, c)
    z_up, z_down = (y, place + nx, c), (y, place - nx, c)
    has_up, has_down = z < nz - 1, z > 0
    last_place = nx * nz - 1
    shard = w_qkv.shape[0]
    hs = shard // 2
    width = tokens_h.shape[1]
    rows = tokens_h.shape[0]
    head = 64
    part = width // 4
    half = width // 2

    barrier = pltpu.get_barrier_semaphore()

    def greet(device):
        pl.semaphore_signal(barrier, inc=1, device_id=device, device_id_type=MESH)

    def when(cond, run):
        if cond is None:
            run()
        else:
            pl.when(cond)(run)

    for device in (x_peer, x_diag, sibling, y_peer):
        greet(device)
    leap = nz - 1
    aims = [(has_down, z - 1), (z >= leap, z - leap), (has_up, z + 1)]
    for cond, zz in ((has_up, z + 1), (has_down, z - 1), (z < nz - leap, z + leap)):
        def both(zz=zz):
            greet((y, zz * nx, c))
            greet((y, zz * nx + 1, c))

        when(cond, both)
    for cond, shift in ((has_up, nx), (has_down, -nx)):
        when(cond, lambda shift=shift: greet((y, place + shift, 1 - c)))

    loads = [
        pltpu.make_async_copy(source, target, load.at[k])
        for k, (source, target) in enumerate(
            (
                (w_qkv_h.at[pl.ds(y * hs, hs), :], w_qkv.at[pl.ds(y * hs, hs), :]),
                (tokens_h, tok.at[x, pl.ds(c * rows, rows), :]),
                (gain_attn_h, gain_attn),
                (w_conv_h.at[:, :, pl.ds(c * half, half)], w_conv),
                (key_bias_h, bias.at[x, c]),
                (w_out_h, wo.at[pl.ds(place * shard, shard), :]),
                (gain_conv_h, gain_conv),
                (lat_taps_h, lat_taps),
                (lon_half_h, lon_half),
                (lat_half_h, lat_half),
                (quad_off_h, quad_off),
                (w_qkv_h.at[pl.ds((1 - y) * hs, hs), :], w_qkv.at[pl.ds((1 - y) * hs, hs), :]),
            )
        )
    ]
    loads[0].start()
    loads[1].start()
    loads[11].start()
    for copy in loads[2:11]:
        copy.start()

    def columns(pick, h):
        return jnp.concatenate(
            [
                w_qkv[pl.ds(h * hs, hs), j * width + pick * part : j * width + (pick + 1) * part]
                for j in range(3)
            ],
            axis=1,
        )

    def spread(h):
        for pick in range(4):
            @pl.when(quad == pick)
            def _(pick=pick):
                ws[pl.ds(h * hs, hs), :] = columns((pick + 2) % 4, h)
                wq[pl.ds(place * shard + h * hs, hs), :] = columns(pick, h)

    loads[0].wait()
    spread(y)
    pl.semaphore_wait(
        barrier,
        4 + 3 * has_up.astype(jnp.int32) + 3 * has_down.astype(jnp.int32) + 2 * (z >= leap).astype(jnp.int32),
    )

    def remote(source, target, send, recv, device):
        return pltpu.make_async_remote_copy(
            src_ref=source, dst_ref=target, send_sem=send, recv_sem=recv,
            device_id=device, device_id_type=MESH,
        )

    start = lambda d: d.start()
    finish = lambda d: d.wait_send()

    def q_at(slot, h):
        return wq.at[pl.ds(slot * shard + h * hs, hs), :]

    def o_at(slot, h, cc):
        return wo.at[pl.ds(slot * shard + h * hs, hs), pl.ds(cc * half, half)]

    def q_cross(k):
        h = y if k == 0 else 1 - y
        return remote(ws.at[pl.ds(h * hs, hs), :], q_at(place, h), xq_send.at[k], xq_recv.at[k], x_peer)

    def q_crossed(k):
        h = y if k == 0 else 1 - y
        return remote(ws.at[pl.ds(h * hs, hs), :], q_at(x_place, h), xq_send.at[k], xq_recv.at[k], x_peer)

    def q_direct(zz, other):
        xx = (1 - x) if other else x
        source = ws.at[pl.ds(y * hs, hs), :] if other else q_at(place, y)
        return remote(
            source, q_at(place, y), dq_send.at[zz * nx + xx], zq_recv.at[place],
            (y, zz * nx + xx, c),
        )

    def q_along(slot, device):
        return remote(q_at(slot, y), q_at(slot, y), zq_send.at[slot], zq_recv.at[slot], device)

    def q_over(slot, h):
        return remote(q_at(slot, h), q_at(slot, h), yq_send.at[slot], yq_recv.at[slot], y_peer)

    def o_cross(slot, k):
        h = y if k == 0 else 1 - y
        return remote(o_at(slot, h, c), o_at(slot, h, c), xo_send.at[k], xo_recv.at[k], x_peer)

    def o_direct(zz, other):
        xx = (1 - x) if other else x
        return remote(
            o_at(place, y, c), o_at(place, y, c), do_send.at[zz * nx + xx], zo_recv.at[place],
            (y, zz * nx + xx, c),
        )

    def o_along(slot, device):
        return remote(o_at(slot, y, c), o_at(slot, y, c), zo_send.at[slot], zo_recv.at[slot], device)

    def o_over(slot, h):
        return remote(o_at(slot, h, c), o_at(slot, h, c), yo_send.at[slot], yo_recv.at[slot], y_peer)

    def o_side(slot, h, cc):
        return remote(
            o_at(slot, h, cc), o_at(slot, h, cc), so_send.at[slot, h], so_recv.at[slot, h], sibling
        )

    def deal(direct, act):
        for cond, zz in aims:
            def both(zz=zz):
                act(direct(zz, True))
                act(direct(zz, False))

            when(cond, both)

    far = []
    for t in range(1, nz):
        for sign, reach, going, device in (
            (-1, z >= t, has_up, z_up),
            (1, z + t <= nz - 1, has_down if 1 <= t < leap - 1 else None, z_down),
        ):
            for xx in (x, 1 - x):
                far.append(
                    (
                        t, reach, (z + sign * t) * nx + xx,
                        None if going is None else jnp.logical_and(reach, going), device,
                    )
                )

    def q_step(t, act):
        for tt, reach, slot, going, device in far:
            if tt == t:
                if act is start:
                    when(reach, lambda slot=slot: q_along(slot, z_up).wait_recv())
                if going is not None:
                    when(going, lambda slot=slot, device=device: act(q_along(slot, device)))
                when(reach, lambda slot=slot: act(q_over(slot, y)))

    def o_step(t, act):
        for tt, reach, slot, going, device in far:
            if tt == t:
                if act is start:
                    when(reach, lambda slot=slot: o_along(slot, z_up).wait_recv())
                if going is not None:
                    when(going, lambda slot=slot, device=device: act(o_along(slot, device)))
                when(reach, lambda slot=slot: act(o_over(slot, y)))
                when(reach, lambda slot=slot: act(o_side(slot, y, c)))

    def o_gather(act):
        for _, reach, slot, _, _ in far:
            if act is start:
                when(reach, lambda slot=slot: o_over(slot, 1 - y).wait_recv())
            when(reach, lambda slot=slot: act(o_side(slot, 1 - y, c)))

    def o_near(act):
        for k, h in ((0, y), (1, 1 - y)):
            if act is start:
                o_cross(x_place, k).wait_recv()
            act(o_side(x_place, h, c))

    def tok_at(b, cc):
        return tok.at[b, pl.ds(cc * rows, rows), :]

    tok_copies = [
        remote(tok_at(x, c), tok_at(x, c), t_send.at[0], t_recv.at[0], x_peer),
        remote(tok_at(x, c), tok_at(x, c), t_send.at[1], t_recv.at[1], sibling),
        remote(tok_at(1 - x, c), tok_at(1 - x, c), t_send.at[2], t_recv.at[2], sibling),
    ]
    bias_copies = [
        remote(bias.at[x, c], bias.at[x, c], b_send.at[k], b_recv.at[k], device)
        for k, device in enumerate((x_peer, sibling, x_diag))
    ]

    deal(q_direct, start)
    loads[1].wait()
    tok_copies[1].start()
    tok_copies[0].start()
    loads[11].wait()
    spread(1 - y)
    q_cross(0).start()
    q_cross(1).start()
    loads[4].wait()
    for copy in bias_copies:
        copy.start()
    loads[2].wait()
    gain_a = gain_attn[...][None]

    def norm_block(b, cc):
        normed[b, pl.ds(cc * rows, rows), :] = norm_rows(tok[b, pl.ds(cc * rows, rows), :], gain_a)

    norm_block(x, c)
    tok_copies[1].wait_recv()
    norm_block(x, 1 - c)
    q_step(1, start)
    tok_copies[0].wait_recv()
    tok_copies[2].start()
    loads[5].wait()
    deal(o_direct, start)
    o_cross(place, 0).start()
    o_cross(place, 1).start()
    norm_block(1 - x, c)
    q_step(2, start)
    tok_copies[2].wait_recv()
    norm_block(1 - x, 1 - c)
    q_step(3, start)
    o_near(start)

    loads[3].wait()
    pair_row = lax.broadcasted_iota(jnp.int32, (2 * head, half), 0)
    pair_col = lax.broadcasted_iota(jnp.int32, (2 * head, half), 1)
    same = lax.rem(lax.div(pair_col, head), 2) == lax.div(pair_row, head)
    for b in range(2):
        wide = jnp.concatenate([w_conv[b], w_conv[b]], axis=0).astype(F32)
        mixer[b] = jnp.where(same, wide, 0.0).astype(BF)
    for copy in bias_copies:
        copy.wait_recv()
    for b in range(2):
        bias_f[b] = jnp.concatenate([bias[b, 0], bias[b, 1]], axis=1).astype(F32)
    for k in range(6, 11):
        loads[k].wait()

    o_step(1, start)
    q_crossed(0).wait_recv()
    q_crossed(1).wait_recv()
    for _, reach, slot, _, _ in far:
        when(reach, lambda slot=slot: q_over(slot, 1 - y).wait_recv())

    def att_copies(b, n):
        return [
            remote(
                att_out.at[b, pl.ds(cc * rows, rows), :], att_in.at[b, quad],
                a_send.at[n, k], a_recv.at[b, quad], device,
            )
            for k, (cc, device) in enumerate(((c, x_peer), (1 - c, x_diag), (1 - c, sibling)))
        ]

    def attend(b, between):
        projected = jnp.dot(normed[b], wq[...], preferred_element_type=F32).astype(BF)
        between()
        pieces = []
        for h in range(3):
            queries = projected[:, h * head : (h + 1) * head] * jnp.asarray(head ** -0.5, BF)
            keys = projected[:, part + h * head : part + (h + 1) * head]
            vals = projected[:, 2 * part + h * head : 2 * part + (h + 1) * head]
            scores = lax.dot_general(
                queries, keys, (((1,), (1,)), ((), ())), preferred_element_type=F32
            ) + bias_f[b, pl.ds(quad * 3 + h, 1), :]
            expd = jnp.exp(scores - jnp.max(scores, axis=-1, keepdims=True))
            totals = jnp.sum(expd, axis=-1, keepdims=True)
            pieces.append(jnp.dot(expd.astype(BF), vals, preferred_element_type=F32) / totals)
        att_out[b] = jnp.concatenate(pieces, axis=1).astype(BF)

    attend(x, lambda: None)
    for copy in att_copies(x, 0):
        copy.start()
    att_in[x, quad] = att_out[x, pl.ds(c * rows, rows), :]
    o_step(2, start)
    attend(1 - x, lambda: None)
    for copy in att_copies(1 - x, 1):
        copy.start()
    att_in[1 - x, quad] = att_out[1 - x, pl.ds(c * rows, rows), :]
    o_step(3, start)
    o_gather(start)

    span = (lon_half[0] + 1).astype(F32)
    limit = lon_half[0].astype(F32)
    lons = 2 * rows
    diff = lax.broadcasted_iota(jnp.int32, (lons, lons), 1) - lax.broadcasted_iota(
        jnp.int32, (lons, lons), 0
    )
    offset = jnp.where(diff >= rows, diff - lons, jnp.where(diff < -rows, diff + lons, diff))
    offset = offset.astype(F32)
    distance = jnp.abs(offset)
    tent = jnp.where(distance <= limit, (1.0 - distance / span) / span, 0.0)
    coeff[:, :lons] = tent.astype(BF)
    coeff[:, lons:] = (tent * offset / span).astype(BF)

    for _, reach, slot, _, _ in far:
        def landed(slot=slot):
            o_side(slot, 0, 1 - c).wait_recv()
            o_side(slot, 1, 1 - c).wait_recv()

        when(reach, landed)
    o_side(x_place, 0, 1 - c).wait_recv()
    o_side(x_place, 1, 1 - c).wait_recv()

    near, away = 2 * (1 - x), 2 * x
    passes = jnp.logical_or(jnp.logical_and(x == 0, has_up), jnp.logical_and(x == 1, has_down))
    gets = jnp.logical_or(jnp.logical_and(x == 0, has_down), jnp.logical_and(x == 1, has_up))
    onward = place + nx * (1 - 2 * x)

    def band(b):
        for source in (x * 2 + 1 - c, (1 - x) * 2 + c, (1 - x) * 2 + 1 - c):
            remote(att_in.at[b, source], att_in.at[b, source], a_send.at[0, 0], a_recv.at[b, source], sibling).wait_recv()
        branch = tok[b, pl.ds(c * rows, rows), :].astype(F32)
        for p in range(4):
            branch = branch + jnp.dot(
                att_in[b, p], wo[p * part : (p + 1) * part, :], preferred_element_type=F32
            )
        return branch.astype(BF)

    gain_c = gain_conv[...][None]
    own_rows = pl.ds(c * rows, rows)
    side_rows = pl.ds((1 - c) * rows, rows)
    own_cols = pl.ds(c * half, half)
    side_cols = pl.ds((1 - c) * half, half)

    def conv_copy(source, which, cc, k, device):
        return remote(
            source, normed_conv.at[which, pl.ds(cc * rows, rows), :],
            c_send.at[k], c_recv.at[which, cc], device,
        )

    stage[0] = norm_rows(band(1 - x), gain_c)
    to_far = [
        conv_copy(stage.at[0, :, own_cols], away, c, 0, (y, onward, c)),
        conv_copy(stage.at[0, :, side_cols], away, c, 1, (y, onward, 1 - c)),
    ]

    @pl.when(passes)
    def _():
        for d in to_far:
            d.start()

    to_side = [conv_copy(stage.at[0, :, side_cols], near, c, 2, sibling)]
    to_side[0].start()
    normed_conv[near, own_rows, :] = stage[0, :, own_cols]

    mid = band(x)
    middle[...] = mid
    stage[1] = norm_rows(mid, gain_c)
    to_side.append(conv_copy(stage.at[1, :, side_cols], 1, c, 3, sibling))
    to_side[1].start()
    to_mid = remote(middle.at[:, side_cols], mid_rows.at[own_rows, :], h_send.at[0], h_recv.at[0], sibling)
    to_mid.start()
    normed_conv[1, own_rows, :] = stage[1, :, own_cols]
    mid_rows[own_rows, :] = middle[:, own_cols]

    @pl.when(jnp.logical_not(gets))
    def _():
        normed_conv[away] = jnp.zeros((lons, half), BF)

    base = quad_off[0]
    wide_ok = lat_half[0] >= 1
    taps = [
        [
            lat_taps[b, base + r] if r == 1 else jnp.where(wide_ok, lat_taps[b, base + r], 0.0)
            for b in range(2)
        ]
        for r in range(3)
    ]

    def mix(values, b):
        return jnp.concatenate(
            [
                lax.dot_general(
                    values[:, p * 2 * head : (p + 1) * 2 * head],
                    mixer[b, :, p * 2 * head : (p + 1) * 2 * head],
                    (((1,), (1,)), ((), ())),
                    preferred_element_type=F32,
                )
                for p in range(half // (2 * head))
            ],
            axis=1,
        ).astype(BF)

    conv_copy(stage.at[1, :, side_cols], 1, 1 - c, 3, sibling).wait_recv()
    for b in range(2):
        gain = jnp.where(place == 0, taps[0][b], 0.0) + jnp.where(place == last_place, taps[2][b], 0.0)
        pole = mix((gain * normed_conv[1].astype(F32)).astype(BF), b)
        polar[b, :rows] = pole[rows:]
        polar[b, rows:] = pole[:rows]
    conv_copy(stage.at[0, :, side_cols], near, 1 - c, 2, sibling).wait_recv()
    remote(middle.at[:, side_cols], mid_rows.at[side_rows, :], h_send.at[0], h_recv.at[0], sibling).wait_recv()

    @pl.when(gets)
    def _():
        conv_copy(stage.at[0, :, own_cols], away, 0, 0, sibling).wait_recv()
        conv_copy(stage.at[0, :, own_cols], away, 1, 0, sibling).wait_recv()

    for b in range(2):
        summed = (
            taps[0][b] * normed_conv[0].astype(F32)
            + taps[1][b] * normed_conv[1].astype(F32)
            + taps[2][b] * normed_conv[2].astype(F32)
        ).astype(BF)
        mixed[b * lons : (b + 1) * lons, :] = (
            mix(summed, b).astype(F32) + polar[b].astype(F32)
        ).astype(BF)

    def convolve(at):
        return (
            mid_rows[at, :].astype(F32)
            + jnp.dot(coeff[at, :], mixed[...], preferred_element_type=F32)
        ).astype(BF)

    done_out[...] = convolve(side_rows)
    to_done = remote(done_out, done_in, h_send.at[1], h_recv.at[1], sibling)
    to_done.start()
    out[:, own_cols] = convolve(own_rows)

    q_cross(0).wait_send()
    q_cross(1).wait_send()
    o_cross(place, 0).wait_send()
    o_cross(place, 1).wait_send()
    deal(q_direct, finish)
    deal(o_direct, finish)
    o_near(finish)
    for t in range(1, nz):
        q_step(t, finish)
        o_step(t, finish)
    o_gather(finish)
    for d in tok_copies + bias_copies + att_copies(x, 0) + att_copies(1 - x, 1) + to_side + [to_mid]:
        d.wait_send()

    @pl.when(passes)
    def _():
        for d in to_far:
            d.wait_send()

    to_done.wait_recv()
    out[:, side_cols] = done_in[...]
    to_done.wait_send()


def in_hbm(value):
    return pltpu.with_memory_space_constraint(value, pltpu.HBM)


def fused_device(
    tokens, gain_attn, w_qkv, key_bias, w_out, gain_conv, w_conv, lat_taps, lon_half, lat_half, quad_off
):
    rows, width = tokens.shape[1:]
    shard = w_qkv.shape[0]
    heads = key_bias.shape[1]
    lat_count = width // shard
    nx = 2
    nz = lat_count // nx
    part, half, lons = width // 4, width // 2, 2 * rows
    vmem = pl.BlockSpec(memory_space=pltpu.VMEM)
    anywhere = pl.BlockSpec(memory_space=pltpu.HBM)
    dma = pltpu.SemaphoreType.DMA
    out = pl.pallas_call(
        lambda *refs: fused_kernel(nx, nz, *refs),
        out_shape=pltpu.VMEM((rows, width), BF),
        in_specs=[anywhere] * 11,
        out_specs=vmem,
        scratch_shapes=[
            pltpu.SMEM((2, lat_taps.shape[0]), F32),
            pltpu.SMEM((1,), jnp.int32),
            pltpu.SMEM((1,), jnp.int32),
            pltpu.SMEM((1,), jnp.int32),
            pltpu.VMEM((width,), F32),
            pltpu.VMEM(w_qkv.shape, BF),
            pltpu.VMEM((width,), F32),
            pltpu.VMEM((2, 64, half), BF),
            dma((12,)),
            pltpu.VMEM((shard, 3 * part), BF),
            pltpu.VMEM((width, 3 * part), BF),
            pltpu.VMEM((width, width), BF),
            pltpu.VMEM((2, lons, width), BF),
            pltpu.VMEM((2, lons, width), BF),
            pltpu.VMEM((2, 2, heads, rows), BF),
            pltpu.VMEM((2, heads, lons), F32),
            pltpu.VMEM((2, lons, part), BF),
            pltpu.VMEM((2, 4, rows, part), BF),
            pltpu.VMEM((2, rows, width), BF),
            pltpu.VMEM((3, lons, half), BF),
            pltpu.VMEM((rows, width), BF),
            pltpu.VMEM((lons, half), BF),
            pltpu.VMEM((2, 128, half), BF),
            pltpu.VMEM((2, lons, half), BF),
            pltpu.VMEM((2 * lons, half), BF),
            pltpu.VMEM((lons, 2 * lons), BF),
            pltpu.VMEM((rows, half), BF),
            pltpu.VMEM((rows, half), BF),
            dma((2,)), dma((2,)),
            dma((lat_count,)), dma((lat_count,)), dma((lat_count,)),
            dma((lat_count,)), dma((lat_count,)),
            dma((2,)), dma((2,)),
            dma((lat_count,)), dma((lat_count,)), dma((lat_count,)),
            dma((lat_count,)), dma((lat_count,)),
            dma((lat_count, 2)), dma((lat_count, 2)),
            dma((3,)), dma((3,)),
            dma((3,)), dma((3,)),
            dma((2, 3)), dma((2, 4)),
            dma((4,)), dma((3, 2)),
            dma((2,)), dma((2,)),
        ],
        compiler_params=pltpu.CompilerParams(
            collective_id=0, has_side_effects=True, vmem_limit_bytes=40 * 1024 * 1024
        ),
    )(
        in_hbm(lat_taps.T), lon_half, lat_half, quad_off,
        *[
            in_hbm(v)
            for v in (
                tokens[0], gain_attn, w_qkv, key_bias[0], w_out, gain_conv, jnp.swapaxes(w_conv, 1, 2)
            )
        ],
    )
    return out[None]


def solution(mesh):
    sizes = (mesh.shape["groups"], mesh.shape["lat"], mesh.shape["lon"])
    return jax.shard_map(
        fused_device if sizes == (2, 8, 2) else per_device,
        mesh=mesh,
        in_specs=(
            P(("groups", "lat"), "lon", None),
            P(),
            P("lat", None),
            P("lat", None, "lon"),
            P("lat", None),
            P(),
            P(),
            P(),
            P("lat"),
            P("lat"),
            P("lat"),
        ),
        out_specs=P(("groups", "lat"), "lon", None),
        check_vma=False,
    )
```

```python
import jax
import jax.numpy as jnp
from jax import lax
from jax.experimental import pallas as pl
from jax.experimental.pallas import tpu as pltpu
from jax.sharding import PartitionSpec as P


def padded(cells, sides, width):
    for axis, dim in sides:
        count = lax.axis_size(axis)
        ends = count - 1
        head = lax.slice_in_dim(cells, 0, width, axis=dim)
        tail = lax.slice_in_dim(cells, cells.shape[dim] - width, cells.shape[dim], axis=dim)
        cells = jnp.concatenate(
            [
                lax.ppermute(tail, axis, [(i, (i + 1) % count) for i in range(ends)]),
                cells,
                lax.ppermute(head, axis, [((i + 1) % count, i) for i in range(ends)]),
            ],
            axis=dim,
        )
    return cells


def layer_norm(inputs, gain):
    values = inputs.astype(jnp.float32)
    average = jnp.mean(values, axis=-1, keepdims=True)
    centered = values - average
    variance = jnp.mean(centered * centered, axis=-1, keepdims=True)
    return centered * lax.rsqrt(variance + 1e-05) * gain


def group_mix(inputs, w_conv):
    basis, length, channels = inputs.shape
    group_width = w_conv.shape[2]
    groups = channels // group_width
    mixed_rows = jnp.einsum(
        "kjgc,kgce->kjge",
        inputs.reshape(basis, length, groups, group_width),
        w_conv.reshape(basis, groups, group_width, group_width),
        preferred_element_type=jnp.float32,
    )
    return mixed_rows.reshape(basis, length, channels).astype(jnp.bfloat16)


def lon_weights(row_ids, col_ids, half_width, lon_total):
    offset_lon = (
        jnp.mod(col_ids[None, :] - row_ids[:, None] + lon_total // 2, lon_total) - lon_total // 2
    )
    distance = jnp.abs(offset_lon).astype(jnp.float32)
    span_plus = (half_width + 1).astype(jnp.float32)
    tent_weight = jnp.where(
        distance <= half_width.astype(jnp.float32), (1.0 - distance / span_plus) / span_plus, 0.0
    )
    odd_weight = tent_weight * offset_lon.astype(jnp.float32) / span_plus
    return jnp.stack([tent_weight, odd_weight]).astype(jnp.bfloat16)


def start_state(query_count, head_count, head_dim):
    running_max = jnp.full((head_count, query_count), -jnp.inf, jnp.float32)
    running_sum = jnp.zeros((head_count, query_count), jnp.float32)
    running_out = jnp.zeros((query_count, head_count, head_dim), jnp.float32)
    return (running_max, running_sum, running_out)


def attend_keys(carry_state, queries, key_rows, value_rows, bias_rows, score_scale):
    key_count = key_rows.shape[0]
    for offset in range(0, key_count, 128):
        running_max, running_sum, running_out = carry_state
        key_block = key_rows[offset : offset + 128]
        value_block = value_rows[offset : offset + 128]
        bias_block = bias_rows[offset : offset + 128]
        scores = (
            jnp.einsum("qhd,khd->hqk", queries, key_block, preferred_element_type=jnp.float32)
            * score_scale
        )
        scores = scores + bias_block.T.astype(jnp.float32)[:, None, :]
        new_max = jnp.maximum(running_max, jnp.max(scores, axis=-1))
        rescale = jnp.exp(running_max - new_max)
        exp_scores = jnp.exp(scores - new_max[:, :, None])
        running_sum = running_sum * rescale + jnp.sum(exp_scores, axis=-1)
        running_out = running_out * rescale.T[:, :, None] + jnp.einsum(
            "hqk,khd->qhd",
            exp_scores.astype(jnp.bfloat16),
            value_block,
            preferred_element_type=jnp.float32,
        )
        carry_state = (new_max, running_sum, running_out)
    return carry_state


def finish_state(carry_state):
    running_max, running_sum, running_out = carry_state
    finished = running_out / running_sum.T[:, :, None]
    return finished.reshape(finished.shape[0], -1).astype(jnp.bfloat16)


def lon_conv(blended, half_width, first_col, out_cols):
    lon_total = blended.shape[1]
    block_cols = min(128, lon_total)
    block_count = lon_total // block_cols
    first_block = jnp.floor_divide(first_col - half_width, block_cols)
    last_block = jnp.floor_divide(first_col + out_cols - 1 + half_width, block_cols)
    turn_count = jnp.minimum(block_count, last_block - first_block + 1)
    row_ids = first_col + jnp.arange(out_cols, dtype=jnp.int32)

    def add_block(turn_index, running_out):
        block_at = jnp.mod(first_block + turn_index, block_count)
        lon_block = lax.dynamic_slice_in_dim(blended, block_at * block_cols, block_cols, 1)
        col_ids = block_at * block_cols + jnp.arange(block_cols, dtype=jnp.int32)
        coeffs = lon_weights(row_ids, col_ids, half_width, lon_total)
        return running_out + jnp.einsum(
            "kjc,kcd->jd", coeffs, lon_block, preferred_element_type=jnp.float32
        )

    initial = jnp.zeros((out_cols, blended.shape[2]), jnp.float32)
    return lax.fori_loop(0, turn_count, add_block, initial)


def per_device(
    tokens,
    gain_attn,
    w_qkv,
    key_bias,
    w_out,
    gain_conv,
    w_conv,
    lat_taps,
    lon_half,
    lat_half,
    quad_off,
):
    own_tokens = tokens[0]
    count_lon, model_width = own_tokens.shape
    head_count = key_bias.shape[1]
    head_dim = model_width // head_count
    score_scale = head_dim ** (-0.5)
    lon_place = lax.axis_index("lon")
    normed = layer_norm(own_tokens, gain_attn).astype(jnp.bfloat16)
    bias_rows = key_bias[0].T
    full_qkv, full_out = (
        lax.all_gather(w_qkv, "lat", axis=0, tiled=True),
        lax.all_gather(w_out, "lat", axis=0, tiled=True),
    )
    projected = jnp.dot(normed, full_qkv, preferred_element_type=jnp.float32).astype(jnp.bfloat16)
    queries = projected[:, :model_width].reshape(count_lon, head_count, head_dim)
    key_here = projected[:, model_width : 2 * model_width]
    value_here = projected[:, 2 * model_width :]
    key_piece = lax.all_gather(key_here, "lon", axis=0, tiled=True)
    value_piece = lax.all_gather(value_here, "lon", axis=0, tiled=True)
    bias_piece = lax.all_gather(bias_rows, "lon", axis=0, tiled=True)
    length = key_piece.shape[0]
    carry_state = attend_keys(
        start_state(count_lon, head_count, head_dim),
        queries,
        key_piece.reshape(length, head_count, head_dim),
        value_piece.reshape(length, head_count, head_dim),
        bias_piece,
        score_scale,
    )
    attended = finish_state(carry_state)
    branch_out = jnp.dot(attended, full_out, preferred_element_type=jnp.float32)
    middle = (own_tokens.astype(jnp.float32) + branch_out).astype(jnp.bfloat16)
    conv_in = layer_norm(middle, gain_conv).astype(jnp.bfloat16)
    stacked = padded(conv_in[None], (("lat", 0),), 1)
    lat_row = lax.axis_index("lat")
    last_band = lax.axis_size("lat") - 1
    offsets = jnp.arange(3, dtype=jnp.int32) - 1
    one_hot = (
        (quad_off[0] + offsets + 1)[:, None]
        == jnp.arange(lat_taps.shape[0], dtype=jnp.int32)[None, :]
    ).astype(jnp.float32)
    tap_vals = jnp.dot(one_hot, lat_taps, precision=lax.Precision.HIGHEST)
    tap_vals = jnp.where((jnp.abs(offsets) <= lat_half[0])[:, None], tap_vals, 0.0)
    summed = jnp.einsum(
        "rk,rjd->kjd", tap_vals, stacked.astype(jnp.float32), precision=lax.Precision.HIGHEST
    ).astype(jnp.bfloat16)
    pole_gain = jnp.where(lat_row == 0, tap_vals[0], 0.0) + jnp.where(
        lat_row == last_band, tap_vals[2], 0.0
    )
    first_col = lon_place * count_lon
    pole_rows = (pole_gain[:, None, None] * conv_in.astype(jnp.float32)[None]).astype(jnp.bfloat16)
    mixed_rows = group_mix(summed, w_conv)
    pole_mixed = group_mix(pole_rows, w_conv)
    circle_rows, pole_all = (
        lax.all_gather(mixed_rows, "lon", axis=1, tiled=True),
        lax.all_gather(pole_mixed, "lon", axis=1, tiled=True),
    )
    lon_total = circle_rows.shape[1]
    blended = (
        circle_rows.astype(jnp.float32)
        + jnp.roll(pole_all, -(lon_total // 2), axis=1).astype(jnp.float32)
    ).astype(jnp.bfloat16)
    conv_out = lon_conv(blended, lon_half[0], first_col, count_lon)
    return (middle.astype(jnp.float32) + conv_out).astype(jnp.bfloat16)[None]


BF = jnp.bfloat16
F32 = jnp.float32
MESH = pl.DeviceIdType.MESH


def norm_rows(values, gain):
    values = values.astype(F32)
    average = jnp.mean(values, axis=-1, keepdims=True)
    centered = values - average
    variance = jnp.mean(centered * centered, axis=-1, keepdims=True)
    return (centered * lax.rsqrt(variance + 1e-05) * gain).astype(BF)


def fused_kernel(
    nx, nz,
    lat_taps_h, lon_half_h, lat_half_h, quad_off_h,
    tokens_h, gain_attn_h, w_qkv_h, key_bias_h, w_out_h, gain_conv_h, w_conv_h,
    out,
    lat_taps, lon_half, lat_half, quad_off, gain_attn, w_qkv, gain_conv, w_conv, load,
    ws, wq, wo, tok, normed, bias, bias_f, att_out, att_in, stage, normed_conv, middle, mid_rows,
    mixer, polar, mixed, coeff, done_out, done_in,
    xq_send, xq_recv, dq_send, zq_send, zq_recv, yq_send, yq_recv,
    xo_send, xo_recv, do_send, zo_send, zo_recv, yo_send, yo_recv, so_send, so_recv,
    t_send, t_recv, b_send, b_recv, a_send, a_recv,
    f_send, f_recv, c_send, c_recv, h_send, h_recv,
):
    y, place, c = lax.axis_index("groups"), lax.axis_index("lat"), lax.axis_index("lon")
    z, x = lax.div(place, nx), lax.rem(place, nx)
    quad = x * 2 + c
    x_place = z * nx + (1 - x)
    x_peer, x_diag = (y, x_place, c), (y, x_place, 1 - c)
    sibling = (y, place, 1 - c)
    y_peer = (1 - y, place, c)
    z_up, z_down = (y, place + nx, c), (y, place - nx, c)
    has_up, has_down = z < nz - 1, z > 0
    last_place = nx * nz - 1
    shard = w_qkv.shape[0]
    hs = shard // 2
    width = tokens_h.shape[1]
    rows = tokens_h.shape[0]
    head = 64
    part = width // 4
    half = width // 2

    barrier = pltpu.get_barrier_semaphore()

    def greet(device):
        pl.semaphore_signal(barrier, inc=1, device_id=device, device_id_type=MESH)

    def when(cond, run):
        if cond is None:
            run()
        else:
            pl.when(cond)(run)

    for device in (x_peer, x_diag, sibling, y_peer):
        greet(device)
    leap = nz - 1
    aims = [(has_down, z - 1), (z >= leap, z - leap), (has_up, z + 1)]
    for cond, zz in ((has_up, z + 1), (has_down, z - 1), (z < nz - leap, z + leap)):
        def both(zz=zz):
            greet((y, zz * nx, c))
            greet((y, zz * nx + 1, c))

        when(cond, both)
    for cond, zz in ((has_up, z + 1), (has_down, z - 1)):
        def others(zz=zz):
            greet((y, zz * nx, 1 - c))
            greet((y, zz * nx + 1, 1 - c))

        when(cond, others)

    loads = [
        pltpu.make_async_copy(source, target, load.at[k])
        for k, (source, target) in enumerate(
            (
                (w_qkv_h.at[pl.ds(y * hs, hs), :], w_qkv.at[pl.ds(y * hs, hs), :]),
                (tokens_h, tok.at[x, pl.ds(c * rows, rows), :]),
                (gain_attn_h, gain_attn),
                (w_conv_h.at[:, :, pl.ds(c * half, half)], w_conv),
                (key_bias_h, bias.at[x, c]),
                (w_out_h, wo.at[pl.ds(place * shard, shard), :]),
                (gain_conv_h, gain_conv),
                (lat_taps_h, lat_taps),
                (lon_half_h, lon_half),
                (lat_half_h, lat_half),
                (quad_off_h, quad_off),
                (w_qkv_h.at[pl.ds((1 - y) * hs, hs), :], w_qkv.at[pl.ds((1 - y) * hs, hs), :]),
            )
        )
    ]
    loads[0].start()
    loads[1].start()
    loads[11].start()
    for copy in loads[2:11]:
        copy.start()

    def columns(pick, h):
        return jnp.concatenate(
            [
                w_qkv[pl.ds(h * hs, hs), j * width + pick * part : j * width + (pick + 1) * part]
                for j in range(3)
            ],
            axis=1,
        )

    def spread(h):
        for pick in range(4):
            @pl.when(quad == pick)
            def _(pick=pick):
                ws[pl.ds(h * hs, hs), :] = columns((pick + 2) % 4, h)
                wq[pl.ds(place * shard + h * hs, hs), :] = columns(pick, h)

    loads[0].wait()
    spread(y)
    pl.semaphore_wait(
        barrier,
        4 + 4 * has_up.astype(jnp.int32) + 4 * has_down.astype(jnp.int32) + 2 * (z >= leap).astype(jnp.int32),
    )

    def remote(source, target, send, recv, device):
        return pltpu.make_async_remote_copy(
            src_ref=source, dst_ref=target, send_sem=send, recv_sem=recv,
            device_id=device, device_id_type=MESH,
        )

    start = lambda d: d.start()
    finish = lambda d: d.wait_send()

    def q_at(slot, h):
        return wq.at[pl.ds(slot * shard + h * hs, hs), :]

    def o_at(slot, h, cc):
        return wo.at[pl.ds(slot * shard + h * hs, hs), pl.ds(cc * half, half)]

    def q_cross(k):
        h = y if k == 0 else 1 - y
        return remote(ws.at[pl.ds(h * hs, hs), :], q_at(place, h), xq_send.at[k], xq_recv.at[k], x_peer)

    def q_crossed(k):
        h = y if k == 0 else 1 - y
        return remote(ws.at[pl.ds(h * hs, hs), :], q_at(x_place, h), xq_send.at[k], xq_recv.at[k], x_peer)

    def q_direct(zz, other):
        xx = (1 - x) if other else x
        source = ws.at[pl.ds(y * hs, hs), :] if other else q_at(place, y)
        return remote(
            source, q_at(place, y), dq_send.at[zz * nx + xx], zq_recv.at[place],
            (y, zz * nx + xx, c),
        )

    def q_along(slot, device):
        return remote(q_at(slot, y), q_at(slot, y), zq_send.at[slot], zq_recv.at[slot], device)

    def q_over(slot, h):
        return remote(q_at(slot, h), q_at(slot, h), yq_send.at[slot], yq_recv.at[slot], y_peer)

    def o_cross(slot, k):
        h = y if k == 0 else 1 - y
        return remote(o_at(slot, h, c), o_at(slot, h, c), xo_send.at[k], xo_recv.at[k], x_peer)

    def o_direct(zz, other):
        xx = (1 - x) if other else x
        return remote(
            o_at(place, y, c), o_at(place, y, c), do_send.at[zz * nx + xx], zo_recv.at[place],
            (y, zz * nx + xx, c),
        )

    def o_along(slot, device):
        return remote(o_at(slot, y, c), o_at(slot, y, c), zo_send.at[slot], zo_recv.at[slot], device)

    def o_over(slot, h):
        return remote(o_at(slot, h, c), o_at(slot, h, c), yo_send.at[slot], yo_recv.at[slot], y_peer)

    def o_side(slot, h, cc):
        return remote(
            o_at(slot, h, cc), o_at(slot, h, cc), so_send.at[slot, h], so_recv.at[slot, h], sibling
        )

    def deal(direct, act):
        for cond, zz in aims:
            def both(zz=zz):
                act(direct(zz, True))
                act(direct(zz, False))

            when(cond, both)

    far = []
    for t in range(1, nz):
        for sign, reach, going, device in (
            (-1, z >= t, has_up, z_up),
            (1, z + t <= nz - 1, has_down if 1 <= t < leap - 1 else None, z_down),
        ):
            for xx in (x, 1 - x):
                far.append(
                    (
                        t * sign, reach, (z + sign * t) * nx + xx,
                        None if going is None else jnp.logical_and(reach, going), device,
                    )
                )

    def q_step(t, act):
        for tt, reach, slot, going, device in far:
            if tt == t:
                if act is start:
                    when(reach, lambda slot=slot: q_along(slot, z_up).wait_recv())
                if going is not None:
                    when(going, lambda slot=slot, device=device: act(q_along(slot, device)))
                when(reach, lambda slot=slot: act(q_over(slot, y)))

    def o_step(t, act):
        for tt, reach, slot, going, device in far:
            if tt == t:
                if act is start:
                    when(reach, lambda slot=slot: o_along(slot, z_up).wait_recv())
                if going is not None:
                    when(going, lambda slot=slot, device=device: act(o_along(slot, device)))
                when(reach, lambda slot=slot: act(o_over(slot, y)))
                when(reach, lambda slot=slot: act(o_side(slot, y, c)))

    def o_gather(act, ts=range(1, nz)):
        for t, reach, slot, _, _ in far:
            if abs(t) not in ts:
                continue
            if act is start:
                when(reach, lambda slot=slot: o_over(slot, 1 - y).wait_recv())
            when(reach, lambda slot=slot: act(o_side(slot, 1 - y, c)))

    def o_near(act):
        for k, h in ((0, y), (1, 1 - y)):
            if act is start:
                o_cross(x_place, k).wait_recv()
            act(o_side(x_place, h, c))

    def tok_at(b, cc):
        return tok.at[b, pl.ds(cc * rows, rows), :]

    tok_copies = [
        remote(tok_at(x, c), tok_at(x, c), t_send.at[0], t_recv.at[0], x_peer),
        remote(tok_at(x, c), tok_at(x, c), t_send.at[1], t_recv.at[1], sibling),
        remote(tok_at(1 - x, c), tok_at(1 - x, c), t_send.at[2], t_recv.at[2], sibling),
    ]
    bias_copies = [
        remote(bias.at[x, c], bias.at[x, c], b_send.at[k], b_recv.at[k], device)
        for k, device in enumerate((x_peer, sibling, x_diag))
    ]

    deal(q_direct, start)
    loads[1].wait()
    tok_copies[1].start()
    tok_copies[0].start()
    loads[11].wait()
    spread(1 - y)
    q_cross(0).start()
    q_cross(1).start()
    loads[4].wait()
    for copy in bias_copies:
        copy.start()
    loads[2].wait()
    gain_a = gain_attn[...][None]

    def norm_block(b, cc):
        normed[b, pl.ds(cc * rows, rows), :] = norm_rows(tok[b, pl.ds(cc * rows, rows), :], gain_a)

    norm_block(x, c)
    tok_copies[1].wait_recv()
    norm_block(x, 1 - c)
    q_step(-1, start)
    q_step(1, start)
    q_step(3, start)
    loads[5].wait()
    deal(o_direct, start)
    o_cross(place, 0).start()
    o_cross(place, 1).start()
    q_step(-2, start)
    q_step(2, start)
    q_step(-3, start)
    tok_copies[0].wait_recv()
    tok_copies[2].start()
    norm_block(1 - x, c)
    tok_copies[2].wait_recv()
    norm_block(1 - x, 1 - c)
    o_near(start)

    loads[3].wait()
    pair_row = lax.broadcasted_iota(jnp.int32, (2 * head, half), 0)
    pair_col = lax.broadcasted_iota(jnp.int32, (2 * head, half), 1)
    same = lax.rem(lax.div(pair_col, head), 2) == lax.div(pair_row, head)
    for b in range(2):
        wide = jnp.concatenate([w_conv[b], w_conv[b]], axis=0).astype(F32)
        mixer[b] = jnp.where(same, wide, 0.0).astype(BF)
    for copy in bias_copies:
        copy.wait_recv()
    for b in range(2):
        bias_f[b] = jnp.concatenate([bias[b, 0], bias[b, 1]], axis=1).astype(F32)
    for k in range(6, 11):
        loads[k].wait()

    o_step(1, start)
    o_step(-1, start)
    o_step(3, start)
    span = (lon_half[0] + 1).astype(F32)
    limit = lon_half[0].astype(F32)
    lons = 2 * rows
    diff = lax.broadcasted_iota(jnp.int32, (lons, lons), 1) - lax.broadcasted_iota(
        jnp.int32, (lons, lons), 0
    )
    offset = jnp.where(diff >= rows, diff - lons, jnp.where(diff < -rows, diff + lons, diff))
    offset = offset.astype(F32)
    distance = jnp.abs(offset)
    tent = jnp.where(distance <= limit, (1.0 - distance / span) / span, 0.0)
    coeff[:, :lons] = tent.astype(BF)
    coeff[:, lons:] = (tent * offset / span).astype(BF)

    q_crossed(0).wait_recv()
    q_crossed(1).wait_recv()
    for _, reach, slot, _, _ in far:
        when(reach, lambda slot=slot: q_over(slot, 1 - y).wait_recv())

    def att_copies(b, n):
        return [
            remote(
                att_out.at[b, pl.ds(cc * rows, rows), :], att_in.at[b, quad],
                a_send.at[n, k], a_recv.at[b, quad], device,
            )
            for k, (cc, device) in enumerate(((c, x_peer), (1 - c, x_diag), (1 - c, sibling)))
        ]

    def attend(b, between):
        projected = jnp.dot(normed[b], wq[...], preferred_element_type=F32).astype(BF)
        between()
        pieces = []
        for h in range(3):
            queries = projected[:, h * head : (h + 1) * head] * jnp.asarray(head ** -0.5, BF)
            keys = projected[:, part + h * head : part + (h + 1) * head]
            vals = projected[:, 2 * part + h * head : 2 * part + (h + 1) * head]
            scores = lax.dot_general(
                queries, keys, (((1,), (1,)), ((), ())), preferred_element_type=F32
            ) + bias_f[b, pl.ds(quad * 3 + h, 1), :]
            expd = jnp.exp(scores - jnp.max(scores, axis=-1, keepdims=True))
            totals = jnp.sum(expd, axis=-1, keepdims=True)
            pieces.append(jnp.dot(expd.astype(BF), vals, preferred_element_type=F32) / totals)
        att_out[b] = jnp.concatenate(pieces, axis=1).astype(BF)

    attend(x, lambda: None)
    for copy in att_copies(x, 0):
        copy.start()
    att_in[x, quad] = att_out[x, pl.ds(c * rows, rows), :]
    o_step(-2, start)
    o_step(2, start)
    attend(1 - x, lambda: None)
    for copy in att_copies(1 - x, 1):
        copy.start()
    att_in[1 - x, quad] = att_out[1 - x, pl.ds(c * rows, rows), :]
    o_step(-3, start)
    o_gather(start)

    for _, reach, slot, _, _ in far:
        def landed(slot=slot):
            o_side(slot, 0, 1 - c).wait_recv()
            o_side(slot, 1, 1 - c).wait_recv()

        when(reach, landed)
    o_side(x_place, 0, 1 - c).wait_recv()
    o_side(x_place, 1, 1 - c).wait_recv()

    near, away = 2 * (1 - x), 2 * x
    passes = jnp.logical_or(jnp.logical_and(x == 0, has_up), jnp.logical_and(x == 1, has_down))
    gets = jnp.logical_or(jnp.logical_and(x == 0, has_down), jnp.logical_and(x == 1, has_up))
    onward = place + nx * (1 - 2 * x)
    split = rows // 2
    passes_own = jnp.logical_or(jnp.logical_and(x == 1, has_up), jnp.logical_and(x == 0, has_down))
    back = (z - 1 + 2 * x) * nx + 1 - x

    def band(b):
        for source in (x * 2 + 1 - c, (1 - x) * 2 + c, (1 - x) * 2 + 1 - c):
            remote(att_in.at[b, source], att_in.at[b, source], a_send.at[0, 0], a_recv.at[b, source], sibling).wait_recv()
        branch = tok[b, pl.ds(c * rows, rows), :].astype(F32)
        for p in range(4):
            branch = branch + jnp.dot(
                att_in[b, p], wo[p * part : (p + 1) * part, :], preferred_element_type=F32
            )
        return branch.astype(BF)

    gain_c = gain_conv[...][None]
    own_rows = pl.ds(c * rows, rows)
    side_rows = pl.ds((1 - c) * rows, rows)
    own_cols = pl.ds(c * half, half)
    side_cols = pl.ds((1 - c) * half, half)

    def conv_copy(source, which, cc, k, device):
        return remote(
            source, normed_conv.at[which, pl.ds(cc * rows, rows), :],
            c_send.at[k], c_recv.at[which, cc], device,
        )

    stage[0] = norm_rows(band(1 - x), gain_c)
    def far_copy(which, first, cc, cols, k, device):
        start_row = 0 if first else split
        target = 2 * x if first else 2 * (1 - x)
        return remote(
            stage.at[which, pl.ds(start_row, split), cols],
            normed_conv.at[target, pl.ds(cc * rows + start_row, split), :],
            f_send.at[k], f_recv.at[cc, 0 if first else 1], device,
        )

    to_far = [
        far_copy(0, True, c, own_cols, 0, (y, onward, c)),
        far_copy(0, True, c, side_cols, 1, (y, onward, 1 - c)),
    ]
    to_back = [
        far_copy(1, False, c, own_cols, 2, (y, back, c)),
        far_copy(1, False, c, side_cols, 3, (y, back, 1 - c)),
    ]

    @pl.when(passes)
    def _():
        for d in to_far:
            d.start()

    to_side = [conv_copy(stage.at[0, :, side_cols], near, c, 2, sibling)]
    to_side[0].start()
    normed_conv[near, own_rows, :] = stage[0, :, own_cols]

    mid = band(x)
    middle[...] = mid
    stage[1] = norm_rows(mid, gain_c)
    @pl.when(passes_own)
    def _():
        for d in to_back:
            d.start()

    to_side.append(conv_copy(stage.at[1, :, side_cols], 1, c, 3, sibling))
    to_side[1].start()
    to_mid = remote(middle.at[:, side_cols], mid_rows.at[own_rows, :], h_send.at[0], h_recv.at[0], sibling)
    to_mid.start()
    normed_conv[1, own_rows, :] = stage[1, :, own_cols]
    mid_rows[own_rows, :] = middle[:, own_cols]

    @pl.when(jnp.logical_not(gets))
    def _():
        normed_conv[away] = jnp.zeros((lons, half), BF)

    base = quad_off[0]
    wide_ok = lat_half[0] >= 1
    taps = [
        [
            lat_taps[b, base + r] if r == 1 else jnp.where(wide_ok, lat_taps[b, base + r], 0.0)
            for b in range(2)
        ]
        for r in range(3)
    ]

    def mix(values, b):
        return jnp.concatenate(
            [
                lax.dot_general(
                    values[:, p * 2 * head : (p + 1) * 2 * head],
                    mixer[b, :, p * 2 * head : (p + 1) * 2 * head],
                    (((1,), (1,)), ((), ())),
                    preferred_element_type=F32,
                )
                for p in range(half // (2 * head))
            ],
            axis=1,
        ).astype(BF)

    conv_copy(stage.at[1, :, side_cols], 1, 1 - c, 3, sibling).wait_recv()
    for b in range(2):
        gain = jnp.where(place == 0, taps[0][b], 0.0) + jnp.where(place == last_place, taps[2][b], 0.0)
        pole = mix((gain * normed_conv[1].astype(F32)).astype(BF), b)
        polar[b, :rows] = pole[rows:]
        polar[b, rows:] = pole[:rows]
    conv_copy(stage.at[0, :, side_cols], near, 1 - c, 2, sibling).wait_recv()
    remote(middle.at[:, side_cols], mid_rows.at[side_rows, :], h_send.at[0], h_recv.at[0], sibling).wait_recv()

    q_cross(0).wait_send()
    q_cross(1).wait_send()
    o_cross(place, 0).wait_send()
    o_cross(place, 1).wait_send()
    deal(q_direct, finish)
    deal(o_direct, finish)
    o_near(finish)
    for t in range(1, nz):
        for signed in (t, -t):
            q_step(signed, finish)
            o_step(signed, finish)
    o_gather(finish)
    for d in tok_copies + bias_copies + att_copies(x, 0) + att_copies(1 - x, 1) + to_side + [to_mid]:
        d.wait_send()

    @pl.when(gets)
    def _():
        for cc in range(2):
            for part in range(2):
                target = normed_conv.at[away, pl.ds(cc * rows + part * split, split), :]
                remote(target, target, f_send.at[0], f_recv.at[cc, part], sibling).wait_recv()

    for b in range(2):
        summed = (
            taps[0][b] * normed_conv[0].astype(F32)
            + taps[1][b] * normed_conv[1].astype(F32)
            + taps[2][b] * normed_conv[2].astype(F32)
        ).astype(BF)
        mixed[b * lons : (b + 1) * lons, :] = (
            mix(summed, b).astype(F32) + polar[b].astype(F32)
        ).astype(BF)

    def convolve(at):
        return (
            mid_rows[at, :].astype(F32)
            + jnp.dot(coeff[at, :], mixed[...], preferred_element_type=F32)
        ).astype(BF)

    done_out[...] = convolve(side_rows)
    to_done = remote(done_out, done_in, h_send.at[1], h_recv.at[1], sibling)
    to_done.start()
    out[:, own_cols] = convolve(own_rows)

    @pl.when(passes_own)
    def _():
        for d in to_back:
            d.wait_send()

    @pl.when(passes)
    def _():
        for d in to_far:
            d.wait_send()

    to_done.wait_recv()
    out[:, side_cols] = done_in[...]
    to_done.wait_send()


def in_hbm(value):
    return pltpu.with_memory_space_constraint(value, pltpu.HBM)


def fused_device(
    tokens, gain_attn, w_qkv, key_bias, w_out, gain_conv, w_conv, lat_taps, lon_half, lat_half, quad_off
):
    rows, width = tokens.shape[1:]
    shard = w_qkv.shape[0]
    heads = key_bias.shape[1]
    lat_count = width // shard
    nx = 2
    nz = lat_count // nx
    part, half, lons = width // 4, width // 2, 2 * rows
    vmem = pl.BlockSpec(memory_space=pltpu.VMEM)
    anywhere = pl.BlockSpec(memory_space=pltpu.HBM)
    dma = pltpu.SemaphoreType.DMA
    out = pl.pallas_call(
        lambda *refs: fused_kernel(nx, nz, *refs),
        out_shape=pltpu.VMEM((rows, width), BF),
        in_specs=[anywhere] * 11,
        out_specs=vmem,
        scratch_shapes=[
            pltpu.SMEM((2, lat_taps.shape[0]), F32),
            pltpu.SMEM((1,), jnp.int32),
            pltpu.SMEM((1,), jnp.int32),
            pltpu.SMEM((1,), jnp.int32),
            pltpu.VMEM((width,), F32),
            pltpu.VMEM(w_qkv.shape, BF),
            pltpu.VMEM((width,), F32),
            pltpu.VMEM((2, 64, half), BF),
            dma((12,)),
            pltpu.VMEM((shard, 3 * part), BF),
            pltpu.VMEM((width, 3 * part), BF),
            pltpu.VMEM((width, width), BF),
            pltpu.VMEM((2, lons, width), BF),
            pltpu.VMEM((2, lons, width), BF),
            pltpu.VMEM((2, 2, heads, rows), BF),
            pltpu.VMEM((2, heads, lons), F32),
            pltpu.VMEM((2, lons, part), BF),
            pltpu.VMEM((2, 4, rows, part), BF),
            pltpu.VMEM((2, rows, width), BF),
            pltpu.VMEM((3, lons, half), BF),
            pltpu.VMEM((rows, width), BF),
            pltpu.VMEM((lons, half), BF),
            pltpu.VMEM((2, 128, half), BF),
            pltpu.VMEM((2, lons, half), BF),
            pltpu.VMEM((2 * lons, half), BF),
            pltpu.VMEM((lons, 2 * lons), BF),
            pltpu.VMEM((rows, half), BF),
            pltpu.VMEM((rows, half), BF),
            dma((2,)), dma((2,)),
            dma((lat_count,)), dma((lat_count,)), dma((lat_count,)),
            dma((lat_count,)), dma((lat_count,)),
            dma((2,)), dma((2,)),
            dma((lat_count,)), dma((lat_count,)), dma((lat_count,)),
            dma((lat_count,)), dma((lat_count,)),
            dma((lat_count, 2)), dma((lat_count, 2)),
            dma((3,)), dma((3,)),
            dma((3,)), dma((3,)),
            dma((2, 3)), dma((2, 4)),
            dma((4,)), dma((2, 2)),
            dma((4,)), dma((3, 2)),
            dma((2,)), dma((2,)),
        ],
        compiler_params=pltpu.CompilerParams(
            collective_id=0, has_side_effects=True, vmem_limit_bytes=40 * 1024 * 1024
        ),
    )(
        in_hbm(lat_taps.T), lon_half, lat_half, quad_off,
        *[
            in_hbm(v)
            for v in (
                tokens[0], gain_attn, w_qkv, key_bias[0], w_out, gain_conv, jnp.swapaxes(w_conv, 1, 2)
            )
        ],
    )
    return out[None]


def solution(mesh):
    sizes = (mesh.shape["groups"], mesh.shape["lat"], mesh.shape["lon"])
    return jax.shard_map(
        fused_device if sizes == (2, 8, 2) else per_device,
        mesh=mesh,
        in_specs=(
            P(("groups", "lat"), "lon", None),
            P(),
            P("lat", None),
            P("lat", None, "lon"),
            P("lat", None),
            P(),
            P(),
            P(),
            P("lat"),
            P("lat"),
            P("lat"),
        ),
        out_specs=P(("groups", "lat"), "lon", None),
        check_vma=False,
    )
```

```python
import jax
import jax.numpy as jnp
from jax import lax
from jax.experimental import pallas as pl
from jax.experimental.pallas import tpu as pltpu
from jax.sharding import PartitionSpec as P


def padded(cells, sides, width):
    for axis, dim in sides:
        count = lax.axis_size(axis)
        ends = count - 1
        head = lax.slice_in_dim(cells, 0, width, axis=dim)
        tail = lax.slice_in_dim(cells, cells.shape[dim] - width, cells.shape[dim], axis=dim)
        cells = jnp.concatenate(
            [
                lax.ppermute(tail, axis, [(i, (i + 1) % count) for i in range(ends)]),
                cells,
                lax.ppermute(head, axis, [((i + 1) % count, i) for i in range(ends)]),
            ],
            axis=dim,
        )
    return cells


def layer_norm(inputs, gain):
    values = inputs.astype(jnp.float32)
    average = jnp.mean(values, axis=-1, keepdims=True)
    centered = values - average
    variance = jnp.mean(centered * centered, axis=-1, keepdims=True)
    return centered * lax.rsqrt(variance + 1e-05) * gain


def group_mix(inputs, w_conv):
    basis, length, channels = inputs.shape
    group_width = w_conv.shape[2]
    groups = channels // group_width
    mixed_rows = jnp.einsum(
        "kjgc,kgce->kjge",
        inputs.reshape(basis, length, groups, group_width),
        w_conv.reshape(basis, groups, group_width, group_width),
        preferred_element_type=jnp.float32,
    )
    return mixed_rows.reshape(basis, length, channels).astype(jnp.bfloat16)


def lon_weights(row_ids, col_ids, half_width, lon_total):
    offset_lon = (
        jnp.mod(col_ids[None, :] - row_ids[:, None] + lon_total // 2, lon_total) - lon_total // 2
    )
    distance = jnp.abs(offset_lon).astype(jnp.float32)
    span_plus = (half_width + 1).astype(jnp.float32)
    tent_weight = jnp.where(
        distance <= half_width.astype(jnp.float32), (1.0 - distance / span_plus) / span_plus, 0.0
    )
    odd_weight = tent_weight * offset_lon.astype(jnp.float32) / span_plus
    return jnp.stack([tent_weight, odd_weight]).astype(jnp.bfloat16)


def start_state(query_count, head_count, head_dim):
    running_max = jnp.full((head_count, query_count), -jnp.inf, jnp.float32)
    running_sum = jnp.zeros((head_count, query_count), jnp.float32)
    running_out = jnp.zeros((query_count, head_count, head_dim), jnp.float32)
    return (running_max, running_sum, running_out)


def attend_keys(carry_state, queries, key_rows, value_rows, bias_rows, score_scale):
    key_count = key_rows.shape[0]
    for offset in range(0, key_count, 128):
        running_max, running_sum, running_out = carry_state
        key_block = key_rows[offset : offset + 128]
        value_block = value_rows[offset : offset + 128]
        bias_block = bias_rows[offset : offset + 128]
        scores = (
            jnp.einsum("qhd,khd->hqk", queries, key_block, preferred_element_type=jnp.float32)
            * score_scale
        )
        scores = scores + bias_block.T.astype(jnp.float32)[:, None, :]
        new_max = jnp.maximum(running_max, jnp.max(scores, axis=-1))
        rescale = jnp.exp(running_max - new_max)
        exp_scores = jnp.exp(scores - new_max[:, :, None])
        running_sum = running_sum * rescale + jnp.sum(exp_scores, axis=-1)
        running_out = running_out * rescale.T[:, :, None] + jnp.einsum(
            "hqk,khd->qhd",
            exp_scores.astype(jnp.bfloat16),
            value_block,
            preferred_element_type=jnp.float32,
        )
        carry_state = (new_max, running_sum, running_out)
    return carry_state


def finish_state(carry_state):
    running_max, running_sum, running_out = carry_state
    finished = running_out / running_sum.T[:, :, None]
    return finished.reshape(finished.shape[0], -1).astype(jnp.bfloat16)


def lon_conv(blended, half_width, first_col, out_cols):
    lon_total = blended.shape[1]
    block_cols = min(128, lon_total)
    block_count = lon_total // block_cols
    first_block = jnp.floor_divide(first_col - half_width, block_cols)
    last_block = jnp.floor_divide(first_col + out_cols - 1 + half_width, block_cols)
    turn_count = jnp.minimum(block_count, last_block - first_block + 1)
    row_ids = first_col + jnp.arange(out_cols, dtype=jnp.int32)

    def add_block(turn_index, running_out):
        block_at = jnp.mod(first_block + turn_index, block_count)
        lon_block = lax.dynamic_slice_in_dim(blended, block_at * block_cols, block_cols, 1)
        col_ids = block_at * block_cols + jnp.arange(block_cols, dtype=jnp.int32)
        coeffs = lon_weights(row_ids, col_ids, half_width, lon_total)
        return running_out + jnp.einsum(
            "kjc,kcd->jd", coeffs, lon_block, preferred_element_type=jnp.float32
        )

    initial = jnp.zeros((out_cols, blended.shape[2]), jnp.float32)
    return lax.fori_loop(0, turn_count, add_block, initial)


def per_device(
    tokens,
    gain_attn,
    w_qkv,
    key_bias,
    w_out,
    gain_conv,
    w_conv,
    lat_taps,
    lon_half,
    lat_half,
    quad_off,
):
    own_tokens = tokens[0]
    count_lon, model_width = own_tokens.shape
    head_count = key_bias.shape[1]
    head_dim = model_width // head_count
    score_scale = head_dim ** (-0.5)
    lon_place = lax.axis_index("lon")
    normed = layer_norm(own_tokens, gain_attn).astype(jnp.bfloat16)
    bias_rows = key_bias[0].T
    full_qkv, full_out = (
        lax.all_gather(w_qkv, "lat", axis=0, tiled=True),
        lax.all_gather(w_out, "lat", axis=0, tiled=True),
    )
    projected = jnp.dot(normed, full_qkv, preferred_element_type=jnp.float32).astype(jnp.bfloat16)
    queries = projected[:, :model_width].reshape(count_lon, head_count, head_dim)
    key_here = projected[:, model_width : 2 * model_width]
    value_here = projected[:, 2 * model_width :]
    key_piece = lax.all_gather(key_here, "lon", axis=0, tiled=True)
    value_piece = lax.all_gather(value_here, "lon", axis=0, tiled=True)
    bias_piece = lax.all_gather(bias_rows, "lon", axis=0, tiled=True)
    length = key_piece.shape[0]
    carry_state = attend_keys(
        start_state(count_lon, head_count, head_dim),
        queries,
        key_piece.reshape(length, head_count, head_dim),
        value_piece.reshape(length, head_count, head_dim),
        bias_piece,
        score_scale,
    )
    attended = finish_state(carry_state)
    branch_out = jnp.dot(attended, full_out, preferred_element_type=jnp.float32)
    middle = (own_tokens.astype(jnp.float32) + branch_out).astype(jnp.bfloat16)
    conv_in = layer_norm(middle, gain_conv).astype(jnp.bfloat16)
    stacked = padded(conv_in[None], (("lat", 0),), 1)
    lat_row = lax.axis_index("lat")
    last_band = lax.axis_size("lat") - 1
    offsets = jnp.arange(3, dtype=jnp.int32) - 1
    one_hot = (
        (quad_off[0] + offsets + 1)[:, None]
        == jnp.arange(lat_taps.shape[0], dtype=jnp.int32)[None, :]
    ).astype(jnp.float32)
    tap_vals = jnp.dot(one_hot, lat_taps, precision=lax.Precision.HIGHEST)
    tap_vals = jnp.where((jnp.abs(offsets) <= lat_half[0])[:, None], tap_vals, 0.0)
    summed = jnp.einsum(
        "rk,rjd->kjd", tap_vals, stacked.astype(jnp.float32), precision=lax.Precision.HIGHEST
    ).astype(jnp.bfloat16)
    pole_gain = jnp.where(lat_row == 0, tap_vals[0], 0.0) + jnp.where(
        lat_row == last_band, tap_vals[2], 0.0
    )
    first_col = lon_place * count_lon
    pole_rows = (pole_gain[:, None, None] * conv_in.astype(jnp.float32)[None]).astype(jnp.bfloat16)
    mixed_rows = group_mix(summed, w_conv)
    pole_mixed = group_mix(pole_rows, w_conv)
    circle_rows, pole_all = (
        lax.all_gather(mixed_rows, "lon", axis=1, tiled=True),
        lax.all_gather(pole_mixed, "lon", axis=1, tiled=True),
    )
    lon_total = circle_rows.shape[1]
    blended = (
        circle_rows.astype(jnp.float32)
        + jnp.roll(pole_all, -(lon_total // 2), axis=1).astype(jnp.float32)
    ).astype(jnp.bfloat16)
    conv_out = lon_conv(blended, lon_half[0], first_col, count_lon)
    return (middle.astype(jnp.float32) + conv_out).astype(jnp.bfloat16)[None]


BF = jnp.bfloat16
F32 = jnp.float32
MESH = pl.DeviceIdType.MESH


def norm_rows(values, gain):
    values = values.astype(F32)
    average = jnp.mean(values, axis=-1, keepdims=True)
    centered = values - average
    variance = jnp.mean(centered * centered, axis=-1, keepdims=True)
    return (centered * lax.rsqrt(variance + 1e-05) * gain).astype(BF)


def fused_kernel(
    nx, nz,
    lat_taps_h, lon_half_h, lat_half_h, quad_off_h,
    tokens_h, gain_attn_h, w_qkv_h, key_bias_h, w_out_h, gain_conv_h, w_conv_h,
    out,
    lat_taps, lon_half, lat_half, quad_off, gain_attn, w_qkv, gain_conv, w_conv, load,
    ws, wq, wo, tok, normed, bias, bias_f, att_out, att_in, stage, normed_conv, middle, mid_rows,
    mixer, polar, mixed, coeff, done_out, done_in,
    xq_send, xq_recv, dq_send, zq_send, zq_recv, yq_send, yq_recv,
    xo_send, xo_recv, do_send, zo_send, zo_recv, yo_send, yo_recv, so_send, so_recv,
    t_send, t_recv, b_send, b_recv, a_send, a_recv,
    f_send, f_recv, c_send, c_recv, h_send, h_recv,
):
    y, place, c = lax.axis_index("groups"), lax.axis_index("lat"), lax.axis_index("lon")
    z, x = lax.div(place, nx), lax.rem(place, nx)
    quad = x * 2 + c
    x_place = z * nx + (1 - x)
    x_peer, x_diag = (y, x_place, c), (y, x_place, 1 - c)
    sibling = (y, place, 1 - c)
    y_peer = (1 - y, place, c)
    z_up, z_down = (y, place + nx, c), (y, place - nx, c)
    has_up, has_down = z < nz - 1, z > 0
    last_place = nx * nz - 1
    shard = w_qkv.shape[0]
    hs = shard // 2
    width = tokens_h.shape[1]
    rows = tokens_h.shape[0]
    head = 64
    part = width // 4
    half = width // 2

    barrier = pltpu.get_barrier_semaphore()

    def greet(device):
        pl.semaphore_signal(barrier, inc=1, device_id=device, device_id_type=MESH)

    def when(cond, run):
        if cond is None:
            run()
        else:
            pl.when(cond)(run)

    for device in (x_peer, x_diag, sibling, y_peer):
        greet(device)
    leap = nz - 1
    aims = [(has_down, z - 1), (z >= leap, z - leap), (has_up, z + 1)]
    for cond, zz in ((has_up, z + 1), (has_down, z - 1), (z < nz - leap, z + leap)):
        def both(zz=zz):
            greet((y, zz * nx, c))
            greet((y, zz * nx + 1, c))

        when(cond, both)
    for cond, zz in ((has_up, z + 1), (has_down, z - 1)):
        def others(zz=zz):
            greet((y, zz * nx, 1 - c))
            greet((y, zz * nx + 1, 1 - c))

        when(cond, others)

    loads = [
        pltpu.make_async_copy(source, target, load.at[k])
        for k, (source, target) in enumerate(
            (
                (w_qkv_h.at[pl.ds(y * hs, hs), :], w_qkv.at[pl.ds(y * hs, hs), :]),
                (tokens_h, tok.at[x, pl.ds(c * rows, rows), :]),
                (gain_attn_h, gain_attn),
                (w_conv_h.at[:, :, pl.ds(c * half, half)], w_conv),
                (key_bias_h, bias.at[x, c]),
                (w_out_h, wo.at[pl.ds(place * shard, shard), :]),
                (gain_conv_h, gain_conv),
                (lat_taps_h, lat_taps),
                (lon_half_h, lon_half),
                (lat_half_h, lat_half),
                (quad_off_h, quad_off),
                (w_qkv_h.at[pl.ds((1 - y) * hs, hs), :], w_qkv.at[pl.ds((1 - y) * hs, hs), :]),
            )
        )
    ]
    loads[0].start()
    loads[1].start()
    loads[11].start()
    for copy in loads[2:11]:
        copy.start()

    def columns(pick, h):
        return jnp.concatenate(
            [
                w_qkv[pl.ds(h * hs, hs), j * width + pick * part : j * width + (pick + 1) * part]
                for j in range(3)
            ],
            axis=1,
        )

    def spread(h):
        for pick in range(4):
            @pl.when(quad == pick)
            def _(pick=pick):
                ws[pl.ds(h * hs, hs), :] = columns((pick + 2) % 4, h)
                wq[pl.ds(place * shard + h * hs, hs), :] = columns(pick, h)

    loads[0].wait()
    spread(y)
    pl.semaphore_wait(
        barrier,
        4 + 4 * has_up.astype(jnp.int32) + 4 * has_down.astype(jnp.int32) + 2 * (z >= leap).astype(jnp.int32),
    )

    def remote(source, target, send, recv, device):
        return pltpu.make_async_remote_copy(
            src_ref=source, dst_ref=target, send_sem=send, recv_sem=recv,
            device_id=device, device_id_type=MESH,
        )

    start = lambda d: d.start()
    finish = lambda d: d.wait_send()

    def q_at(slot, h):
        return wq.at[pl.ds(slot * shard + h * hs, hs), :]

    def o_at(slot, h, cc):
        return wo.at[pl.ds(slot * shard + h * hs, hs), pl.ds(cc * half, half)]

    def q_cross(k):
        h = y if k == 0 else 1 - y
        return remote(ws.at[pl.ds(h * hs, hs), :], q_at(place, h), xq_send.at[k], xq_recv.at[k], x_peer)

    def q_crossed(k):
        h = y if k == 0 else 1 - y
        return remote(ws.at[pl.ds(h * hs, hs), :], q_at(x_place, h), xq_send.at[k], xq_recv.at[k], x_peer)

    def q_direct(zz, other):
        xx = (1 - x) if other else x
        source = ws.at[pl.ds(y * hs, hs), :] if other else q_at(place, y)
        return remote(
            source, q_at(place, y), dq_send.at[zz * nx + xx], zq_recv.at[place],
            (y, zz * nx + xx, c),
        )

    def q_along(slot, device):
        return remote(q_at(slot, y), q_at(slot, y), zq_send.at[slot], zq_recv.at[slot], device)

    def q_over(slot, h):
        return remote(q_at(slot, h), q_at(slot, h), yq_send.at[slot], yq_recv.at[slot], y_peer)

    def o_cross(slot, k):
        h = y if k == 0 else 1 - y
        return remote(o_at(slot, h, c), o_at(slot, h, c), xo_send.at[k], xo_recv.at[k], x_peer)

    def o_direct(zz, other):
        xx = (1 - x) if other else x
        return remote(
            o_at(place, y, c), o_at(place, y, c), do_send.at[zz * nx + xx], zo_recv.at[place],
            (y, zz * nx + xx, c),
        )

    def o_along(slot, device):
        return remote(o_at(slot, y, c), o_at(slot, y, c), zo_send.at[slot], zo_recv.at[slot], device)

    def o_over(slot, h):
        return remote(o_at(slot, h, c), o_at(slot, h, c), yo_send.at[slot], yo_recv.at[slot], y_peer)

    def o_side(slot, h, cc):
        return remote(
            o_at(slot, h, cc), o_at(slot, h, cc), so_send.at[slot, h], so_recv.at[slot, h], sibling
        )

    def deal(direct, act):
        for cond, zz in aims:
            def both(zz=zz):
                act(direct(zz, True))
                act(direct(zz, False))

            when(cond, both)

    far = []
    for t in range(1, nz):
        for sign, reach, going, device in (
            (-1, z >= t, has_up, z_up),
            (1, z + t <= nz - 1, has_down if 1 <= t < leap - 1 else None, z_down),
        ):
            for xx in (x, 1 - x):
                far.append(
                    (
                        t * sign, reach, (z + sign * t) * nx + xx,
                        None if going is None else jnp.logical_and(reach, going), device,
                    )
                )

    def q_step(t, act):
        for tt, reach, slot, going, device in far:
            if tt == t:
                if act is start:
                    when(reach, lambda slot=slot: q_along(slot, z_up).wait_recv())
                if going is not None:
                    when(going, lambda slot=slot, device=device: act(q_along(slot, device)))
                when(reach, lambda slot=slot: act(q_over(slot, y)))

    def o_step(t, act):
        for tt, reach, slot, going, device in far:
            if tt == t:
                if act is start:
                    when(reach, lambda slot=slot: o_along(slot, z_up).wait_recv())
                if going is not None:
                    when(going, lambda slot=slot, device=device: act(o_along(slot, device)))
                when(reach, lambda slot=slot: act(o_over(slot, y)))
                when(reach, lambda slot=slot: act(o_side(slot, y, c)))

    def o_gather(act, ts=range(1, nz)):
        for t, reach, slot, _, _ in far:
            if abs(t) not in ts:
                continue
            if act is start:
                when(reach, lambda slot=slot: o_over(slot, 1 - y).wait_recv())
            when(reach, lambda slot=slot: act(o_side(slot, 1 - y, c)))

    def o_near(act):
        for k, h in ((0, y), (1, 1 - y)):
            if act is start:
                o_cross(x_place, k).wait_recv()
            act(o_side(x_place, h, c))

    def tok_at(b, cc):
        return tok.at[b, pl.ds(cc * rows, rows), :]

    tok_copies = [
        remote(tok_at(x, c), tok_at(x, c), t_send.at[0], t_recv.at[0], x_peer),
        remote(tok_at(x, c), tok_at(x, c), t_send.at[1], t_recv.at[1], sibling),
        remote(tok_at(1 - x, c), tok_at(1 - x, c), t_send.at[2], t_recv.at[2], sibling),
    ]
    bias_copies = [
        remote(bias.at[x, c], bias.at[x, c], b_send.at[k], b_recv.at[k], device)
        for k, device in enumerate((x_peer, sibling, x_diag))
    ]

    deal(q_direct, start)
    loads[1].wait()
    tok_copies[0].start()
    tok_copies[1].start()
    loads[11].wait()
    spread(1 - y)
    q_cross(0).start()
    q_cross(1).start()
    loads[4].wait()
    for copy in bias_copies:
        copy.start()
    loads[2].wait()
    gain_a = gain_attn[...][None]

    def norm_block(b, cc):
        normed[b, pl.ds(cc * rows, rows), :] = norm_rows(tok[b, pl.ds(cc * rows, rows), :], gain_a)

    norm_block(x, c)
    tok_copies[1].wait_recv()
    norm_block(x, 1 - c)
    q_step(-1, start)
    q_step(1, start)
    q_step(3, start)
    loads[5].wait()
    deal(o_direct, start)
    o_cross(place, 0).start()
    o_cross(place, 1).start()
    q_step(2, start)
    q_step(-2, start)
    q_step(-3, start)
    tok_copies[0].wait_recv()
    tok_copies[2].start()
    norm_block(1 - x, c)
    tok_copies[2].wait_recv()
    norm_block(1 - x, 1 - c)

    loads[3].wait()
    pair_row = lax.broadcasted_iota(jnp.int32, (2 * head, half), 0)
    pair_col = lax.broadcasted_iota(jnp.int32, (2 * head, half), 1)
    same = lax.rem(lax.div(pair_col, head), 2) == lax.div(pair_row, head)
    for b in range(2):
        wide = jnp.concatenate([w_conv[b], w_conv[b]], axis=0).astype(F32)
        mixer[b] = jnp.where(same, wide, 0.0).astype(BF)
    for copy in bias_copies:
        copy.wait_recv()
    for b in range(2):
        bias_f[b] = jnp.concatenate([bias[b, 0], bias[b, 1]], axis=1).astype(F32)
    for k in range(6, 11):
        loads[k].wait()

    o_step(1, start)
    o_step(-1, start)
    o_step(3, start)
    span = (lon_half[0] + 1).astype(F32)
    limit = lon_half[0].astype(F32)
    lons = 2 * rows
    diff = lax.broadcasted_iota(jnp.int32, (lons, lons), 1) - lax.broadcasted_iota(
        jnp.int32, (lons, lons), 0
    )
    offset = jnp.where(diff >= rows, diff - lons, jnp.where(diff < -rows, diff + lons, diff))
    offset = offset.astype(F32)
    distance = jnp.abs(offset)
    tent = jnp.where(distance <= limit, (1.0 - distance / span) / span, 0.0)
    coeff[:, :lons] = tent.astype(BF)
    coeff[:, lons:] = (tent * offset / span).astype(BF)

    q_crossed(0).wait_recv()
    q_crossed(1).wait_recv()
    for _, reach, slot, _, _ in far:
        when(reach, lambda slot=slot: q_over(slot, 1 - y).wait_recv())

    def att_copies(b, n):
        return [
            remote(
                att_out.at[b, pl.ds(cc * rows, rows), :], att_in.at[b, quad],
                a_send.at[n, k], a_recv.at[b, quad], device,
            )
            for k, (cc, device) in enumerate(((c, x_peer), (1 - c, x_diag), (1 - c, sibling)))
        ]

    def attend(b, between):
        projected = jnp.dot(normed[b], wq[...], preferred_element_type=F32).astype(BF)
        between()
        pieces = []
        for h in range(3):
            queries = projected[:, h * head : (h + 1) * head] * jnp.asarray(head ** -0.5, BF)
            keys = projected[:, part + h * head : part + (h + 1) * head]
            vals = projected[:, 2 * part + h * head : 2 * part + (h + 1) * head]
            scores = lax.dot_general(
                queries, keys, (((1,), (1,)), ((), ())), preferred_element_type=F32
            ) + bias_f[b, pl.ds(quad * 3 + h, 1), :]
            expd = jnp.exp(scores - jnp.max(scores, axis=-1, keepdims=True))
            totals = jnp.sum(expd, axis=-1, keepdims=True)
            pieces.append(jnp.dot(expd.astype(BF), vals, preferred_element_type=F32) / totals)
        att_out[b] = jnp.concatenate(pieces, axis=1).astype(BF)

    o_near(start)
    attend(x, lambda: None)
    for copy in att_copies(x, 0):
        copy.start()
    att_in[x, quad] = att_out[x, pl.ds(c * rows, rows), :]
    o_step(-2, start)
    o_step(2, start)
    attend(1 - x, lambda: None)
    for copy in att_copies(1 - x, 1):
        copy.start()
    att_in[1 - x, quad] = att_out[1 - x, pl.ds(c * rows, rows), :]
    o_step(-3, start)
    o_gather(start)

    for _, reach, slot, _, _ in far:
        def landed(slot=slot):
            o_side(slot, 0, 1 - c).wait_recv()
            o_side(slot, 1, 1 - c).wait_recv()

        when(reach, landed)
    o_side(x_place, 0, 1 - c).wait_recv()
    o_side(x_place, 1, 1 - c).wait_recv()

    near, away = 2 * (1 - x), 2 * x
    passes = jnp.logical_or(jnp.logical_and(x == 0, has_up), jnp.logical_and(x == 1, has_down))
    gets = jnp.logical_or(jnp.logical_and(x == 0, has_down), jnp.logical_and(x == 1, has_up))
    onward = place + nx * (1 - 2 * x)
    split = rows // 2
    passes_own = jnp.logical_or(jnp.logical_and(x == 1, has_up), jnp.logical_and(x == 0, has_down))
    back = (z - 1 + 2 * x) * nx + 1 - x

    def band(b):
        for source in (x * 2 + 1 - c, (1 - x) * 2 + c, (1 - x) * 2 + 1 - c):
            remote(att_in.at[b, source], att_in.at[b, source], a_send.at[0, 0], a_recv.at[b, source], sibling).wait_recv()
        branch = tok[b, pl.ds(c * rows, rows), :].astype(F32)
        for p in range(4):
            branch = branch + jnp.dot(
                att_in[b, p], wo[p * part : (p + 1) * part, :], preferred_element_type=F32
            )
        return branch.astype(BF)

    gain_c = gain_conv[...][None]
    own_rows = pl.ds(c * rows, rows)
    side_rows = pl.ds((1 - c) * rows, rows)
    own_cols = pl.ds(c * half, half)
    side_cols = pl.ds((1 - c) * half, half)

    def conv_copy(source, which, cc, k, device):
        return remote(
            source, normed_conv.at[which, pl.ds(cc * rows, rows), :],
            c_send.at[k], c_recv.at[which, cc], device,
        )

    stage[0] = norm_rows(band(1 - x), gain_c)
    def far_copy(which, first, cc, cols, k, device):
        start_row = 0 if first else split
        target = 2 * x if first else 2 * (1 - x)
        return remote(
            stage.at[which, pl.ds(start_row, split), cols],
            normed_conv.at[target, pl.ds(cc * rows + start_row, split), :],
            f_send.at[k], f_recv.at[cc, 0 if first else 1], device,
        )

    to_far = [
        far_copy(0, True, c, own_cols, 0, (y, onward, c)),
        far_copy(0, True, c, side_cols, 1, (y, onward, 1 - c)),
    ]
    to_back = [
        far_copy(1, False, c, own_cols, 2, (y, back, c)),
        far_copy(1, False, c, side_cols, 3, (y, back, 1 - c)),
    ]

    @pl.when(passes)
    def _():
        for d in to_far:
            d.start()

    to_side = [conv_copy(stage.at[0, :, side_cols], near, c, 2, sibling)]
    to_side[0].start()
    normed_conv[near, own_rows, :] = stage[0, :, own_cols]

    mid = band(x)
    middle[...] = mid
    stage[1] = norm_rows(mid, gain_c)
    @pl.when(passes_own)
    def _():
        for d in to_back:
            d.start()

    to_side.append(conv_copy(stage.at[1, :, side_cols], 1, c, 3, sibling))
    to_side[1].start()
    to_mid = remote(middle.at[:, side_cols], mid_rows.at[own_rows, :], h_send.at[0], h_recv.at[0], sibling)
    to_mid.start()
    normed_conv[1, own_rows, :] = stage[1, :, own_cols]
    mid_rows[own_rows, :] = middle[:, own_cols]

    @pl.when(jnp.logical_not(gets))
    def _():
        normed_conv[away] = jnp.zeros((lons, half), BF)

    base = quad_off[0]
    wide_ok = lat_half[0] >= 1
    taps = [
        [
            lat_taps[b, base + r] if r == 1 else jnp.where(wide_ok, lat_taps[b, base + r], 0.0)
            for b in range(2)
        ]
        for r in range(3)
    ]

    def mix(values, b):
        return jnp.concatenate(
            [
                lax.dot_general(
                    values[:, p * 2 * head : (p + 1) * 2 * head],
                    mixer[b, :, p * 2 * head : (p + 1) * 2 * head],
                    (((1,), (1,)), ((), ())),
                    preferred_element_type=F32,
                )
                for p in range(half // (2 * head))
            ],
            axis=1,
        ).astype(BF)

    conv_copy(stage.at[1, :, side_cols], 1, 1 - c, 3, sibling).wait_recv()
    for b in range(2):
        gain = jnp.where(place == 0, taps[0][b], 0.0) + jnp.where(place == last_place, taps[2][b], 0.0)
        pole = mix((gain * normed_conv[1].astype(F32)).astype(BF), b)
        polar[b, :rows] = pole[rows:]
        polar[b, rows:] = pole[:rows]
    conv_copy(stage.at[0, :, side_cols], near, 1 - c, 2, sibling).wait_recv()
    remote(middle.at[:, side_cols], mid_rows.at[side_rows, :], h_send.at[0], h_recv.at[0], sibling).wait_recv()

    q_cross(0).wait_send()
    q_cross(1).wait_send()
    o_cross(place, 0).wait_send()
    o_cross(place, 1).wait_send()
    deal(q_direct, finish)
    deal(o_direct, finish)
    o_near(finish)
    for t in range(1, nz):
        for signed in (t, -t):
            q_step(signed, finish)
            o_step(signed, finish)
    o_gather(finish)
    for d in tok_copies + bias_copies + att_copies(x, 0) + att_copies(1 - x, 1) + to_side + [to_mid]:
        d.wait_send()

    @pl.when(gets)
    def _():
        for cc in range(2):
            for part in range(2):
                target = normed_conv.at[away, pl.ds(cc * rows + part * split, split), :]
                remote(target, target, f_send.at[0], f_recv.at[cc, part], sibling).wait_recv()

    for b in range(2):
        summed = (
            taps[0][b] * normed_conv[0].astype(F32)
            + taps[1][b] * normed_conv[1].astype(F32)
            + taps[2][b] * normed_conv[2].astype(F32)
        ).astype(BF)
        mixed[b * lons : (b + 1) * lons, :] = (
            mix(summed, b).astype(F32) + polar[b].astype(F32)
        ).astype(BF)

    def convolve(at):
        return (
            mid_rows[at, :].astype(F32)
            + jnp.dot(coeff[at, :], mixed[...], preferred_element_type=F32)
        ).astype(BF)

    done_out[...] = convolve(side_rows)
    to_done = remote(done_out, done_in, h_send.at[1], h_recv.at[1], sibling)
    to_done.start()
    out[:, own_cols] = convolve(own_rows)

    @pl.when(passes_own)
    def _():
        for d in to_back:
            d.wait_send()

    @pl.when(passes)
    def _():
        for d in to_far:
            d.wait_send()

    to_done.wait_recv()
    out[:, side_cols] = done_in[...]
    to_done.wait_send()


def in_hbm(value):
    return pltpu.with_memory_space_constraint(value, pltpu.HBM)


def fused_device(
    tokens, gain_attn, w_qkv, key_bias, w_out, gain_conv, w_conv, lat_taps, lon_half, lat_half, quad_off
):
    rows, width = tokens.shape[1:]
    shard = w_qkv.shape[0]
    heads = key_bias.shape[1]
    lat_count = width // shard
    nx = 2
    nz = lat_count // nx
    part, half, lons = width // 4, width // 2, 2 * rows
    vmem = pl.BlockSpec(memory_space=pltpu.VMEM)
    anywhere = pl.BlockSpec(memory_space=pltpu.HBM)
    dma = pltpu.SemaphoreType.DMA
    out = pl.pallas_call(
        lambda *refs: fused_kernel(nx, nz, *refs),
        out_shape=pltpu.VMEM((rows, width), BF),
        in_specs=[anywhere] * 11,
        out_specs=vmem,
        scratch_shapes=[
            pltpu.SMEM((2, lat_taps.shape[0]), F32),
            pltpu.SMEM((1,), jnp.int32),
            pltpu.SMEM((1,), jnp.int32),
            pltpu.SMEM((1,), jnp.int32),
            pltpu.VMEM((width,), F32),
            pltpu.VMEM(w_qkv.shape, BF),
            pltpu.VMEM((width,), F32),
            pltpu.VMEM((2, 64, half), BF),
            dma((12,)),
            pltpu.VMEM((shard, 3 * part), BF),
            pltpu.VMEM((width, 3 * part), BF),
            pltpu.VMEM((width, width), BF),
            pltpu.VMEM((2, lons, width), BF),
            pltpu.VMEM((2, lons, width), BF),
            pltpu.VMEM((2, 2, heads, rows), BF),
            pltpu.VMEM((2, heads, lons), F32),
            pltpu.VMEM((2, lons, part), BF),
            pltpu.VMEM((2, 4, rows, part), BF),
            pltpu.VMEM((2, rows, width), BF),
            pltpu.VMEM((3, lons, half), BF),
            pltpu.VMEM((rows, width), BF),
            pltpu.VMEM((lons, half), BF),
            pltpu.VMEM((2, 128, half), BF),
            pltpu.VMEM((2, lons, half), BF),
            pltpu.VMEM((2 * lons, half), BF),
            pltpu.VMEM((lons, 2 * lons), BF),
            pltpu.VMEM((rows, half), BF),
            pltpu.VMEM((rows, half), BF),
            dma((2,)), dma((2,)),
            dma((lat_count,)), dma((lat_count,)), dma((lat_count,)),
            dma((lat_count,)), dma((lat_count,)),
            dma((2,)), dma((2,)),
            dma((lat_count,)), dma((lat_count,)), dma((lat_count,)),
            dma((lat_count,)), dma((lat_count,)),
            dma((lat_count, 2)), dma((lat_count, 2)),
            dma((3,)), dma((3,)),
            dma((3,)), dma((3,)),
            dma((2, 3)), dma((2, 4)),
            dma((4,)), dma((2, 2)),
            dma((4,)), dma((3, 2)),
            dma((2,)), dma((2,)),
        ],
        compiler_params=pltpu.CompilerParams(
            collective_id=0, has_side_effects=True, vmem_limit_bytes=40 * 1024 * 1024
        ),
    )(
        in_hbm(lat_taps.T), lon_half, lat_half, quad_off,
        *[
            in_hbm(v)
            for v in (
                tokens[0], gain_attn, w_qkv, key_bias[0], w_out, gain_conv, jnp.swapaxes(w_conv, 1, 2)
            )
        ],
    )
    return out[None]


def solution(mesh):
    sizes = (mesh.shape["groups"], mesh.shape["lat"], mesh.shape["lon"])
    return jax.shard_map(
        fused_device if sizes == (2, 8, 2) else per_device,
        mesh=mesh,
        in_specs=(
            P(("groups", "lat"), "lon", None),
            P(),
            P("lat", None),
            P("lat", None, "lon"),
            P("lat", None),
            P(),
            P(),
            P(),
            P("lat"),
            P("lat"),
            P("lat"),
        ),
        out_specs=P(("groups", "lat"), "lon", None),
        check_vma=False,
    )
```

```python
import jax
import jax.numpy as jnp
from jax import lax
from jax.experimental import pallas as pl
from jax.experimental.pallas import tpu as pltpu
from jax.sharding import PartitionSpec as P


def padded(cells, sides, width):
    for axis, dim in sides:
        count = lax.axis_size(axis)
        ends = count - 1
        head = lax.slice_in_dim(cells, 0, width, axis=dim)
        tail = lax.slice_in_dim(cells, cells.shape[dim] - width, cells.shape[dim], axis=dim)
        cells = jnp.concatenate(
            [
                lax.ppermute(tail, axis, [(i, (i + 1) % count) for i in range(ends)]),
                cells,
                lax.ppermute(head, axis, [((i + 1) % count, i) for i in range(ends)]),
            ],
            axis=dim,
        )
    return cells


def layer_norm(inputs, gain):
    values = inputs.astype(jnp.float32)
    average = jnp.mean(values, axis=-1, keepdims=True)
    centered = values - average
    variance = jnp.mean(centered * centered, axis=-1, keepdims=True)
    return centered * lax.rsqrt(variance + 1e-05) * gain


def group_mix(inputs, w_conv):
    basis, length, channels = inputs.shape
    group_width = w_conv.shape[2]
    groups = channels // group_width
    mixed_rows = jnp.einsum(
        "kjgc,kgce->kjge",
        inputs.reshape(basis, length, groups, group_width),
        w_conv.reshape(basis, groups, group_width, group_width),
        preferred_element_type=jnp.float32,
    )
    return mixed_rows.reshape(basis, length, channels).astype(jnp.bfloat16)


def lon_weights(row_ids, col_ids, half_width, lon_total):
    offset_lon = (
        jnp.mod(col_ids[None, :] - row_ids[:, None] + lon_total // 2, lon_total) - lon_total // 2
    )
    distance = jnp.abs(offset_lon).astype(jnp.float32)
    span_plus = (half_width + 1).astype(jnp.float32)
    tent_weight = jnp.where(
        distance <= half_width.astype(jnp.float32), (1.0 - distance / span_plus) / span_plus, 0.0
    )
    odd_weight = tent_weight * offset_lon.astype(jnp.float32) / span_plus
    return jnp.stack([tent_weight, odd_weight]).astype(jnp.bfloat16)


def start_state(query_count, head_count, head_dim):
    running_max = jnp.full((head_count, query_count), -jnp.inf, jnp.float32)
    running_sum = jnp.zeros((head_count, query_count), jnp.float32)
    running_out = jnp.zeros((query_count, head_count, head_dim), jnp.float32)
    return (running_max, running_sum, running_out)


def attend_keys(carry_state, queries, key_rows, value_rows, bias_rows, score_scale):
    key_count = key_rows.shape[0]
    for offset in range(0, key_count, 128):
        running_max, running_sum, running_out = carry_state
        key_block = key_rows[offset : offset + 128]
        value_block = value_rows[offset : offset + 128]
        bias_block = bias_rows[offset : offset + 128]
        scores = (
            jnp.einsum("qhd,khd->hqk", queries, key_block, preferred_element_type=jnp.float32)
            * score_scale
        )
        scores = scores + bias_block.T.astype(jnp.float32)[:, None, :]
        new_max = jnp.maximum(running_max, jnp.max(scores, axis=-1))
        rescale = jnp.exp(running_max - new_max)
        exp_scores = jnp.exp(scores - new_max[:, :, None])
        running_sum = running_sum * rescale + jnp.sum(exp_scores, axis=-1)
        running_out = running_out * rescale.T[:, :, None] + jnp.einsum(
            "hqk,khd->qhd",
            exp_scores.astype(jnp.bfloat16),
            value_block,
            preferred_element_type=jnp.float32,
        )
        carry_state = (new_max, running_sum, running_out)
    return carry_state


def finish_state(carry_state):
    running_max, running_sum, running_out = carry_state
    finished = running_out / running_sum.T[:, :, None]
    return finished.reshape(finished.shape[0], -1).astype(jnp.bfloat16)


def lon_conv(blended, half_width, first_col, out_cols):
    lon_total = blended.shape[1]
    block_cols = min(128, lon_total)
    block_count = lon_total // block_cols
    first_block = jnp.floor_divide(first_col - half_width, block_cols)
    last_block = jnp.floor_divide(first_col + out_cols - 1 + half_width, block_cols)
    turn_count = jnp.minimum(block_count, last_block - first_block + 1)
    row_ids = first_col + jnp.arange(out_cols, dtype=jnp.int32)

    def add_block(turn_index, running_out):
        block_at = jnp.mod(first_block + turn_index, block_count)
        lon_block = lax.dynamic_slice_in_dim(blended, block_at * block_cols, block_cols, 1)
        col_ids = block_at * block_cols + jnp.arange(block_cols, dtype=jnp.int32)
        coeffs = lon_weights(row_ids, col_ids, half_width, lon_total)
        return running_out + jnp.einsum(
            "kjc,kcd->jd", coeffs, lon_block, preferred_element_type=jnp.float32
        )

    initial = jnp.zeros((out_cols, blended.shape[2]), jnp.float32)
    return lax.fori_loop(0, turn_count, add_block, initial)


def per_device(
    tokens,
    gain_attn,
    w_qkv,
    key_bias,
    w_out,
    gain_conv,
    w_conv,
    lat_taps,
    lon_half,
    lat_half,
    quad_off,
):
    own_tokens = tokens[0]
    count_lon, model_width = own_tokens.shape
    head_count = key_bias.shape[1]
    head_dim = model_width // head_count
    score_scale = head_dim ** (-0.5)
    lon_place = lax.axis_index("lon")
    normed = layer_norm(own_tokens, gain_attn).astype(jnp.bfloat16)
    bias_rows = key_bias[0].T
    full_qkv, full_out = (
        lax.all_gather(w_qkv, "lat", axis=0, tiled=True),
        lax.all_gather(w_out, "lat", axis=0, tiled=True),
    )
    projected = jnp.dot(normed, full_qkv, preferred_element_type=jnp.float32).astype(jnp.bfloat16)
    queries = projected[:, :model_width].reshape(count_lon, head_count, head_dim)
    key_here = projected[:, model_width : 2 * model_width]
    value_here = projected[:, 2 * model_width :]
    key_piece = lax.all_gather(key_here, "lon", axis=0, tiled=True)
    value_piece = lax.all_gather(value_here, "lon", axis=0, tiled=True)
    bias_piece = lax.all_gather(bias_rows, "lon", axis=0, tiled=True)
    length = key_piece.shape[0]
    carry_state = attend_keys(
        start_state(count_lon, head_count, head_dim),
        queries,
        key_piece.reshape(length, head_count, head_dim),
        value_piece.reshape(length, head_count, head_dim),
        bias_piece,
        score_scale,
    )
    attended = finish_state(carry_state)
    branch_out = jnp.dot(attended, full_out, preferred_element_type=jnp.float32)
    middle = (own_tokens.astype(jnp.float32) + branch_out).astype(jnp.bfloat16)
    conv_in = layer_norm(middle, gain_conv).astype(jnp.bfloat16)
    stacked = padded(conv_in[None], (("lat", 0),), 1)
    lat_row = lax.axis_index("lat")
    last_band = lax.axis_size("lat") - 1
    offsets = jnp.arange(3, dtype=jnp.int32) - 1
    one_hot = (
        (quad_off[0] + offsets + 1)[:, None]
        == jnp.arange(lat_taps.shape[0], dtype=jnp.int32)[None, :]
    ).astype(jnp.float32)
    tap_vals = jnp.dot(one_hot, lat_taps, precision=lax.Precision.HIGHEST)
    tap_vals = jnp.where((jnp.abs(offsets) <= lat_half[0])[:, None], tap_vals, 0.0)
    summed = jnp.einsum(
        "rk,rjd->kjd", tap_vals, stacked.astype(jnp.float32), precision=lax.Precision.HIGHEST
    ).astype(jnp.bfloat16)
    pole_gain = jnp.where(lat_row == 0, tap_vals[0], 0.0) + jnp.where(
        lat_row == last_band, tap_vals[2], 0.0
    )
    first_col = lon_place * count_lon
    pole_rows = (pole_gain[:, None, None] * conv_in.astype(jnp.float32)[None]).astype(jnp.bfloat16)
    mixed_rows = group_mix(summed, w_conv)
    pole_mixed = group_mix(pole_rows, w_conv)
    circle_rows, pole_all = (
        lax.all_gather(mixed_rows, "lon", axis=1, tiled=True),
        lax.all_gather(pole_mixed, "lon", axis=1, tiled=True),
    )
    lon_total = circle_rows.shape[1]
    blended = (
        circle_rows.astype(jnp.float32)
        + jnp.roll(pole_all, -(lon_total // 2), axis=1).astype(jnp.float32)
    ).astype(jnp.bfloat16)
    conv_out = lon_conv(blended, lon_half[0], first_col, count_lon)
    return (middle.astype(jnp.float32) + conv_out).astype(jnp.bfloat16)[None]


BF = jnp.bfloat16
F32 = jnp.float32
MESH = pl.DeviceIdType.MESH


def norm_rows(values, gain):
    values = values.astype(F32)
    average = jnp.mean(values, axis=-1, keepdims=True)
    centered = values - average
    variance = jnp.mean(centered * centered, axis=-1, keepdims=True)
    return (centered * lax.rsqrt(variance + 1e-05) * gain).astype(BF)


def fused_kernel(
    nx, nz,
    lat_taps_h, lon_half_h, lat_half_h, quad_off_h,
    tokens_h, gain_attn_h, w_qkv_h, key_bias_h, w_out_h, gain_conv_h, w_conv_h,
    out,
    lat_taps, lon_half, lat_half, quad_off, gain_attn, w_qkv, gain_conv, w_conv, load,
    ws, wq, wo, tok, normed, bias, bias_f, att_out, att_in, stage, normed_conv, middle, mid_rows,
    mixer, polar, mixed, coeff, done_out, done_in,
    xq_send, xq_recv, dq_send, zq_send, zq_recv, yq_send, yq_recv,
    xo_send, xo_recv, do_send, zo_send, zo_recv, yo_send, yo_recv, so_send, so_recv,
    t_send, t_recv, b_send, b_recv, a_send, a_recv,
    f_send, f_recv, c_send, c_recv, h_send, h_recv,
):
    y, place, c = lax.axis_index("groups"), lax.axis_index("lat"), lax.axis_index("lon")
    z, x = lax.div(place, nx), lax.rem(place, nx)
    quad = x * 2 + c
    x_place = z * nx + (1 - x)
    x_peer, x_diag = (y, x_place, c), (y, x_place, 1 - c)
    sibling = (y, place, 1 - c)
    y_peer = (1 - y, place, c)
    z_up, z_down = (y, place + nx, c), (y, place - nx, c)
    has_up, has_down = z < nz - 1, z > 0
    last_place = nx * nz - 1
    shard = w_qkv.shape[0]
    hs = shard // 2
    width = tokens_h.shape[1]
    rows = tokens_h.shape[0]
    head = 64
    part = width // 4
    half = width // 2

    barrier = pltpu.get_barrier_semaphore()

    def greet(device):
        pl.semaphore_signal(barrier, inc=1, device_id=device, device_id_type=MESH)

    def when(cond, run):
        if cond is None:
            run()
        else:
            pl.when(cond)(run)

    for device in (x_peer, x_diag, sibling, y_peer):
        greet(device)
    leap = nz - 1
    aims = [(has_down, z - 1), (z >= leap, z - leap), (has_up, z + 1)]
    for cond, zz in ((has_up, z + 1), (has_down, z - 1), (z < nz - leap, z + leap)):
        def both(zz=zz):
            greet((y, zz * nx, c))
            greet((y, zz * nx + 1, c))

        when(cond, both)
    for cond, zz in ((has_up, z + 1), (has_down, z - 1)):
        def others(zz=zz):
            greet((y, zz * nx, 1 - c))
            greet((y, zz * nx + 1, 1 - c))

        when(cond, others)

    loads = [
        pltpu.make_async_copy(source, target, load.at[k])
        for k, (source, target) in enumerate(
            (
                (w_qkv_h.at[pl.ds(y * hs, hs), :], w_qkv.at[pl.ds(y * hs, hs), :]),
                (tokens_h, tok.at[x, pl.ds(c * rows, rows), :]),
                (gain_attn_h, gain_attn),
                (w_conv_h.at[:, :, pl.ds(c * half, half)], w_conv),
                (key_bias_h, bias.at[x, c]),
                (w_out_h, wo.at[pl.ds(place * shard, shard), :]),
                (gain_conv_h, gain_conv),
                (lat_taps_h, lat_taps),
                (lon_half_h, lon_half),
                (lat_half_h, lat_half),
                (quad_off_h, quad_off),
                (w_qkv_h.at[pl.ds((1 - y) * hs, hs), :], w_qkv.at[pl.ds((1 - y) * hs, hs), :]),
            )
        )
    ]
    loads[0].start()
    loads[1].start()
    loads[11].start()
    for copy in loads[2:11]:
        copy.start()

    def columns(pick, h):
        return jnp.concatenate(
            [
                w_qkv[pl.ds(h * hs, hs), j * width + pick * part : j * width + (pick + 1) * part]
                for j in range(3)
            ],
            axis=1,
        )

    def spread(h):
        for pick in range(4):
            @pl.when(quad == pick)
            def _(pick=pick):
                ws[pl.ds(h * hs, hs), :] = columns((pick + 2) % 4, h)
                wq[pl.ds(place * shard + h * hs, hs), :] = columns(pick, h)

    loads[0].wait()
    spread(y)
    pl.semaphore_wait(
        barrier,
        4 + 4 * has_up.astype(jnp.int32) + 4 * has_down.astype(jnp.int32) + 2 * (z >= leap).astype(jnp.int32),
    )

    def remote(source, target, send, recv, device):
        return pltpu.make_async_remote_copy(
            src_ref=source, dst_ref=target, send_sem=send, recv_sem=recv,
            device_id=device, device_id_type=MESH,
        )

    start = lambda d: d.start()
    finish = lambda d: d.wait_send()

    def q_at(slot, h):
        return wq.at[pl.ds(slot * shard + h * hs, hs), :]

    def o_at(slot, h, cc):
        return wo.at[pl.ds(slot * shard + h * hs, hs), pl.ds(cc * half, half)]

    def q_cross(k):
        h = y if k == 0 else 1 - y
        return remote(ws.at[pl.ds(h * hs, hs), :], q_at(place, h), xq_send.at[k], xq_recv.at[k], x_peer)

    def q_crossed(k):
        h = y if k == 0 else 1 - y
        return remote(ws.at[pl.ds(h * hs, hs), :], q_at(x_place, h), xq_send.at[k], xq_recv.at[k], x_peer)

    def q_direct(zz, other):
        xx = (1 - x) if other else x
        source = ws.at[pl.ds(y * hs, hs), :] if other else q_at(place, y)
        return remote(
            source, q_at(place, y), dq_send.at[zz * nx + xx], zq_recv.at[place],
            (y, zz * nx + xx, c),
        )

    def q_along(slot, device):
        return remote(q_at(slot, y), q_at(slot, y), zq_send.at[slot], zq_recv.at[slot], device)

    def q_over(slot, h):
        return remote(q_at(slot, h), q_at(slot, h), yq_send.at[slot], yq_recv.at[slot], y_peer)

    def o_cross(slot, k):
        h = y if k == 0 else 1 - y
        return remote(o_at(slot, h, c), o_at(slot, h, c), xo_send.at[k], xo_recv.at[k], x_peer)

    def o_direct(zz, other):
        xx = (1 - x) if other else x
        return remote(
            o_at(place, y, c), o_at(place, y, c), do_send.at[zz * nx + xx], zo_recv.at[place],
            (y, zz * nx + xx, c),
        )

    def o_along(slot, device):
        return remote(o_at(slot, y, c), o_at(slot, y, c), zo_send.at[slot], zo_recv.at[slot], device)

    def o_over(slot, h):
        return remote(o_at(slot, h, c), o_at(slot, h, c), yo_send.at[slot], yo_recv.at[slot], y_peer)

    def o_side(slot, h, cc):
        return remote(
            o_at(slot, h, cc), o_at(slot, h, cc), so_send.at[slot, h], so_recv.at[slot, h], sibling
        )

    def deal(direct, act):
        for cond, zz in aims:
            def both(zz=zz):
                act(direct(zz, True))
                act(direct(zz, False))

            when(cond, both)

    far = []
    for t in range(1, nz):
        for sign, reach, going, device in (
            (-1, z >= t, has_up, z_up),
            (1, z + t <= nz - 1, has_down if 1 <= t < leap - 1 else None, z_down),
        ):
            for xx in (x, 1 - x):
                far.append(
                    (
                        t * sign, reach, (z + sign * t) * nx + xx,
                        None if going is None else jnp.logical_and(reach, going), device,
                    )
                )

    def q_step(t, act):
        for tt, reach, slot, going, device in far:
            if tt == t:
                if act is start:
                    when(reach, lambda slot=slot: q_along(slot, z_up).wait_recv())
                if going is not None:
                    when(going, lambda slot=slot, device=device: act(q_along(slot, device)))
                when(reach, lambda slot=slot: act(q_over(slot, y)))

    def o_step(t, act):
        for tt, reach, slot, going, device in far:
            if tt == t:
                if act is start:
                    when(reach, lambda slot=slot: o_along(slot, z_up).wait_recv())
                if going is not None:
                    when(going, lambda slot=slot, device=device: act(o_along(slot, device)))
                when(reach, lambda slot=slot: act(o_over(slot, y)))
                when(reach, lambda slot=slot: act(o_side(slot, y, c)))

    def o_gather(act, ts=range(1, nz)):
        for t, reach, slot, _, _ in far:
            if abs(t) not in ts:
                continue
            if act is start:
                when(reach, lambda slot=slot: o_over(slot, 1 - y).wait_recv())
            when(reach, lambda slot=slot: act(o_side(slot, 1 - y, c)))

    def o_near(act):
        for k, h in ((0, y), (1, 1 - y)):
            if act is start:
                o_cross(x_place, k).wait_recv()
            act(o_side(x_place, h, c))

    def tok_at(b, cc):
        return tok.at[b, pl.ds(cc * rows, rows), :]

    tok_copies = [
        remote(tok_at(x, c), tok_at(x, c), t_send.at[0], t_recv.at[0], x_peer),
        remote(tok_at(x, c), tok_at(x, c), t_send.at[1], t_recv.at[1], sibling),
        remote(tok_at(1 - x, c), tok_at(1 - x, c), t_send.at[2], t_recv.at[2], sibling),
    ]
    bias_copies = [
        remote(bias.at[x, c], bias.at[x, c], b_send.at[k], b_recv.at[k], device)
        for k, device in enumerate((x_peer, sibling, x_diag))
    ]

    deal(q_direct, start)
    loads[1].wait()
    tok_copies[0].start()
    tok_copies[1].start()
    loads[11].wait()
    spread(1 - y)
    q_cross(0).start()
    q_cross(1).start()
    loads[4].wait()
    for copy in bias_copies:
        copy.start()
    loads[2].wait()
    gain_a = gain_attn[...][None]

    def norm_block(b, cc):
        normed[b, pl.ds(cc * rows, rows), :] = norm_rows(tok[b, pl.ds(cc * rows, rows), :], gain_a)

    norm_block(x, c)
    tok_copies[1].wait_recv()
    norm_block(x, 1 - c)
    q_step(-1, start)
    q_step(1, start)
    q_step(3, start)
    loads[5].wait()
    deal(o_direct, start)
    o_cross(place, 0).start()
    o_cross(place, 1).start()
    q_step(2, start)
    q_step(-2, start)
    q_step(-3, start)
    tok_copies[0].wait_recv()
    tok_copies[2].start()
    norm_block(1 - x, c)
    o_step(1, start)
    tok_copies[2].wait_recv()
    norm_block(1 - x, 1 - c)

    loads[3].wait()
    pair_row = lax.broadcasted_iota(jnp.int32, (2 * head, half), 0)
    pair_col = lax.broadcasted_iota(jnp.int32, (2 * head, half), 1)
    same = lax.rem(lax.div(pair_col, head), 2) == lax.div(pair_row, head)
    for b in range(2):
        wide = jnp.concatenate([w_conv[b], w_conv[b]], axis=0).astype(F32)
        mixer[b] = jnp.where(same, wide, 0.0).astype(BF)
    for copy in bias_copies:
        copy.wait_recv()
    for b in range(2):
        bias_f[b] = jnp.concatenate([bias[b, 0], bias[b, 1]], axis=1).astype(F32)
    for k in range(6, 11):
        loads[k].wait()

    o_step(-1, start)
    o_step(3, start)
    span = (lon_half[0] + 1).astype(F32)
    limit = lon_half[0].astype(F32)
    lons = 2 * rows
    diff = lax.broadcasted_iota(jnp.int32, (lons, lons), 1) - lax.broadcasted_iota(
        jnp.int32, (lons, lons), 0
    )
    offset = jnp.where(diff >= rows, diff - lons, jnp.where(diff < -rows, diff + lons, diff))
    offset = offset.astype(F32)
    distance = jnp.abs(offset)
    tent = jnp.where(distance <= limit, (1.0 - distance / span) / span, 0.0)
    coeff[:, :lons] = tent.astype(BF)
    coeff[:, lons:] = (tent * offset / span).astype(BF)

    q_crossed(0).wait_recv()
    q_crossed(1).wait_recv()
    for _, reach, slot, _, _ in far:
        when(reach, lambda slot=slot: q_over(slot, 1 - y).wait_recv())

    def att_copies(b, n):
        return [
            remote(
                att_out.at[b, pl.ds(cc * rows, rows), :], att_in.at[b, quad],
                a_send.at[n, k], a_recv.at[b, quad], device,
            )
            for k, (cc, device) in enumerate(((c, x_peer), (1 - c, x_diag), (1 - c, sibling)))
        ]

    def attend(b, between):
        projected = jnp.dot(normed[b], wq[...], preferred_element_type=F32).astype(BF)
        between()
        pieces = []
        for h in range(3):
            queries = projected[:, h * head : (h + 1) * head] * jnp.asarray(head ** -0.5, BF)
            keys = projected[:, part + h * head : part + (h + 1) * head]
            vals = projected[:, 2 * part + h * head : 2 * part + (h + 1) * head]
            scores = lax.dot_general(
                queries, keys, (((1,), (1,)), ((), ())), preferred_element_type=F32
            ) + bias_f[b, pl.ds(quad * 3 + h, 1), :]
            expd = jnp.exp(scores - jnp.max(scores, axis=-1, keepdims=True))
            totals = jnp.sum(expd, axis=-1, keepdims=True)
            pieces.append(jnp.dot(expd.astype(BF), vals, preferred_element_type=F32) / totals)
        att_out[b] = jnp.concatenate(pieces, axis=1).astype(BF)

    attend(x, lambda: None)
    for copy in att_copies(x, 0):
        copy.start()
    att_in[x, quad] = att_out[x, pl.ds(c * rows, rows), :]
    o_near(start)
    o_step(-2, start)
    o_step(2, start)
    attend(1 - x, lambda: None)
    for copy in att_copies(1 - x, 1):
        copy.start()
    att_in[1 - x, quad] = att_out[1 - x, pl.ds(c * rows, rows), :]
    o_step(-3, start)
    o_gather(start)

    for _, reach, slot, _, _ in far:
        def landed(slot=slot):
            o_side(slot, 0, 1 - c).wait_recv()
            o_side(slot, 1, 1 - c).wait_recv()

        when(reach, landed)
    o_side(x_place, 0, 1 - c).wait_recv()
    o_side(x_place, 1, 1 - c).wait_recv()

    near, away = 2 * (1 - x), 2 * x
    passes = jnp.logical_or(jnp.logical_and(x == 0, has_up), jnp.logical_and(x == 1, has_down))
    gets = jnp.logical_or(jnp.logical_and(x == 0, has_down), jnp.logical_and(x == 1, has_up))
    onward = place + nx * (1 - 2 * x)
    split = rows // 2
    passes_own = jnp.logical_or(jnp.logical_and(x == 1, has_up), jnp.logical_and(x == 0, has_down))
    back = (z - 1 + 2 * x) * nx + 1 - x

    def band(b):
        for source in (x * 2 + 1 - c, (1 - x) * 2 + c, (1 - x) * 2 + 1 - c):
            remote(att_in.at[b, source], att_in.at[b, source], a_send.at[0, 0], a_recv.at[b, source], sibling).wait_recv()
        branch = tok[b, pl.ds(c * rows, rows), :].astype(F32)
        for p in range(4):
            branch = branch + jnp.dot(
                att_in[b, p], wo[p * part : (p + 1) * part, :], preferred_element_type=F32
            )
        return branch.astype(BF)

    gain_c = gain_conv[...][None]
    own_rows = pl.ds(c * rows, rows)
    side_rows = pl.ds((1 - c) * rows, rows)
    own_cols = pl.ds(c * half, half)
    side_cols = pl.ds((1 - c) * half, half)

    def conv_copy(source, which, cc, k, device):
        return remote(
            source, normed_conv.at[which, pl.ds(cc * rows, rows), :],
            c_send.at[k], c_recv.at[which, cc], device,
        )

    stage[0] = norm_rows(band(1 - x), gain_c)
    def far_copy(which, first, cc, cols, k, device):
        start_row = 0 if first else split
        target = 2 * x if first else 2 * (1 - x)
        return remote(
            stage.at[which, pl.ds(start_row, split), cols],
            normed_conv.at[target, pl.ds(cc * rows + start_row, split), :],
            f_send.at[k], f_recv.at[cc, 0 if first else 1], device,
        )

    to_far = [
        far_copy(0, True, c, own_cols, 0, (y, onward, c)),
        far_copy(0, True, c, side_cols, 1, (y, onward, 1 - c)),
    ]
    to_back = [
        far_copy(1, False, c, own_cols, 2, (y, back, c)),
        far_copy(1, False, c, side_cols, 3, (y, back, 1 - c)),
    ]

    @pl.when(passes)
    def _():
        for d in to_far:
            d.start()

    to_side = [conv_copy(stage.at[0, :, side_cols], near, c, 2, sibling)]
    to_side[0].start()
    normed_conv[near, own_rows, :] = stage[0, :, own_cols]

    mid = band(x)
    middle[...] = mid
    stage[1] = norm_rows(mid, gain_c)
    @pl.when(passes_own)
    def _():
        for d in to_back:
            d.start()

    to_side.append(conv_copy(stage.at[1, :, side_cols], 1, c, 3, sibling))
    to_side[1].start()
    to_mid = remote(middle.at[:, side_cols], mid_rows.at[own_rows, :], h_send.at[0], h_recv.at[0], sibling)
    to_mid.start()
    normed_conv[1, own_rows, :] = stage[1, :, own_cols]
    mid_rows[own_rows, :] = middle[:, own_cols]

    @pl.when(jnp.logical_not(gets))
    def _():
        normed_conv[away] = jnp.zeros((lons, half), BF)

    base = quad_off[0]
    wide_ok = lat_half[0] >= 1
    taps = [
        [
            lat_taps[b, base + r] if r == 1 else jnp.where(wide_ok, lat_taps[b, base + r], 0.0)
            for b in range(2)
        ]
        for r in range(3)
    ]

    def mix(values, b):
        return jnp.concatenate(
            [
                lax.dot_general(
                    values[:, p * 2 * head : (p + 1) * 2 * head],
                    mixer[b, :, p * 2 * head : (p + 1) * 2 * head],
                    (((1,), (1,)), ((), ())),
                    preferred_element_type=F32,
                )
                for p in range(half // (2 * head))
            ],
            axis=1,
        ).astype(BF)

    conv_copy(stage.at[1, :, side_cols], 1, 1 - c, 3, sibling).wait_recv()
    for b in range(2):
        gain = jnp.where(place == 0, taps[0][b], 0.0) + jnp.where(place == last_place, taps[2][b], 0.0)
        pole = mix((gain * normed_conv[1].astype(F32)).astype(BF), b)
        polar[b, :rows] = pole[rows:]
        polar[b, rows:] = pole[:rows]
    conv_copy(stage.at[0, :, side_cols], near, 1 - c, 2, sibling).wait_recv()
    remote(middle.at[:, side_cols], mid_rows.at[side_rows, :], h_send.at[0], h_recv.at[0], sibling).wait_recv()

    q_cross(0).wait_send()
    q_cross(1).wait_send()
    o_cross(place, 0).wait_send()
    o_cross(place, 1).wait_send()
    deal(q_direct, finish)
    deal(o_direct, finish)
    o_near(finish)
    for t in range(1, nz):
        for signed in (t, -t):
            q_step(signed, finish)
            o_step(signed, finish)
    o_gather(finish)
    for d in tok_copies + bias_copies + att_copies(x, 0) + att_copies(1 - x, 1) + to_side + [to_mid]:
        d.wait_send()

    @pl.when(gets)
    def _():
        for cc in range(2):
            for part in range(2):
                target = normed_conv.at[away, pl.ds(cc * rows + part * split, split), :]
                remote(target, target, f_send.at[0], f_recv.at[cc, part], sibling).wait_recv()

    for b in range(2):
        summed = (
            taps[0][b] * normed_conv[0].astype(F32)
            + taps[1][b] * normed_conv[1].astype(F32)
            + taps[2][b] * normed_conv[2].astype(F32)
        ).astype(BF)
        mixed[b * lons : (b + 1) * lons, :] = (
            mix(summed, b).astype(F32) + polar[b].astype(F32)
        ).astype(BF)

    def convolve(at):
        return (
            mid_rows[at, :].astype(F32)
            + jnp.dot(coeff[at, :], mixed[...], preferred_element_type=F32)
        ).astype(BF)

    done_out[...] = convolve(side_rows)
    to_done = remote(done_out, done_in, h_send.at[1], h_recv.at[1], sibling)
    to_done.start()
    out[:, own_cols] = convolve(own_rows)

    @pl.when(passes_own)
    def _():
        for d in to_back:
            d.wait_send()

    @pl.when(passes)
    def _():
        for d in to_far:
            d.wait_send()

    to_done.wait_recv()
    out[:, side_cols] = done_in[...]
    to_done.wait_send()


def in_hbm(value):
    return pltpu.with_memory_space_constraint(value, pltpu.HBM)


def fused_device(
    tokens, gain_attn, w_qkv, key_bias, w_out, gain_conv, w_conv, lat_taps, lon_half, lat_half, quad_off
):
    rows, width = tokens.shape[1:]
    shard = w_qkv.shape[0]
    heads = key_bias.shape[1]
    lat_count = width // shard
    nx = 2
    nz = lat_count // nx
    part, half, lons = width // 4, width // 2, 2 * rows
    vmem = pl.BlockSpec(memory_space=pltpu.VMEM)
    anywhere = pl.BlockSpec(memory_space=pltpu.HBM)
    dma = pltpu.SemaphoreType.DMA
    out = pl.pallas_call(
        lambda *refs: fused_kernel(nx, nz, *refs),
        out_shape=pltpu.VMEM((rows, width), BF),
        in_specs=[anywhere] * 11,
        out_specs=vmem,
        scratch_shapes=[
            pltpu.SMEM((2, lat_taps.shape[0]), F32),
            pltpu.SMEM((1,), jnp.int32),
            pltpu.SMEM((1,), jnp.int32),
            pltpu.SMEM((1,), jnp.int32),
            pltpu.VMEM((width,), F32),
            pltpu.VMEM(w_qkv.shape, BF),
            pltpu.VMEM((width,), F32),
            pltpu.VMEM((2, 64, half), BF),
            dma((12,)),
            pltpu.VMEM((shard, 3 * part), BF),
            pltpu.VMEM((width, 3 * part), BF),
            pltpu.VMEM((width, width), BF),
            pltpu.VMEM((2, lons, width), BF),
            pltpu.VMEM((2, lons, width), BF),
            pltpu.VMEM((2, 2, heads, rows), BF),
            pltpu.VMEM((2, heads, lons), F32),
            pltpu.VMEM((2, lons, part), BF),
            pltpu.VMEM((2, 4, rows, part), BF),
            pltpu.VMEM((2, rows, width), BF),
            pltpu.VMEM((3, lons, half), BF),
            pltpu.VMEM((rows, width), BF),
            pltpu.VMEM((lons, half), BF),
            pltpu.VMEM((2, 128, half), BF),
            pltpu.VMEM((2, lons, half), BF),
            pltpu.VMEM((2 * lons, half), BF),
            pltpu.VMEM((lons, 2 * lons), BF),
            pltpu.VMEM((rows, half), BF),
            pltpu.VMEM((rows, half), BF),
            dma((2,)), dma((2,)),
            dma((lat_count,)), dma((lat_count,)), dma((lat_count,)),
            dma((lat_count,)), dma((lat_count,)),
            dma((2,)), dma((2,)),
            dma((lat_count,)), dma((lat_count,)), dma((lat_count,)),
            dma((lat_count,)), dma((lat_count,)),
            dma((lat_count, 2)), dma((lat_count, 2)),
            dma((3,)), dma((3,)),
            dma((3,)), dma((3,)),
            dma((2, 3)), dma((2, 4)),
            dma((4,)), dma((2, 2)),
            dma((4,)), dma((3, 2)),
            dma((2,)), dma((2,)),
        ],
        compiler_params=pltpu.CompilerParams(
            collective_id=0, has_side_effects=True, vmem_limit_bytes=40 * 1024 * 1024
        ),
    )(
        in_hbm(lat_taps.T), lon_half, lat_half, quad_off,
        *[
            in_hbm(v)
            for v in (
                tokens[0], gain_attn, w_qkv, key_bias[0], w_out, gain_conv, jnp.swapaxes(w_conv, 1, 2)
            )
        ],
    )
    return out[None]


def solution(mesh):
    sizes = (mesh.shape["groups"], mesh.shape["lat"], mesh.shape["lon"])
    return jax.shard_map(
        fused_device if sizes == (2, 8, 2) else per_device,
        mesh=mesh,
        in_specs=(
            P(("groups", "lat"), "lon", None),
            P(),
            P("lat", None),
            P("lat", None, "lon"),
            P("lat", None),
            P(),
            P(),
            P(),
            P("lat"),
            P("lat"),
            P("lat"),
        ),
        out_specs=P(("groups", "lat"), "lon", None),
        check_vma=False,
    )
```

```python
import jax
import jax.numpy as jnp
from jax import lax
from jax.experimental import pallas as pl
from jax.experimental.pallas import tpu as pltpu
from jax.sharding import PartitionSpec as P


def padded(cells, sides, width):
    for axis, dim in sides:
        count = lax.axis_size(axis)
        ends = count - 1
        head = lax.slice_in_dim(cells, 0, width, axis=dim)
        tail = lax.slice_in_dim(cells, cells.shape[dim] - width, cells.shape[dim], axis=dim)
        cells = jnp.concatenate(
            [
                lax.ppermute(tail, axis, [(i, (i + 1) % count) for i in range(ends)]),
                cells,
                lax.ppermute(head, axis, [((i + 1) % count, i) for i in range(ends)]),
            ],
            axis=dim,
        )
    return cells


def layer_norm(inputs, gain):
    values = inputs.astype(jnp.float32)
    average = jnp.mean(values, axis=-1, keepdims=True)
    centered = values - average
    variance = jnp.mean(centered * centered, axis=-1, keepdims=True)
    return centered * lax.rsqrt(variance + 1e-05) * gain


def group_mix(inputs, w_conv):
    basis, length, channels = inputs.shape
    group_width = w_conv.shape[2]
    groups = channels // group_width
    mixed_rows = jnp.einsum(
        "kjgc,kgce->kjge",
        inputs.reshape(basis, length, groups, group_width),
        w_conv.reshape(basis, groups, group_width, group_width),
        preferred_element_type=jnp.float32,
    )
    return mixed_rows.reshape(basis, length, channels).astype(jnp.bfloat16)


def lon_weights(row_ids, col_ids, half_width, lon_total):
    offset_lon = (
        jnp.mod(col_ids[None, :] - row_ids[:, None] + lon_total // 2, lon_total) - lon_total // 2
    )
    distance = jnp.abs(offset_lon).astype(jnp.float32)
    span_plus = (half_width + 1).astype(jnp.float32)
    tent_weight = jnp.where(
        distance <= half_width.astype(jnp.float32), (1.0 - distance / span_plus) / span_plus, 0.0
    )
    odd_weight = tent_weight * offset_lon.astype(jnp.float32) / span_plus
    return jnp.stack([tent_weight, odd_weight]).astype(jnp.bfloat16)


def start_state(query_count, head_count, head_dim):
    running_max = jnp.full((head_count, query_count), -jnp.inf, jnp.float32)
    running_sum = jnp.zeros((head_count, query_count), jnp.float32)
    running_out = jnp.zeros((query_count, head_count, head_dim), jnp.float32)
    return (running_max, running_sum, running_out)


def attend_keys(carry_state, queries, key_rows, value_rows, bias_rows, score_scale):
    key_count = key_rows.shape[0]
    for offset in range(0, key_count, 128):
        running_max, running_sum, running_out = carry_state
        key_block = key_rows[offset : offset + 128]
        value_block = value_rows[offset : offset + 128]
        bias_block = bias_rows[offset : offset + 128]
        scores = (
            jnp.einsum("qhd,khd->hqk", queries, key_block, preferred_element_type=jnp.float32)
            * score_scale
        )
        scores = scores + bias_block.T.astype(jnp.float32)[:, None, :]
        new_max = jnp.maximum(running_max, jnp.max(scores, axis=-1))
        rescale = jnp.exp(running_max - new_max)
        exp_scores = jnp.exp(scores - new_max[:, :, None])
        running_sum = running_sum * rescale + jnp.sum(exp_scores, axis=-1)
        running_out = running_out * rescale.T[:, :, None] + jnp.einsum(
            "hqk,khd->qhd",
            exp_scores.astype(jnp.bfloat16),
            value_block,
            preferred_element_type=jnp.float32,
        )
        carry_state = (new_max, running_sum, running_out)
    return carry_state


def finish_state(carry_state):
    running_max, running_sum, running_out = carry_state
    finished = running_out / running_sum.T[:, :, None]
    return finished.reshape(finished.shape[0], -1).astype(jnp.bfloat16)


def lon_conv(blended, half_width, first_col, out_cols):
    lon_total = blended.shape[1]
    block_cols = min(128, lon_total)
    block_count = lon_total // block_cols
    first_block = jnp.floor_divide(first_col - half_width, block_cols)
    last_block = jnp.floor_divide(first_col + out_cols - 1 + half_width, block_cols)
    turn_count = jnp.minimum(block_count, last_block - first_block + 1)
    row_ids = first_col + jnp.arange(out_cols, dtype=jnp.int32)

    def add_block(turn_index, running_out):
        block_at = jnp.mod(first_block + turn_index, block_count)
        lon_block = lax.dynamic_slice_in_dim(blended, block_at * block_cols, block_cols, 1)
        col_ids = block_at * block_cols + jnp.arange(block_cols, dtype=jnp.int32)
        coeffs = lon_weights(row_ids, col_ids, half_width, lon_total)
        return running_out + jnp.einsum(
            "kjc,kcd->jd", coeffs, lon_block, preferred_element_type=jnp.float32
        )

    initial = jnp.zeros((out_cols, blended.shape[2]), jnp.float32)
    return lax.fori_loop(0, turn_count, add_block, initial)


def per_device(
    tokens,
    gain_attn,
    w_qkv,
    key_bias,
    w_out,
    gain_conv,
    w_conv,
    lat_taps,
    lon_half,
    lat_half,
    quad_off,
):
    own_tokens = tokens[0]
    count_lon, model_width = own_tokens.shape
    head_count = key_bias.shape[1]
    head_dim = model_width // head_count
    score_scale = head_dim ** (-0.5)
    lon_place = lax.axis_index("lon")
    normed = layer_norm(own_tokens, gain_attn).astype(jnp.bfloat16)
    bias_rows = key_bias[0].T
    full_qkv, full_out = (
        lax.all_gather(w_qkv, "lat", axis=0, tiled=True),
        lax.all_gather(w_out, "lat", axis=0, tiled=True),
    )
    projected = jnp.dot(normed, full_qkv, preferred_element_type=jnp.float32).astype(jnp.bfloat16)
    queries = projected[:, :model_width].reshape(count_lon, head_count, head_dim)
    key_here = projected[:, model_width : 2 * model_width]
    value_here = projected[:, 2 * model_width :]
    key_piece = lax.all_gather(key_here, "lon", axis=0, tiled=True)
    value_piece = lax.all_gather(value_here, "lon", axis=0, tiled=True)
    bias_piece = lax.all_gather(bias_rows, "lon", axis=0, tiled=True)
    length = key_piece.shape[0]
    carry_state = attend_keys(
        start_state(count_lon, head_count, head_dim),
        queries,
        key_piece.reshape(length, head_count, head_dim),
        value_piece.reshape(length, head_count, head_dim),
        bias_piece,
        score_scale,
    )
    attended = finish_state(carry_state)
    branch_out = jnp.dot(attended, full_out, preferred_element_type=jnp.float32)
    middle = (own_tokens.astype(jnp.float32) + branch_out).astype(jnp.bfloat16)
    conv_in = layer_norm(middle, gain_conv).astype(jnp.bfloat16)
    stacked = padded(conv_in[None], (("lat", 0),), 1)
    lat_row = lax.axis_index("lat")
    last_band = lax.axis_size("lat") - 1
    offsets = jnp.arange(3, dtype=jnp.int32) - 1
    one_hot = (
        (quad_off[0] + offsets + 1)[:, None]
        == jnp.arange(lat_taps.shape[0], dtype=jnp.int32)[None, :]
    ).astype(jnp.float32)
    tap_vals = jnp.dot(one_hot, lat_taps, precision=lax.Precision.HIGHEST)
    tap_vals = jnp.where((jnp.abs(offsets) <= lat_half[0])[:, None], tap_vals, 0.0)
    summed = jnp.einsum(
        "rk,rjd->kjd", tap_vals, stacked.astype(jnp.float32), precision=lax.Precision.HIGHEST
    ).astype(jnp.bfloat16)
    pole_gain = jnp.where(lat_row == 0, tap_vals[0], 0.0) + jnp.where(
        lat_row == last_band, tap_vals[2], 0.0
    )
    first_col = lon_place * count_lon
    pole_rows = (pole_gain[:, None, None] * conv_in.astype(jnp.float32)[None]).astype(jnp.bfloat16)
    mixed_rows = group_mix(summed, w_conv)
    pole_mixed = group_mix(pole_rows, w_conv)
    circle_rows, pole_all = (
        lax.all_gather(mixed_rows, "lon", axis=1, tiled=True),
        lax.all_gather(pole_mixed, "lon", axis=1, tiled=True),
    )
    lon_total = circle_rows.shape[1]
    blended = (
        circle_rows.astype(jnp.float32)
        + jnp.roll(pole_all, -(lon_total // 2), axis=1).astype(jnp.float32)
    ).astype(jnp.bfloat16)
    conv_out = lon_conv(blended, lon_half[0], first_col, count_lon)
    return (middle.astype(jnp.float32) + conv_out).astype(jnp.bfloat16)[None]


BF = jnp.bfloat16
F32 = jnp.float32
MESH = pl.DeviceIdType.MESH


def norm_rows(values, gain):
    values = values.astype(F32)
    average = jnp.mean(values, axis=-1, keepdims=True)
    centered = values - average
    variance = jnp.mean(centered * centered, axis=-1, keepdims=True)
    return (centered * lax.rsqrt(variance + 1e-05) * gain).astype(BF)


def fused_kernel(
    nx, nz,
    lat_taps_h, lon_half_h, lat_half_h, quad_off_h,
    tokens_h, gain_attn_h, w_qkv_h, key_bias_h, w_out_h, gain_conv_h, w_conv_h,
    out,
    lat_taps, lon_half, lat_half, quad_off, gain_attn, w_qkv, gain_conv, w_conv, load,
    ws, wq, wo, tok, normed, bias, bias_f, att_out, att_in, stage, normed_conv, middle, mid_rows,
    mixer, polar, mixed, coeff, done_out, done_in,
    xq_send, xq_recv, dq_send, zq_send, zq_recv, yq_send, yq_recv,
    xo_send, xo_recv, do_send, zo_send, zo_recv, yo_send, yo_recv, so_send, so_recv,
    t_send, t_recv, b_send, b_recv, a_send, a_recv,
    f_send, f_recv, c_send, c_recv, h_send, h_recv,
):
    y, place, c = lax.axis_index("groups"), lax.axis_index("lat"), lax.axis_index("lon")
    z, x = lax.div(place, nx), lax.rem(place, nx)
    quad = x * 2 + c
    x_place = z * nx + (1 - x)
    x_peer, x_diag = (y, x_place, c), (y, x_place, 1 - c)
    sibling = (y, place, 1 - c)
    y_peer = (1 - y, place, c)
    z_up, z_down = (y, place + nx, c), (y, place - nx, c)
    has_up, has_down = z < nz - 1, z > 0
    last_place = nx * nz - 1
    shard = w_qkv.shape[0]
    hs = shard // 2
    width = tokens_h.shape[1]
    rows = tokens_h.shape[0]
    head = 64
    part = width // 4
    half = width // 2

    barrier = pltpu.get_barrier_semaphore()

    def greet(device):
        pl.semaphore_signal(barrier, inc=1, device_id=device, device_id_type=MESH)

    def when(cond, run):
        if cond is None:
            run()
        else:
            pl.when(cond)(run)

    for device in (x_peer, x_diag, sibling, y_peer):
        greet(device)
    leap = nz - 1
    aims = [(has_down, z - 1), (z >= leap, z - leap), (has_up, z + 1)]
    for cond, zz in ((has_up, z + 1), (has_down, z - 1), (z < nz - leap, z + leap)):
        def both(zz=zz):
            greet((y, zz * nx, c))
            greet((y, zz * nx + 1, c))

        when(cond, both)
    for cond, zz in ((has_up, z + 1), (has_down, z - 1)):
        def others(zz=zz):
            greet((y, zz * nx, 1 - c))
            greet((y, zz * nx + 1, 1 - c))

        when(cond, others)

    loads = [
        pltpu.make_async_copy(source, target, load.at[k])
        for k, (source, target) in enumerate(
            (
                (w_qkv_h.at[pl.ds(y * hs, hs), :], w_qkv.at[pl.ds(y * hs, hs), :]),
                (tokens_h, tok.at[x, pl.ds(c * rows, rows), :]),
                (gain_attn_h, gain_attn),
                (w_conv_h.at[:, :, pl.ds(c * half, half)], w_conv),
                (key_bias_h, bias.at[x, c]),
                (w_out_h, wo.at[pl.ds(place * shard, shard), :]),
                (gain_conv_h, gain_conv),
                (lat_taps_h, lat_taps),
                (lon_half_h, lon_half),
                (lat_half_h, lat_half),
                (quad_off_h, quad_off),
                (w_qkv_h.at[pl.ds((1 - y) * hs, hs), :], w_qkv.at[pl.ds((1 - y) * hs, hs), :]),
            )
        )
    ]
    loads[0].start()
    loads[1].start()
    loads[11].start()
    for copy in loads[2:11]:
        copy.start()

    def columns(pick, h):
        return jnp.concatenate(
            [
                w_qkv[pl.ds(h * hs, hs), j * width + pick * part : j * width + (pick + 1) * part]
                for j in range(3)
            ],
            axis=1,
        )

    def spread(h):
        for pick in range(4):
            @pl.when(quad == pick)
            def _(pick=pick):
                ws[pl.ds(h * hs, hs), :] = columns((pick + 2) % 4, h)
                wq[pl.ds(place * shard + h * hs, hs), :] = columns(pick, h)

    loads[0].wait()
    spread(y)
    pl.semaphore_wait(
        barrier,
        4 + 4 * has_up.astype(jnp.int32) + 4 * has_down.astype(jnp.int32) + 2 * (z >= leap).astype(jnp.int32),
    )

    def remote(source, target, send, recv, device):
        return pltpu.make_async_remote_copy(
            src_ref=source, dst_ref=target, send_sem=send, recv_sem=recv,
            device_id=device, device_id_type=MESH,
        )

    start = lambda d: d.start()
    finish = lambda d: d.wait_send()

    def q_at(slot, h):
        return wq.at[pl.ds(slot * shard + h * hs, hs), :]

    def o_at(slot, h, cc):
        return wo.at[pl.ds(slot * shard + h * hs, hs), pl.ds(cc * half, half)]

    def q_cross(k):
        h = y if k == 0 else 1 - y
        return remote(ws.at[pl.ds(h * hs, hs), :], q_at(place, h), xq_send.at[k], xq_recv.at[k], x_peer)

    def q_crossed(k):
        h = y if k == 0 else 1 - y
        return remote(ws.at[pl.ds(h * hs, hs), :], q_at(x_place, h), xq_send.at[k], xq_recv.at[k], x_peer)

    def q_direct(zz, other):
        xx = (1 - x) if other else x
        source = ws.at[pl.ds(y * hs, hs), :] if other else q_at(place, y)
        return remote(
            source, q_at(place, y), dq_send.at[zz * nx + xx], zq_recv.at[place],
            (y, zz * nx + xx, c),
        )

    def q_along(slot, device):
        return remote(q_at(slot, y), q_at(slot, y), zq_send.at[slot], zq_recv.at[slot], device)

    def q_over(slot, h):
        return remote(q_at(slot, h), q_at(slot, h), yq_send.at[slot], yq_recv.at[slot], y_peer)

    def o_cross(slot, k):
        h = y if k == 0 else 1 - y
        return remote(o_at(slot, h, c), o_at(slot, h, c), xo_send.at[k], xo_recv.at[k], x_peer)

    def o_direct(zz, other):
        xx = (1 - x) if other else x
        return remote(
            o_at(place, y, c), o_at(place, y, c), do_send.at[zz * nx + xx], zo_recv.at[place],
            (y, zz * nx + xx, c),
        )

    def o_along(slot, device):
        return remote(o_at(slot, y, c), o_at(slot, y, c), zo_send.at[slot], zo_recv.at[slot], device)

    def o_over(slot, h):
        return remote(o_at(slot, h, c), o_at(slot, h, c), yo_send.at[slot], yo_recv.at[slot], y_peer)

    def o_side(slot, h, cc):
        return remote(
            o_at(slot, h, cc), o_at(slot, h, cc), so_send.at[slot, h], so_recv.at[slot, h], sibling
        )

    def deal(direct, act):
        for cond, zz in aims if direct is q_direct else aims[::-1]:
            def both(zz=zz):
                act(direct(zz, True))
                act(direct(zz, False))

            when(cond, both)

    far = []
    for t in range(1, nz):
        for sign, reach, going, device in (
            (-1, z >= t, has_up, z_up),
            (1, z + t <= nz - 1, has_down if 1 <= t < leap - 1 else None, z_down),
        ):
            for xx in (x, 1 - x):
                far.append(
                    (
                        t * sign, reach, (z + sign * t) * nx + xx,
                        None if going is None else jnp.logical_and(reach, going), device,
                    )
                )

    def q_step(t, act):
        for tt, reach, slot, going, device in far:
            if tt == t:
                if act is start:
                    when(reach, lambda slot=slot: q_along(slot, z_up).wait_recv())
                if going is not None:
                    when(going, lambda slot=slot, device=device: act(q_along(slot, device)))
                when(reach, lambda slot=slot: act(q_over(slot, y)))

    def o_step(t, act):
        for tt, reach, slot, going, device in far:
            if tt == t:
                if act is start:
                    when(reach, lambda slot=slot: o_along(slot, z_up).wait_recv())
                if going is not None:
                    when(going, lambda slot=slot, device=device: act(o_along(slot, device)))
                when(reach, lambda slot=slot: act(o_over(slot, y)))
                when(reach, lambda slot=slot: act(o_side(slot, y, c)))

    def o_gather(act, ts=range(1, nz)):
        for t, reach, slot, _, _ in far:
            if abs(t) not in ts:
                continue
            if act is start:
                when(reach, lambda slot=slot: o_over(slot, 1 - y).wait_recv())
            when(reach, lambda slot=slot: act(o_side(slot, 1 - y, c)))

    def o_near(act):
        for k, h in ((0, y), (1, 1 - y)):
            if act is start:
                o_cross(x_place, k).wait_recv()
            act(o_side(x_place, h, c))

    def tok_at(b, cc):
        return tok.at[b, pl.ds(cc * rows, rows), :]

    tok_copies = [
        remote(tok_at(x, c), tok_at(x, c), t_send.at[0], t_recv.at[0], x_peer),
        remote(tok_at(x, c), tok_at(x, c), t_send.at[1], t_recv.at[1], sibling),
        remote(tok_at(1 - x, c), tok_at(1 - x, c), t_send.at[2], t_recv.at[2], sibling),
    ]
    bias_copies = [
        remote(bias.at[x, c], bias.at[x, c], b_send.at[k], b_recv.at[k], device)
        for k, device in enumerate((x_peer, sibling, x_diag))
    ]

    deal(q_direct, start)
    loads[1].wait()
    tok_copies[0].start()
    tok_copies[1].start()
    loads[11].wait()
    spread(1 - y)
    q_cross(0).start()
    q_cross(1).start()
    loads[4].wait()
    for copy in bias_copies:
        copy.start()
    loads[2].wait()
    gain_a = gain_attn[...][None]

    def norm_block(b, cc):
        normed[b, pl.ds(cc * rows, rows), :] = norm_rows(tok[b, pl.ds(cc * rows, rows), :], gain_a)

    norm_block(x, c)
    tok_copies[1].wait_recv()
    norm_block(x, 1 - c)
    q_step(-1, start)
    q_step(1, start)
    q_step(3, start)
    loads[5].wait()
    deal(o_direct, start)
    o_cross(place, 0).start()
    o_cross(place, 1).start()
    q_step(2, start)
    q_step(-2, start)
    q_step(-3, start)
    tok_copies[0].wait_recv()
    tok_copies[2].start()
    norm_block(1 - x, c)
    tok_copies[2].wait_recv()
    norm_block(1 - x, 1 - c)

    loads[3].wait()
    pair_row = lax.broadcasted_iota(jnp.int32, (2 * head, half), 0)
    pair_col = lax.broadcasted_iota(jnp.int32, (2 * head, half), 1)
    same = lax.rem(lax.div(pair_col, head), 2) == lax.div(pair_row, head)
    for b in range(2):
        wide = jnp.concatenate([w_conv[b], w_conv[b]], axis=0).astype(F32)
        mixer[b] = jnp.where(same, wide, 0.0).astype(BF)
    for copy in bias_copies:
        copy.wait_recv()
    for b in range(2):
        bias_f[b] = jnp.concatenate([bias[b, 0], bias[b, 1]], axis=1).astype(F32)
    for k in range(6, 11):
        loads[k].wait()

    o_step(1, start)
    o_step(-1, start)
    o_step(3, start)
    span = (lon_half[0] + 1).astype(F32)
    limit = lon_half[0].astype(F32)
    lons = 2 * rows
    diff = lax.broadcasted_iota(jnp.int32, (lons, lons), 1) - lax.broadcasted_iota(
        jnp.int32, (lons, lons), 0
    )
    offset = jnp.where(diff >= rows, diff - lons, jnp.where(diff < -rows, diff + lons, diff))
    offset = offset.astype(F32)
    distance = jnp.abs(offset)
    tent = jnp.where(distance <= limit, (1.0 - distance / span) / span, 0.0)
    coeff[:, :lons] = tent.astype(BF)
    coeff[:, lons:] = (tent * offset / span).astype(BF)

    q_crossed(0).wait_recv()
    q_crossed(1).wait_recv()
    for _, reach, slot, _, _ in far:
        when(reach, lambda slot=slot: q_over(slot, 1 - y).wait_recv())

    def att_copies(b, n):
        return [
            remote(
                att_out.at[b, pl.ds(cc * rows, rows), :], att_in.at[b, quad],
                a_send.at[n, k], a_recv.at[b, quad], device,
            )
            for k, (cc, device) in enumerate(((c, x_peer), (1 - c, x_diag), (1 - c, sibling)))
        ]

    def attend(b, between):
        projected = jnp.dot(normed[b], wq[...], preferred_element_type=F32).astype(BF)
        between()
        pieces = []
        for h in range(3):
            queries = projected[:, h * head : (h + 1) * head] * jnp.asarray(head ** -0.5, BF)
            keys = projected[:, part + h * head : part + (h + 1) * head]
            vals = projected[:, 2 * part + h * head : 2 * part + (h + 1) * head]
            scores = lax.dot_general(
                queries, keys, (((1,), (1,)), ((), ())), preferred_element_type=F32
            ) + bias_f[b, pl.ds(quad * 3 + h, 1), :]
            expd = jnp.exp(scores - jnp.max(scores, axis=-1, keepdims=True))
            totals = jnp.sum(expd, axis=-1, keepdims=True)
            pieces.append(jnp.dot(expd.astype(BF), vals, preferred_element_type=F32) / totals)
        att_out[b] = jnp.concatenate(pieces, axis=1).astype(BF)

    o_near(start)
    attend(x, lambda: None)
    for copy in att_copies(x, 0):
        copy.start()
    att_in[x, quad] = att_out[x, pl.ds(c * rows, rows), :]
    o_step(-2, start)
    o_step(2, start)
    attend(1 - x, lambda: None)
    for copy in att_copies(1 - x, 1):
        copy.start()
    att_in[1 - x, quad] = att_out[1 - x, pl.ds(c * rows, rows), :]
    o_step(-3, start)
    o_gather(start)

    for _, reach, slot, _, _ in far:
        def landed(slot=slot):
            o_side(slot, 0, 1 - c).wait_recv()
            o_side(slot, 1, 1 - c).wait_recv()

        when(reach, landed)
    o_side(x_place, 0, 1 - c).wait_recv()
    o_side(x_place, 1, 1 - c).wait_recv()

    near, away = 2 * (1 - x), 2 * x
    passes = jnp.logical_or(jnp.logical_and(x == 0, has_up), jnp.logical_and(x == 1, has_down))
    gets = jnp.logical_or(jnp.logical_and(x == 0, has_down), jnp.logical_and(x == 1, has_up))
    onward = place + nx * (1 - 2 * x)
    split = rows // 2
    passes_own = jnp.logical_or(jnp.logical_and(x == 1, has_up), jnp.logical_and(x == 0, has_down))
    back = (z - 1 + 2 * x) * nx + 1 - x

    def band(b):
        for source in (x * 2 + 1 - c, (1 - x) * 2 + c, (1 - x) * 2 + 1 - c):
            remote(att_in.at[b, source], att_in.at[b, source], a_send.at[0, 0], a_recv.at[b, source], sibling).wait_recv()
        branch = tok[b, pl.ds(c * rows, rows), :].astype(F32)
        for p in range(4):
            branch = branch + jnp.dot(
                att_in[b, p], wo[p * part : (p + 1) * part, :], preferred_element_type=F32
            )
        return branch.astype(BF)

    gain_c = gain_conv[...][None]
    own_rows = pl.ds(c * rows, rows)
    side_rows = pl.ds((1 - c) * rows, rows)
    own_cols = pl.ds(c * half, half)
    side_cols = pl.ds((1 - c) * half, half)

    def conv_copy(source, which, cc, k, device):
        return remote(
            source, normed_conv.at[which, pl.ds(cc * rows, rows), :],
            c_send.at[k], c_recv.at[which, cc], device,
        )

    stage[0] = norm_rows(band(1 - x), gain_c)
    def far_copy(which, first, cc, cols, k, device):
        start_row = 0 if first else split
        target = 2 * x if first else 2 * (1 - x)
        return remote(
            stage.at[which, pl.ds(start_row, split), cols],
            normed_conv.at[target, pl.ds(cc * rows + start_row, split), :],
            f_send.at[k], f_recv.at[cc, 0 if first else 1], device,
        )

    to_far = [
        far_copy(0, True, c, own_cols, 0, (y, onward, c)),
        far_copy(0, True, c, side_cols, 1, (y, onward, 1 - c)),
    ]
    to_back = [
        far_copy(1, False, c, own_cols, 2, (y, back, c)),
        far_copy(1, False, c, side_cols, 3, (y, back, 1 - c)),
    ]

    @pl.when(passes)
    def _():
        for d in to_far:
            d.start()

    to_side = [conv_copy(stage.at[0, :, side_cols], near, c, 2, sibling)]
    to_side[0].start()
    normed_conv[near, own_rows, :] = stage[0, :, own_cols]

    mid = band(x)
    middle[...] = mid
    stage[1] = norm_rows(mid, gain_c)
    @pl.when(passes_own)
    def _():
        for d in to_back:
            d.start()

    to_side.append(conv_copy(stage.at[1, :, side_cols], 1, c, 3, sibling))
    to_side[1].start()
    to_mid = remote(middle.at[:, side_cols], mid_rows.at[own_rows, :], h_send.at[0], h_recv.at[0], sibling)
    to_mid.start()
    normed_conv[1, own_rows, :] = stage[1, :, own_cols]
    mid_rows[own_rows, :] = middle[:, own_cols]

    @pl.when(jnp.logical_not(gets))
    def _():
        normed_conv[away] = jnp.zeros((lons, half), BF)

    base = quad_off[0]
    wide_ok = lat_half[0] >= 1
    taps = [
        [
            lat_taps[b, base + r] if r == 1 else jnp.where(wide_ok, lat_taps[b, base + r], 0.0)
            for b in range(2)
        ]
        for r in range(3)
    ]

    def mix(values, b):
        return jnp.concatenate(
            [
                lax.dot_general(
                    values[:, p * 2 * head : (p + 1) * 2 * head],
                    mixer[b, :, p * 2 * head : (p + 1) * 2 * head],
                    (((1,), (1,)), ((), ())),
                    preferred_element_type=F32,
                )
                for p in range(half // (2 * head))
            ],
            axis=1,
        ).astype(BF)

    conv_copy(stage.at[1, :, side_cols], 1, 1 - c, 3, sibling).wait_recv()
    for b in range(2):
        gain = jnp.where(place == 0, taps[0][b], 0.0) + jnp.where(place == last_place, taps[2][b], 0.0)
        pole = mix((gain * normed_conv[1].astype(F32)).astype(BF), b)
        polar[b, :rows] = pole[rows:]
        polar[b, rows:] = pole[:rows]
    conv_copy(stage.at[0, :, side_cols], near, 1 - c, 2, sibling).wait_recv()
    remote(middle.at[:, side_cols], mid_rows.at[side_rows, :], h_send.at[0], h_recv.at[0], sibling).wait_recv()

    q_cross(0).wait_send()
    q_cross(1).wait_send()
    o_cross(place, 0).wait_send()
    o_cross(place, 1).wait_send()
    deal(q_direct, finish)
    deal(o_direct, finish)
    o_near(finish)
    for t in range(1, nz):
        for signed in (t, -t):
            q_step(signed, finish)
            o_step(signed, finish)
    o_gather(finish)
    for d in tok_copies + bias_copies + att_copies(x, 0) + att_copies(1 - x, 1) + to_side + [to_mid]:
        d.wait_send()

    @pl.when(gets)
    def _():
        for cc in range(2):
            for part in range(2):
                target = normed_conv.at[away, pl.ds(cc * rows + part * split, split), :]
                remote(target, target, f_send.at[0], f_recv.at[cc, part], sibling).wait_recv()

    for b in range(2):
        summed = (
            taps[0][b] * normed_conv[0].astype(F32)
            + taps[1][b] * normed_conv[1].astype(F32)
            + taps[2][b] * normed_conv[2].astype(F32)
        ).astype(BF)
        mixed[b * lons : (b + 1) * lons, :] = (
            mix(summed, b).astype(F32) + polar[b].astype(F32)
        ).astype(BF)

    def convolve(at):
        return (
            mid_rows[at, :].astype(F32)
            + jnp.dot(coeff[at, :], mixed[...], preferred_element_type=F32)
        ).astype(BF)

    done_out[...] = convolve(side_rows)
    to_done = remote(done_out, done_in, h_send.at[1], h_recv.at[1], sibling)
    to_done.start()
    out[:, own_cols] = convolve(own_rows)

    @pl.when(passes_own)
    def _():
        for d in to_back:
            d.wait_send()

    @pl.when(passes)
    def _():
        for d in to_far:
            d.wait_send()

    to_done.wait_recv()
    out[:, side_cols] = done_in[...]
    to_done.wait_send()


def in_hbm(value):
    return pltpu.with_memory_space_constraint(value, pltpu.HBM)


def fused_device(
    tokens, gain_attn, w_qkv, key_bias, w_out, gain_conv, w_conv, lat_taps, lon_half, lat_half, quad_off
):
    rows, width = tokens.shape[1:]
    shard = w_qkv.shape[0]
    heads = key_bias.shape[1]
    lat_count = width // shard
    nx = 2
    nz = lat_count // nx
    part, half, lons = width // 4, width // 2, 2 * rows
    vmem = pl.BlockSpec(memory_space=pltpu.VMEM)
    anywhere = pl.BlockSpec(memory_space=pltpu.HBM)
    dma = pltpu.SemaphoreType.DMA
    out = pl.pallas_call(
        lambda *refs: fused_kernel(nx, nz, *refs),
        out_shape=pltpu.VMEM((rows, width), BF),
        in_specs=[anywhere] * 11,
        out_specs=vmem,
        scratch_shapes=[
            pltpu.SMEM((2, lat_taps.shape[0]), F32),
            pltpu.SMEM((1,), jnp.int32),
            pltpu.SMEM((1,), jnp.int32),
            pltpu.SMEM((1,), jnp.int32),
            pltpu.VMEM((width,), F32),
            pltpu.VMEM(w_qkv.shape, BF),
            pltpu.VMEM((width,), F32),
            pltpu.VMEM((2, 64, half), BF),
            dma((12,)),
            pltpu.VMEM((shard, 3 * part), BF),
            pltpu.VMEM((width, 3 * part), BF),
            pltpu.VMEM((width, width), BF),
            pltpu.VMEM((2, lons, width), BF),
            pltpu.VMEM((2, lons, width), BF),
            pltpu.VMEM((2, 2, heads, rows), BF),
            pltpu.VMEM((2, heads, lons), F32),
            pltpu.VMEM((2, lons, part), BF),
            pltpu.VMEM((2, 4, rows, part), BF),
            pltpu.VMEM((2, rows, width), BF),
            pltpu.VMEM((3, lons, half), BF),
            pltpu.VMEM((rows, width), BF),
            pltpu.VMEM((lons, half), BF),
            pltpu.VMEM((2, 128, half), BF),
            pltpu.VMEM((2, lons, half), BF),
            pltpu.VMEM((2 * lons, half), BF),
            pltpu.VMEM((lons, 2 * lons), BF),
            pltpu.VMEM((rows, half), BF),
            pltpu.VMEM((rows, half), BF),
            dma((2,)), dma((2,)),
            dma((lat_count,)), dma((lat_count,)), dma((lat_count,)),
            dma((lat_count,)), dma((lat_count,)),
            dma((2,)), dma((2,)),
            dma((lat_count,)), dma((lat_count,)), dma((lat_count,)),
            dma((lat_count,)), dma((lat_count,)),
            dma((lat_count, 2)), dma((lat_count, 2)),
            dma((3,)), dma((3,)),
            dma((3,)), dma((3,)),
            dma((2, 3)), dma((2, 4)),
            dma((4,)), dma((2, 2)),
            dma((4,)), dma((3, 2)),
            dma((2,)), dma((2,)),
        ],
        compiler_params=pltpu.CompilerParams(
            collective_id=0, has_side_effects=True, vmem_limit_bytes=40 * 1024 * 1024
        ),
    )(
        in_hbm(lat_taps.T), lon_half, lat_half, quad_off,
        *[
            in_hbm(v)
            for v in (
                tokens[0], gain_attn, w_qkv, key_bias[0], w_out, gain_conv, jnp.swapaxes(w_conv, 1, 2)
            )
        ],
    )
    return out[None]


def solution(mesh):
    sizes = (mesh.shape["groups"], mesh.shape["lat"], mesh.shape["lon"])
    return jax.shard_map(
        fused_device if sizes == (2, 8, 2) else per_device,
        mesh=mesh,
        in_specs=(
            P(("groups", "lat"), "lon", None),
            P(),
            P("lat", None),
            P("lat", None, "lon"),
            P("lat", None),
            P(),
            P(),
            P(),
            P("lat"),
            P("lat"),
            P("lat"),
        ),
        out_specs=P(("groups", "lat"), "lon", None),
        check_vma=False,
    )
```
